256 devices in a mesh: grid: 256 (over x, y, z, core).
Axes of the slice: x: 4, y: 4, z: 8, core: 2. Of those that a mesh axis runs over, the one named last changes fastest.
Arguments:
- right_sides: float32 [32, 256, 48, 128], P(None, 'grid'), may hold values from -54 to 54, as said below
- recycle: float32 [2, 24, 256, 48, 128], P(None, None, 'grid'), may hold values from -6 to 6
- medium: float32 [256, 48, 128], P('grid'), may hold values from 0.05 to 1
- shift_table: float32 [8], replicated, may hold values from 0.25 to 2
- shift_index: int32 [2], replicated, may hold values from 0 to 7
Outputs:
- solution: float32 [32, 256, 48, 128], P(None, 'grid')
- residue: float32 [32, 256, 48, 128], P(None, 'grid')
The draws below stay inside these ranges and needn't reach their ends.
Inputs may be any that keep to these rules, and one draw needn't show every extreme that they name: `right_sides`: finite real values.
All inputs are finite; a program needn't handle non-finite values.
Results may differ from the reference program's by a relative error of at most 0.0003.
Values sent between devices are 32-bit elements; how exact they have to be, the bound alone decides.
No kernel may reach another device: no remote copies, remote signals or barrier semaphores. Data moves between devices by JAX's collectives and lax.ppermute only.
A program may use at most 64 MiB of HBM per device.

```python
import math
import jax
import jax.numpy as jnp
from jax import lax

NX = 48
NY = 128
K = 24
B = 16
STEPS = 3
SHIFTS = 8
S = 32
NZ = 256


def draw_right_sides(key, part):
    keys = jax.random.split(key, 3)
    plane = jnp.exp(jax.random.uniform(keys[1], (NZ,), jnp.float32, math.log(0.3), math.log(3.0)))
    rising = 0.5 + jnp.arange(NZ, dtype=jnp.float32) / max(NZ - 1, 1)
    column = jnp.exp(jax.random.uniform(keys[2], (S,), jnp.float32, math.log(0.3), math.log(3.0)))
    rough = jnp.clip(jax.random.normal(keys[0], (S, NZ, NX, NY), jnp.float32), -4.0, 4.0)
    return rough * column[:, None, None, None] * (plane * rising)[None, :, None, None]


def level_of(rng, shape, shards, low, high):
    factor_of, own = 1.0, jax.random.fold_in(rng, 6)
    for axis_at, blocks in shards:
        heights = jnp.exp(jax.random.uniform(jax.random.fold_in(own, axis_at), (blocks,), jnp.float32, low / len(shards), high / len(shards)))
        factor_of = factor_of * jnp.repeat(heights, shape[axis_at] // blocks).reshape([-1 if axis == axis_at else 1 for axis in range(len(shape))])
    return factor_of


def gaussian(key, shape, scale, most, cuts=(), kind=jnp.bfloat16):
    entries = scale * jax.random.normal(key, shape, jnp.float32)
    if cuts:
        entries = entries * level_of(key, shape, cuts, -0.22, 0.18)
    return jnp.clip(entries, -most, most).astype(kind)


def setup_inputs(seed: int = 0) -> dict:
    key_of = jax.random.split(jax.random.key(seed), 6)
    return {
        "right_sides": draw_right_sides(jax.random.fold_in(key_of[5], 71), 0),
        "recycle": gaussian(key_of[1], (2, K, NZ, NX, NY), 1.0, 6.0, ((2, 256),), jnp.float32),
        "medium": jnp.clip(jnp.exp(math.log(1.0) - 2.9957323 * jax.random.uniform(key_of[2], (NZ, NX, NY), jnp.float32) ** level_of(key_of[2], (NZ, NX, NY), ((0, 256),), -0.2, 0.2)), 0.05, 1.0),
        "shift_table": jnp.clip(jnp.exp(jax.random.uniform(key_of[3], (SHIFTS,), jnp.float32, math.log(0.25), math.log(2.0))), 0.25, 2.0),
        "shift_index": jax.random.randint(key_of[4], (2,), 0, SHIFTS).astype(jnp.int32),
    }


highest = lax.Precision.HIGHEST

def operate(field, diagonal_field):
    padded = jnp.pad(field, ((0, 0), (1, 1), (1, 1), (1, 1)))
    beside = padded[:, 2:, 1:-1, 1:-1] + padded[:, :-2, 1:-1, 1:-1]
    beside = beside + padded[:, 1:-1, 2:, 1:-1] + padded[:, 1:-1, :-2, 1:-1]
    beside = beside + padded[:, 1:-1, 1:-1, 2:] + padded[:, 1:-1, 1:-1, :-2]
    return diagonal_field * field - beside

def flat_rows(field):
    return field.reshape(field.shape[0], -1)

def gram_of(left, right):
    return jnp.dot(left, right.T, precision=highest)

def combine(coeffs, vectors):
    return jnp.dot(coeffs, vectors, precision=highest)

def lower_solve(factor, values):
    return jax.scipy.linalg.solve_triangular(factor, values, lower=True)

def upper_solve(factor, values):
    return jax.scipy.linalg.solve_triangular(factor, values, lower=True, trans=1)

def least_squares(hessenberg, target):
    normal_factor = jnp.linalg.cholesky(jnp.dot(hessenberg.T, hessenberg, precision=highest))
    right_part = jnp.dot(hessenberg.T, target, precision=highest)
    return upper_solve(normal_factor, lower_solve(normal_factor, right_part))

def reference(right_sides, recycle, medium, shift_table, shift_index):
    field_shape = right_sides.shape[1:]
    solutions = []
    residues = []
    for member in range(2):
        diagonal_field = 6.0 + shift_table[shift_index[member]] + medium
        sources = flat_rows(right_sides[member * B:(member + 1) * B])
        basis_u = recycle[member]
        applied_u = flat_rows(operate(basis_u, diagonal_field))
        factor = jnp.linalg.cholesky(gram_of(applied_u, applied_u))
        projected = lower_solve(factor, gram_of(applied_u, sources))
        residual = sources - combine(upper_solve(factor, projected).T, applied_u)
        resid_factor = jnp.linalg.cholesky(gram_of(residual, residual))
        blocks = [lower_solve(resid_factor, residual)]
        hess_cols = []
        recycle_cols = []
        for number in range(STEPS):
            applied = flat_rows(operate(blocks[number].reshape((B,) + field_shape), diagonal_field))
            recycle_part = lower_solve(factor, gram_of(applied_u, applied))
            krylov_parts = [gram_of(block, applied) for block in blocks]
            applied = applied - combine(upper_solve(factor, recycle_part).T, applied_u)
            for block, part in zip(blocks, krylov_parts):
                applied = applied - combine(part.T, block)
            new_factor = jnp.linalg.cholesky(gram_of(applied, applied))
            hess_cols.append(jnp.concatenate(krylov_parts + [new_factor.T, jnp.zeros(((STEPS - 1 - number) * B, B), jnp.float32)], axis=0))
            recycle_cols.append(recycle_part)
            blocks.append(lower_solve(new_factor, applied))
        hessenberg = jnp.concatenate(hess_cols, axis=1)
        recycle_coef = jnp.concatenate(recycle_cols, axis=1)
        target = jnp.concatenate([resid_factor.T, jnp.zeros((STEPS * B, B), jnp.float32)], axis=0)
        minimizer = least_squares(hessenberg, target)
        back_coef = upper_solve(factor, projected - combine(recycle_coef, minimizer))
        krylov = jnp.concatenate(blocks[:STEPS], axis=0)
        solution = combine(minimizer.T, krylov) + combine(back_coef.T, flat_rows(basis_u))
        residue = combine((target - combine(hessenberg, minimizer)).T, jnp.concatenate(blocks, axis=0))
        solutions.append(solution.reshape((B,) + field_shape))
        residues.append(residue.reshape((B,) + field_shape))
    return (jnp.concatenate(solutions, axis=0), jnp.concatenate(residues, axis=0))
```

```python
import jax
import jax.numpy as jnp
from jax import lax
from jax.experimental import pallas as pl
from jax.experimental.pallas import tpu as pltpu
from jax.sharding import Mesh
from jax.sharding import PartitionSpec as P

GRID = ("grid_0", "grid_1", "grid_2", "grid_3")
STAGES = (("grid_0", "grid_1", "grid_3"), ("grid_2",))
NX = 48
NY = 128
K = 24
B = 16
SHIFT = 0.5
HIGH = lax.Precision.HIGHEST
F32 = jnp.float32
BF16 = jnp.bfloat16
PARAMS = pltpu.CompilerParams(vmem_limit_bytes=56 << 20)
VMEM = pl.BlockSpec(memory_space=pltpu.VMEM)
SMEM = pl.BlockSpec(memory_space=pltpu.SMEM)


def iota(shape, dim):
    return lax.broadcasted_iota(jnp.int32, shape, dim)


def small(left, right):
    return jnp.dot(left, right, precision=HIGH, preferred_element_type=F32)


def halves(values):
    top = values.astype(BF16)
    return top, (values - top.astype(F32)).astype(BF16)


def row_products(left, right):
    dims = (((1,), (1,)), ((), ()))
    n = left.shape[0]
    l_top, l_rest = halves(left)
    r_top, r_rest = halves(right)
    both = lax.dot_general(
        jnp.concatenate([l_top, l_rest], axis=0), r_top, dims, preferred_element_type=F32
    )
    last = lax.dot_general(l_top, r_rest, dims, preferred_element_type=F32)
    return both[:n] + both[n:] + last


def combination(coeffs, fields):
    c_both, c_top = coeffs
    n = c_top.shape[0]
    f_top, f_rest = halves(fields)
    both = jnp.dot(c_both, f_top, preferred_element_type=F32)
    last = jnp.dot(c_top, f_rest, preferred_element_type=F32)
    return both[:n] + both[n:] + last


def split_coeffs(coeffs):
    top, rest = halves(coeffs)
    return jnp.concatenate([top, rest], axis=0), top


def neighbours(x, read, before, after):
    f = read(x)
    total = before + after
    if x > 0:
        total = total + read(x - 1)
    if x < NX - 1:
        total = total + read(x + 1)
    lane = iota(f.shape, 1)
    total = total + jnp.where(lane == 0, 0.0, pltpu.roll(f, 1, 1))
    return total + jnp.where(lane == NY - 1, 0.0, pltpu.roll(f, NY - 1, 1))


def transposed(values):
    rows = values.shape[0]
    return jnp.concatenate([values, jnp.zeros((128 - rows, 128), F32)], axis=0).T


def eliminate(system, count):
    lane = iota((1, 128), 1)
    row = iota(system.shape, 0)
    for k in range(count):
        pivot_row = system[k : k + 1]
        pivot = jnp.where(lane < 64, pivot_row[:, k : k + 1], pivot_row[:, 64 + k : 65 + k])
        scaled = pivot_row / pivot
        column = jnp.where(lane < 64, system[:, k : k + 1], system[:, 64 + k : 65 + k])
        system = jnp.where(row == k, scaled, system - column * scaled)
    return system


def apply_kernel(table, index, u, u_before, u_after, medium, f_out):
    for g in range(2):
        rows = slice(K * g, K * g + K)
        base = 6.0 + table[index[g]]
        for x in range(NX):
            diagonal = medium[x : x + 1, :] + base
            f_out[x, rows] = diagonal * u[x, rows] - neighbours(
                x, lambda i: u[i, rows], u_before[x, rows], u_after[x, rows]
            )


def first_gram_kernel(f, b, b_before, b_after, medium, b1_out, gram_out):
    total = jnp.zeros((2 * K, 128), F32)
    zeros = jnp.zeros((8, 2 * NY), F32)
    tops = [jnp.zeros((B, NY), F32) for _ in range(2)]
    squares = [jnp.zeros((B, NY), F32) for _ in range(2)]

    def next_field(x):
        out = (medium[x : x + 1, :] - SHIFT) * b[x] - neighbours(
            x, lambda i: b[i], b_before[x], b_after[x]
        )
        b1_out[x] = out
        return out

    for x in range(0, NX, 2):
        fields = jnp.concatenate([f[x], f[x + 1]], axis=1)
        b_pair = jnp.concatenate([b[x], b[x + 1]], axis=1)
        b1_pair = jnp.concatenate([next_field(x), next_field(x + 1)], axis=1)
        right = []
        for g in range(2):
            bg = b_pair[B * g : B * g + B]
            b1g = b1_pair[B * g : B * g + B]
            right += [fields[K * g : K * g + K], bg, b1g, zeros]
            top = bg * b1g
            square = bg * bg
            tops[g] = tops[g] + top[:, :NY] + top[:, NY:]
            squares[g] = squares[g] + square[:, :NY] + square[:, NY:]
        total = total + row_products(fields, jnp.concatenate(right, axis=0))
    lane = iota((K, 128), 1)
    row = iota((K, 128), 0)
    packed = jnp.where(lane < 64, total[:K], total[K:])
    for g in range(2):
        here = (row == 0) & (lane == 64 * g + 56)
        packed = jnp.where(here, jnp.sum(tops[g], keepdims=True), packed)
        here = (row == 0) & (lane == 64 * g + 57)
        packed = jnp.where(here, jnp.sum(squares[g], keepdims=True), packed)
    gram_out[...] = packed


def inverse_kernel(gram, out):
    lane = iota((K, 128), 1)
    row = iota((K, 128), 0)
    place = lane & 63
    unit = jnp.where(place == row + K, 1.0, 0.0)
    out[...] = eliminate(jnp.where(place < K, gram[...], unit), K)


def second_gram_kernel(f, f_before, f_after, b1, medium, fields_out, gram_out):
    total = jnp.zeros((2 * K, 128), F32)

    def next_field(x):
        return (medium[x : x + 1, :] - SHIFT) * f[x] - neighbours(
            x, lambda i: f[i], f_before[x], f_after[x]
        )

    for x in range(0, NX, 2):
        nexts = [next_field(x), next_field(x + 1)]
        for i in range(2):
            for g in range(2):
                at = 40 * g
                fields_out[x + i, at : at + K] = nexts[i][K * g : K * g + K]
                fields_out[x + i, at + K : at + K + B] = b1[x + i, B * g : B * g + B]
        f_pair = jnp.concatenate([f[x], f[x + 1]], axis=1)
        f1_pair = jnp.concatenate(nexts, axis=1)
        b1_pair = jnp.concatenate([b1[x], b1[x + 1]], axis=1)
        right = []
        for g in range(2):
            right += [
                f_pair[K * g : K * g + K],
                f1_pair[K * g : K * g + K],
                b1_pair[B * g : B * g + B],
            ]
        total = total + row_products(f1_pair, jnp.concatenate(right, axis=0))
    lane = iota((K, 128), 1)
    gram_out[...] = jnp.where(lane < 64, total[:K], total[K:])


def krylov_kernel(
    first, inverse, second, f, b, fields, before, after, medium, q_out, last_out, coef_out, shift_out
):
    first_t = transposed(first[...])
    second_t = transposed(second[...])
    inverse_t = transposed(inverse[...])
    coeffs = []
    thetas = []
    for g in range(2):
        at = 64 * g
        ginv = inverse_t[at + K : at + 2 * K, :K]
        fb = first_t[at + K : at + K + B, :K]
        fb1 = first_t[at + K + B : at + K + 2 * B, :K]
        ff1 = second_t[at : at + K, :K]
        f1f1 = second_t[at + K : at + 2 * K, :K]
        f1b1 = second_t[at + 2 * K : at + 2 * K + B, :K]
        theta = first_t[at + 56 : at + 57, :1] / first_t[at + 57 : at + 58, :1]
        z0 = small(fb, ginv)
        z1 = small(fb1 - small(z0, ff1), ginv)
        z2 = small(f1b1 - small(z0, f1f1) - small(z1, ff1), ginv)
        z2 = z2 - theta * z1
        mixed = z1 - theta * z0
        zero = jnp.zeros((B, K), F32)
        pad = jnp.zeros((B, 8), F32)
        table = jnp.concatenate(
            [
                jnp.concatenate([z0, zero, zero, pad], axis=1),
                jnp.concatenate([mixed, z0, zero, pad], axis=1),
                jnp.concatenate([z2 - theta * mixed, mixed, z0, pad], axis=1),
            ],
            axis=0,
        )
        coeffs.append(split_coeffs(-table))
        thetas.append(theta)
        for i, z in enumerate((z0, z1, z2, ginv)):
            coef_out[g, 24 * i : 24 * i + z.shape[0], :K] = z
        shift_out[8 * g : 8 * g + 8, :] = jnp.broadcast_to(theta, (8, 128))

    def next_field(x, g):
        rows = slice(40 * g, 40 * g + 40)
        return (medium[x : x + 1, :] - SHIFT - thetas[g]) * fields[x, rows] - neighbours(
            x, lambda i: fields[i, rows], before[x, rows], after[x, rows]
        )

    zeros = jnp.zeros((8, 2 * NY), F32)
    for x in range(0, NX, 2):
        for g in range(2):
            nexts = jnp.concatenate([next_field(x, g), next_field(x + 1, g)], axis=1)
            rows = slice(40 * g, 40 * g + 40)
            firsts = jnp.concatenate([fields[x, rows], fields[x + 1, rows]], axis=1)
            frows = slice(K * g, K * g + K)
            brows = slice(B * g, B * g + B)
            f_pair = jnp.concatenate([f[x, frows], f[x + 1, frows]], axis=1)
            b0 = jnp.concatenate([b[x, brows], b[x + 1, brows]], axis=1)
            theta = thetas[g]
            made = combination(
                coeffs[g], jnp.concatenate([f_pair, firsts[:K], nexts[:K], zeros], axis=0)
            )
            b1 = firsts[K:]
            q1 = b1 - theta * b0
            made = made + jnp.concatenate([b0, q1, nexts[K:] - theta * q1], axis=0)
            for i in range(2):
                part = made[:, NY * i : NY * i + NY]
                q_out[x + i, 48 * g : 48 * g + 48] = part
                last_out[x + i, brows] = part[2 * B :]


def moment_kernel(q, last, last_before, last_after, fields, medium, shift, t_out, gram_out):
    zeros = jnp.zeros((40, 2 * NY), F32)
    grams = []
    for g in range(2):
        theta = shift[8 * g : 8 * g + 1, :]
        brows = slice(B * g, B * g + B)

        def next_field(x):
            out = (medium[x : x + 1, :] - SHIFT - theta) * last[x, brows] - neighbours(
                x, lambda i: last[i, brows], last_before[x, brows], last_after[x, brows]
            )
            t_out[x, brows] = out
            return out

        qrows = slice(48 * g, 48 * g + 48)
        frows = slice(40 * g, 40 * g + K)
        total = jnp.zeros((64, 128), F32)
        for x in range(0, NX, 2):
            left = jnp.concatenate(
                [
                    jnp.concatenate([q[x, qrows], q[x + 1, qrows]], axis=1),
                    jnp.concatenate([next_field(x), next_field(x + 1)], axis=1),
                ],
                axis=0,
            )
            f1 = jnp.concatenate([fields[x, frows], fields[x + 1, frows]], axis=1)
            total = total + row_products(left, jnp.concatenate([left, f1, zeros], axis=0))
        grams.append(total)
    lane = iota((B, 128), 1)
    row = iota((B, 128), 0)
    column = lane & 15
    strips = []
    for gram in grams:
        strips.append(
            jnp.where(
                lane < 32,
                gram[:16],
                jnp.where(
                    lane < 64,
                    pltpu.roll(gram[16:32], 16, 1),
                    jnp.where(
                        lane < 96, pltpu.roll(gram[32:48], 32, 1), pltpu.roll(gram[48:64], 48, 1)
                    ),
                ),
            )
        )
    packed = jnp.where(row <= column, strips[0], strips[1])
    packed = jnp.where(lane < 112, packed, 0.0)
    on_diagonal = jnp.where((row == column) & (lane < 112), strips[1], 0.0)
    for k in range(7):
        inside = (lane >= 16 * k) & (lane < 16 * k + 16)
        own = jnp.sum(jnp.where(inside, on_diagonal, 0.0), axis=1, keepdims=True)
        packed = jnp.where(lane == 112 + k, own, packed)
    low = jnp.zeros((8, 128), F32)
    lane8 = iota((8, 128), 1)
    for g in range(2):
        for half in range(2):
            at = 24 * (2 * g + half)
            piece = pltpu.roll(grams[g][32 + 8 * half : 40 + 8 * half], (at - 64) % 128, 1)
            low = jnp.where((lane8 >= at) & (lane8 < at + K), piece, low)
    gram_out[:B] = packed
    gram_out[B:] = low


def finish_kernel(table, index, moments, coef, shift, u, f, q, t, solution_out, residue_out):
    packed = moments[:B]
    turned = transposed(packed)
    lane = iota((B, 128), 1)
    row = iota((B, 128), 0)
    column = lane & 15
    flipped = turned[:B]
    for k in range(1, 7):
        flipped = flipped + pltpu.roll(turned[16 * k : 16 * k + 16], 16 * k, 1)
    diagonal = packed
    for k in range(7):
        diagonal = jnp.where(
            (lane >= 16 * k) & (lane < 16 * k + 16), packed[:, 112 + k : 113 + k], diagonal
        )
    strips = [
        jnp.where(row <= column, packed, flipped),
        jnp.where(row == column, diagonal, jnp.where(row > column, packed, flipped)),
    ]
    shifts = []
    thirds = []
    blocks = [[], [], []]
    parts = []
    for g in range(2):
        c = 6.0 + SHIFT + table[index[g]] + shift[8 * g : 8 * g + 1, :]
        shifts.append(c)
        at = 48 * g
        f1q2 = jnp.concatenate(
            [moments[B:, at : at + K], moments[B:, at + K : at + 2 * K]], axis=0
        )
        z3 = small(f1q2, coef[g, 72 : 72 + K, :K])
        thirds.append(z3)
        taken = lax.dot_general(
            z3, f1q2, (((1,), (1,)), ((), ())), precision=HIGH, preferred_element_type=F32
        )
        wide = jnp.concatenate([taken, jnp.zeros((B, 112), F32)], axis=1)
        strip = strips[g] - pltpu.roll(wide, 96, 1)
        once = pltpu.roll(strip, 16, 1)
        twice = pltpu.roll(strip, 32, 1)
        squared = strip + 2.0 * c * once + c * c * twice
        right = strip + c * once
        parts.append(
            [
                jnp.where(
                    lane < 48,
                    pltpu.roll(squared, 128 - 16 * (i + 1), 1),
                    pltpu.roll(right, 48 - 16 * i, 1),
                )
                for i in (1, 2, 3)
            ]
        )
    system = jnp.concatenate(
        [jnp.where(lane < 64, parts[0][i], pltpu.roll(parts[1][i], 64, 1)) for i in range(3)],
        axis=0,
    )
    solved = transposed(eliminate(system, 48))
    coeffs = []
    for g in range(2):
        c = shifts[g][:, :1]
        ys = solved[64 * g + 48 : 64 * g + 64]
        y1, y2, y3 = (ys[:, 16 * i : 16 * i + 16] for i in range(3))
        z0, z1, z2 = (coef[g, 24 * i : 24 * i + B, :K] for i in range(3))
        on_f = small(y3, thirds[g])
        on_u = z0 - small(y1, z1) - small(y2, z2) - on_f
        none = jnp.zeros((B, K), F32)
        rows = jnp.concatenate(
            [
                jnp.concatenate([on_u, none, y1, y2, y3, jnp.zeros((B, B), F32)], axis=1),
                jnp.concatenate(
                    [none, on_f, -c * y1, -y1 - c * y2, -y2 - c * y3, -y3], axis=1
                ),
            ],
            axis=0,
        )
        coeffs.append(split_coeffs(rows))
    for x in range(0, NX, 2):
        for g in range(2):
            krows = slice(K * g, K * g + K)
            brows = slice(B * g, B * g + B)
            qrows = slice(48 * g, 48 * g + 48)

            def stack(x):
                return jnp.concatenate(
                    [u[x, krows], f[x, krows], q[x, qrows], t[x, brows]], axis=0
                )

            made = combination(
                coeffs[g], jnp.concatenate([stack(x), stack(x + 1)], axis=1)
            )
            for i in range(2):
                part = made[:, NY * i : NY * i + NY]
                solution_out[x + i, brows] = part[:B]
                residue_out[x + i, brows] = part[B:] + q[x + i, 48 * g : 48 * g + B]


def call(kernel, shapes, scalars, *arrays):
    out = [jax.ShapeDtypeStruct(s, F32) for s in shapes]
    count = len(arrays) - scalars
    return pl.pallas_call(
        kernel,
        out_shape=out,
        in_specs=[SMEM] * scalars + [VMEM] * count,
        out_specs=[VMEM] * len(out),
        compiler_params=PARAMS,
        name=kernel.__name__,
    )(*arrays)


def everyone(values):
    for axes in STAGES:
        size = lax.axis_size(axes)
        spread = jnp.broadcast_to(values[None], (size, *values.shape))
        values = jnp.sum(lax.all_to_all(spread, axes, 0, 0, tiled=True), axis=0)
    return values


def beside(values):
    count = lax.axis_size(GRID)
    ends = count - 1
    before = lax.ppermute(values, GRID, [(i, i + 1) for i in range(ends)])
    after = lax.ppermute(values, GRID, [(i + 1, i) for i in range(ends)])
    return before, after


def on_device(right_sides, recycle, medium, shift_table, shift_index):
    med = medium[0]
    u = jnp.transpose(recycle.reshape(2 * K, NX, NY), (1, 0, 2))
    b = jnp.transpose(right_sides.reshape(2 * B, NX, NY), (1, 0, 2))
    u_sides = beside(u)
    b_sides = beside(b)
    (f,) = call(apply_kernel, [(NX, 2 * K, NY)], 2, shift_table, shift_index, u, *u_sides, med)
    f_sides = beside(f)
    b1, gram = call(
        first_gram_kernel, [(NX, 2 * B, NY), (K, 128)], 0, f, b, *b_sides, med
    )
    first = everyone(gram)
    (inverse,) = call(inverse_kernel, [(K, 128)], 0, first)
    fields, gram = call(
        second_gram_kernel, [(NX, 80, NY), (K, 128)], 0, f, *f_sides, b1, med
    )
    field_sides = beside(fields)
    second = everyone(gram)
    q, last, coef, shift = call(
        krylov_kernel,
        [(NX, 96, NY), (NX, 2 * B, NY), (2, 96, 128), (16, 128)],
        0,
        first,
        inverse,
        second,
        f,
        b,
        fields,
        *field_sides,
        med,
    )
    last_sides = beside(last)
    t, gram = call(
        moment_kernel,
        [(NX, 2 * B, NY), (K, 128)],
        0,
        q,
        last,
        *last_sides,
        fields,
        med,
        shift,
    )
    moments = everyone(gram)
    solution, residue = call(
        finish_kernel,
        [(NX, 2 * B, NY)] * 2,
        2,
        shift_table,
        shift_index,
        moments,
        coef,
        shift,
        u,
        f,
        q,
        t,
    )
    shape = right_sides.shape
    return (
        jnp.transpose(solution, (1, 0, 2)).reshape(shape),
        jnp.transpose(residue, (1, 0, 2)).reshape(shape),
    )


def solution(mesh):
    torus = Mesh(mesh.devices.reshape(4, 4, 8, 2), GRID)
    in_specs = (
        P(None, GRID, None, None),
        P(None, None, GRID, None, None),
        P(GRID, None, None),
        P(),
        P(),
    )
    out_specs = (P(None, GRID, None, None), P(None, GRID, None, None))
    return jax.shard_map(
        on_device, mesh=torus, in_specs=in_specs, out_specs=out_specs, check_vma=False
    )
```

```python
import jax
import jax.numpy as jnp
from jax import lax
from jax.experimental import pallas as pl
from jax.experimental.pallas import tpu as pltpu
from jax.sharding import Mesh
from jax.sharding import PartitionSpec as P

GRID = ("grid_0", "grid_1", "grid_2", "grid_3")
CORES = "grid_3"
STAGES = (("grid_0", "grid_1"), "grid_2")
NX = 48
NY = 128
K = 24
B = 16
SHIFT = 0.5
HIGH = lax.Precision.HIGHEST
F32 = jnp.float32
BF16 = jnp.bfloat16
PARAMS = pltpu.CompilerParams(vmem_limit_bytes=24 << 20)
VMEM = pl.BlockSpec(memory_space=pltpu.VMEM)
SMEM = pl.BlockSpec(memory_space=pltpu.SMEM)


def iota(shape, dim):
    return lax.broadcasted_iota(jnp.int32, shape, dim)


def small(left, right):
    return jnp.dot(left, right, precision=HIGH, preferred_element_type=F32)


def halves(values):
    top = values.astype(BF16)
    return top, (values - top.astype(F32)).astype(BF16)


def row_products(left, right):
    dims = (((1,), (1,)), ((), ()))
    n = left.shape[0]
    l_top, l_rest = halves(left)
    r_top, r_rest = halves(right)
    both = lax.dot_general(
        jnp.concatenate([l_top, l_rest], axis=0), r_top, dims, preferred_element_type=F32
    )
    last = lax.dot_general(l_top, r_rest, dims, preferred_element_type=F32)
    return both[:n] + both[n:] + last


def combination(coeffs, fields):
    c_both, c_top = coeffs
    n = c_top.shape[0]
    f_top, f_rest = halves(fields)
    both = jnp.dot(c_both, f_top, preferred_element_type=F32)
    last = jnp.dot(c_top, f_rest, preferred_element_type=F32)
    return both[:n] + both[n:] + last


def split_coeffs(coeffs):
    top, rest = halves(coeffs)
    return jnp.concatenate([top, rest], axis=0), top


def neighbours(x, read, before, after):
    f = read(x)
    total = before + after
    if x > 0:
        total = total + read(x - 1)
    if x < NX - 1:
        total = total + read(x + 1)
    lane = iota(f.shape, 1)
    total = total + jnp.where(lane == 0, 0.0, pltpu.roll(f, 1, 1))
    return total + jnp.where(lane == NY - 1, 0.0, pltpu.roll(f, NY - 1, 1))


def transposed(values):
    rows = values.shape[0]
    return jnp.concatenate([values, jnp.zeros((128 - rows, 128), F32)], axis=0).T


def eliminate(system, count):
    lane = iota((1, 128), 1)
    row = iota(system.shape, 0)

    def column(k):
        return jnp.where(lane < 64, system[:, k : k + 1], system[:, 64 + k : 65 + k])

    for k in range(0, count, 2):
        one = system[k : k + 1]
        two = system[k + 1 : k + 2]
        left = column(k)
        right = column(k + 1)
        a, b = left[k : k + 1], right[k : k + 1]
        c, d = left[k + 1 : k + 2], right[k + 1 : k + 2]
        inverse = 1.0 / (a * d - b * c)
        new_one = (d * inverse) * one - (b * inverse) * two
        new_two = (a * inverse) * two - (c * inverse) * one
        changed = system - left * new_one - right * new_two
        system = jnp.where(row == k, new_one, jnp.where(row == k + 1, new_two, changed))
    return system


def over_copies(parts):
    total = parts[0]
    for i in range(1, parts.shape[0]):
        total = total + parts[i]
    return total


def apply_kernel(table, index, u, u_before, u_after, medium, f_out):
    for g in range(2):
        rows = slice(K * g, K * g + K)
        base = 6.0 + table[index[g]]
        for x in range(NX):
            diagonal = medium[x : x + 1, :] + base
            f_out[x, rows] = diagonal * u[x, rows] - neighbours(
                x, lambda i: u[i, rows], u_before[x, rows], u_after[x, rows]
            )


def first_gram_kernel(f, b, b_before, b_after, medium, b1_out, gram_out):
    total = jnp.zeros((2 * K, 128), F32)
    zeros = jnp.zeros((8, 2 * NY), F32)
    tops = [jnp.zeros((B, NY), F32) for _ in range(2)]
    squares = [jnp.zeros((B, NY), F32) for _ in range(2)]

    def next_field(x):
        out = (medium[x : x + 1, :] - SHIFT) * b[x] - neighbours(
            x, lambda i: b[i], b_before[x], b_after[x]
        )
        b1_out[x] = out
        return out

    for x in range(0, NX, 2):
        fields = jnp.concatenate([f[x], f[x + 1]], axis=1)
        b_pair = jnp.concatenate([b[x], b[x + 1]], axis=1)
        b1_pair = jnp.concatenate([next_field(x), next_field(x + 1)], axis=1)
        right = []
        for g in range(2):
            bg = b_pair[B * g : B * g + B]
            b1g = b1_pair[B * g : B * g + B]
            right += [fields[K * g : K * g + K], bg, b1g, zeros]
            top = bg * b1g
            square = bg * bg
            tops[g] = tops[g] + top[:, :NY] + top[:, NY:]
            squares[g] = squares[g] + square[:, :NY] + square[:, NY:]
        total = total + row_products(fields, jnp.concatenate(right, axis=0))
    lane = iota((K, 128), 1)
    row = iota((K, 128), 0)
    packed = jnp.where(lane < 64, total[:K], total[K:])
    for g in range(2):
        here = (row == 0) & (lane == 64 * g + 56)
        packed = jnp.where(here, jnp.sum(tops[g], keepdims=True), packed)
        here = (row == 0) & (lane == 64 * g + 57)
        packed = jnp.where(here, jnp.sum(squares[g], keepdims=True), packed)
    gram_out[...] = packed


def second_gram_kernel(f, f_before, f_after, b1, first, medium, fields_out, gram_out):
    total = jnp.zeros((2 * K, 128), F32)

    def next_field(x):
        return (medium[x : x + 1, :] - SHIFT) * f[x] - neighbours(
            x, lambda i: f[i], f_before[x], f_after[x]
        )

    for x in range(0, NX, 2):
        nexts = [next_field(x), next_field(x + 1)]
        for i in range(2):
            for g in range(2):
                at = 40 * g
                fields_out[x + i, at : at + K] = nexts[i][K * g : K * g + K]
                fields_out[x + i, at + K : at + K + B] = b1[x + i, B * g : B * g + B]
        f_pair = jnp.concatenate([f[x], f[x + 1]], axis=1)
        f1_pair = jnp.concatenate(nexts, axis=1)
        b1_pair = jnp.concatenate([b1[x], b1[x + 1]], axis=1)
        right = []
        for g in range(2):
            right += [
                f_pair[K * g : K * g + K],
                f1_pair[K * g : K * g + K],
                b1_pair[B * g : B * g + B],
            ]
        total = total + row_products(f1_pair, jnp.concatenate(right, axis=0))
    lane = iota((K, 128), 1)
    gram_out[:K] = first[...]
    gram_out[K:] = jnp.where(lane < 64, total[:K], total[K:])


def krylov_kernel(
    grams, f, b, fields, before, after, medium, q_out, last_out, coef_out, shift_out
):
    gram = over_copies(grams)
    first = gram[:K]
    lane = iota((K, 128), 1)
    row = iota((K, 128), 0)
    place = lane & 63
    unit = jnp.where(place == row + K, 1.0, 0.0)
    inverse_t = transposed(eliminate(jnp.where(place < K, first, unit), K))
    first_t = transposed(first)
    second_t = transposed(gram[K:])
    coeffs = []
    thetas = []
    for g in range(2):
        at = 64 * g
        ginv = inverse_t[at + K : at + 2 * K, :K]
        fb = first_t[at + K : at + K + B, :K]
        fb1 = first_t[at + K + B : at + K + 2 * B, :K]
        ff1 = second_t[at : at + K, :K]
        f1f1 = second_t[at + K : at + 2 * K, :K]
        f1b1 = second_t[at + 2 * K : at + 2 * K + B, :K]
        theta = first_t[at + 56 : at + 57, :1] / first_t[at + 57 : at + 58, :1]
        z0 = small(fb, ginv)
        z1 = small(fb1 - small(z0, ff1), ginv)
        z2 = small(f1b1 - small(z0, f1f1) - small(z1, ff1), ginv)
        z2 = z2 - theta * z1
        mixed = z1 - theta * z0
        zero = jnp.zeros((B, K), F32)
        pad = jnp.zeros((B, 8), F32)
        table = jnp.concatenate(
            [
                jnp.concatenate([z0, zero, zero, pad], axis=1),
                jnp.concatenate([mixed, z0, zero, pad], axis=1),
                jnp.concatenate([z2 - theta * mixed, mixed, z0, pad], axis=1),
            ],
            axis=0,
        )
        coeffs.append(split_coeffs(-table))
        thetas.append(theta)
        for i, z in enumerate((z0, z1, z2, ginv)):
            coef_out[g, 24 * i : 24 * i + z.shape[0], :K] = z
        shift_out[8 * g : 8 * g + 8, :] = jnp.broadcast_to(theta, (8, 128))

    def next_field(x, g):
        rows = slice(40 * g, 40 * g + 40)
        return (medium[x : x + 1, :] - SHIFT - thetas[g]) * fields[x, rows] - neighbours(
            x, lambda i: fields[i, rows], before[x, rows], after[x, rows]
        )

    zeros = jnp.zeros((8, 2 * NY), F32)
    for x in range(0, NX, 2):
        for g in range(2):
            nexts = jnp.concatenate([next_field(x, g), next_field(x + 1, g)], axis=1)
            rows = slice(40 * g, 40 * g + 40)
            firsts = jnp.concatenate([fields[x, rows], fields[x + 1, rows]], axis=1)
            frows = slice(K * g, K * g + K)
            brows = slice(B * g, B * g + B)
            f_pair = jnp.concatenate([f[x, frows], f[x + 1, frows]], axis=1)
            b0 = jnp.concatenate([b[x, brows], b[x + 1, brows]], axis=1)
            theta = thetas[g]
            made = combination(
                coeffs[g], jnp.concatenate([f_pair, firsts[:K], nexts[:K], zeros], axis=0)
            )
            b1 = firsts[K:]
            q1 = b1 - theta * b0
            made = made + jnp.concatenate([b0, q1, nexts[K:] - theta * q1], axis=0)
            for i in range(2):
                part = made[:, NY * i : NY * i + NY]
                q_out[x + i, 48 * g : 48 * g + 48] = part
                last_out[x + i, brows] = part[2 * B :]


def basis_gram_kernel(q, fields, gram_out):
    for g in range(2):
        qrows = slice(48 * g, 48 * g + 48)
        frows = slice(40 * g, 40 * g + K)
        total = jnp.zeros((48, 128), F32)
        none = jnp.zeros((B, 2 * NY), F32)
        pad = jnp.zeros((40, 2 * NY), F32)
        for x in range(0, NX, 2):
            left = jnp.concatenate([q[x, qrows], q[x + 1, qrows]], axis=1)
            f1 = jnp.concatenate([fields[x, frows], fields[x + 1, frows]], axis=1)
            total = total + row_products(left, jnp.concatenate([left, none, f1, pad], axis=0))
        gram_out[g] = total


def moment_kernel(last, last_before, last_after, basis_gram, medium, shift, t_out, gram_out):
    def next_field(x, g):
        theta = shift[8 * g : 8 * g + 1, :]
        brows = slice(B * g, B * g + B)
        out = (medium[x : x + 1, :] - SHIFT - theta) * last[x, brows] - neighbours(
            x, lambda i: last[i, brows], last_before[x, brows], last_after[x, brows]
        )
        t_out[x, brows] = out
        return out

    total = jnp.zeros((2 * B, 128), F32)
    pad = jnp.zeros((64, 2 * NY), F32)
    for x in range(0, NX, 2):
        left = []
        right = []
        for g in range(2):
            brows = slice(B * g, B * g + B)
            made = jnp.concatenate([next_field(x, g), next_field(x + 1, g)], axis=1)
            left.append(made)
            right.append(jnp.concatenate([last[x, brows], last[x + 1, brows]], axis=1))
            right.append(made)
        total = total + row_products(
            jnp.concatenate(left, axis=0), jnp.concatenate(right + [pad], axis=0)
        )
    grams = [basis_gram[0], basis_gram[1]]
    ends = [pltpu.roll(total[:B], 80, 1), pltpu.roll(total[B:], 48, 1)]
    lane = iota((B, 128), 1)
    row = iota((B, 128), 0)
    column = lane & 15
    strips = []
    for gram, end in zip(grams, ends):
        middle = jnp.where(lane < 64, pltpu.roll(gram[16:32], 16, 1), pltpu.roll(gram[32:48], 32, 1))
        strips.append(jnp.where(lane < 32, gram[:16], jnp.where(lane < 80, middle, end)))
    packed = jnp.where(row <= column, strips[0], strips[1])
    packed = jnp.where(lane < 112, packed, 0.0)
    on_diagonal = jnp.where((row == column) & (lane < 112), strips[1], 0.0)
    for k in range(7):
        inside = (lane >= 16 * k) & (lane < 16 * k + 16)
        own = jnp.sum(jnp.where(inside, on_diagonal, 0.0), axis=1, keepdims=True)
        packed = jnp.where(lane == 112 + k, own, packed)
    low = jnp.zeros((8, 128), F32)
    lane8 = iota((8, 128), 1)
    for g in range(2):
        for half in range(2):
            at = 24 * (2 * g + half)
            piece = pltpu.roll(grams[g][32 + 8 * half : 40 + 8 * half], (at - 64) % 128, 1)
            low = jnp.where((lane8 >= at) & (lane8 < at + K), piece, low)
    gram_out[:B] = packed
    gram_out[B:] = low


def finish_kernel(table, index, moments, coef, shift, u, f, q, t, solution_out, residue_out):
    summed = over_copies(moments)
    packed = summed[:B]
    turned = transposed(packed)
    lane = iota((B, 128), 1)
    row = iota((B, 128), 0)
    column = lane & 15
    flipped = turned[:B]
    for k in range(1, 7):
        flipped = flipped + pltpu.roll(turned[16 * k : 16 * k + 16], 16 * k, 1)
    diagonal = packed
    for k in range(7):
        diagonal = jnp.where(
            (lane >= 16 * k) & (lane < 16 * k + 16), packed[:, 112 + k : 113 + k], diagonal
        )
    strips = [
        jnp.where(row <= column, packed, flipped),
        jnp.where(row == column, diagonal, jnp.where(row > column, packed, flipped)),
    ]
    shifts = []
    thirds = []
    blocks = [[], [], []]
    parts = []
    for g in range(2):
        c = 6.0 + SHIFT + table[index[g]] + shift[8 * g : 8 * g + 1, :]
        shifts.append(c)
        at = 48 * g
        f1q2 = jnp.concatenate(
            [summed[B:, at : at + K], summed[B:, at + K : at + 2 * K]], axis=0
        )
        z3 = small(f1q2, coef[g, 72 : 72 + K, :K])
        thirds.append(z3)
        taken = lax.dot_general(
            z3, f1q2, (((1,), (1,)), ((), ())), precision=HIGH, preferred_element_type=F32
        )
        wide = jnp.concatenate([taken, jnp.zeros((B, 112), F32)], axis=1)
        strip = strips[g] - pltpu.roll(wide, 96, 1)
        once = pltpu.roll(strip, 16, 1)
        twice = pltpu.roll(strip, 32, 1)
        squared = strip + 2.0 * c * once + c * c * twice
        right = strip + c * once
        parts.append(
            [
                jnp.where(
                    lane < 48,
                    pltpu.roll(squared, 128 - 16 * (i + 1), 1),
                    pltpu.roll(right, 48 - 16 * i, 1),
                )
                for i in (1, 2, 3)
            ]
        )
    system = jnp.concatenate(
        [jnp.where(lane < 64, parts[0][i], pltpu.roll(parts[1][i], 64, 1)) for i in range(3)],
        axis=0,
    )
    solved = transposed(eliminate(system, 48))
    coeffs = []
    for g in range(2):
        c = shifts[g][:, :1]
        ys = solved[64 * g + 48 : 64 * g + 64]
        y1, y2, y3 = (ys[:, 16 * i : 16 * i + 16] for i in range(3))
        z0, z1, z2 = (coef[g, 24 * i : 24 * i + B, :K] for i in range(3))
        on_f = small(y3, thirds[g])
        on_u = z0 - small(y1, z1) - small(y2, z2) - on_f
        none = jnp.zeros((B, K), F32)
        rows = jnp.concatenate(
            [
                jnp.concatenate([on_u, none, y1, y2, y3, jnp.zeros((B, B), F32)], axis=1),
                jnp.concatenate(
                    [none, on_f, -c * y1, -y1 - c * y2, -y2 - c * y3, -y3], axis=1
                ),
            ],
            axis=0,
        )
        coeffs.append(split_coeffs(rows))
    for x in range(0, NX, 2):
        for g in range(2):
            krows = slice(K * g, K * g + K)
            brows = slice(B * g, B * g + B)
            qrows = slice(48 * g, 48 * g + 48)

            def stack(x):
                return jnp.concatenate(
                    [u[x, krows], f[x, krows], q[x, qrows], t[x, brows]], axis=0
                )

            made = combination(
                coeffs[g], jnp.concatenate([stack(x), stack(x + 1)], axis=1)
            )
            for i in range(2):
                part = made[:, NY * i : NY * i + NY]
                solution_out[brows, x + i, :] = part[:B]
                residue_out[brows, x + i, :] = part[B:] + q[x + i, 48 * g : 48 * g + B]


def call(kernel, shapes, scalars, *arrays, final=False):
    if final:
        out = [jax.ShapeDtypeStruct(s, F32) for s in shapes]
    else:
        out = [pltpu.VMEM(s, F32) for s in shapes]
    here = [pltpu.with_memory_space_constraint(a, pltpu.VMEM) for a in arrays[scalars:]]
    return pl.pallas_call(
        kernel,
        out_shape=out,
        in_specs=[SMEM] * scalars + [VMEM] * len(here),
        out_specs=[VMEM] * len(out),
        compiler_params=PARAMS,
        name=kernel.__name__,
    )(*arrays[:scalars], *here)


def everyone(values):
    values = values + lax.ppermute(values, CORES, [(0, 1), (1, 0)])
    for number, axes in enumerate(STAGES):
        if number:
            values = jnp.sum(values, axis=0)
        size = lax.axis_size(axes)
        spread = jnp.broadcast_to(values[None], (size, *values.shape))
        values = lax.all_to_all(spread, axes, 0, 0, tiled=True)
    return values


def beside(values):
    count = lax.axis_size(GRID)
    edges = [(i, i + 1) for i in range(1, count - 1, 2)]
    across = lax.ppermute(values, GRID, edges + [(j, i) for i, j in edges])
    sibling = lax.ppermute(values, CORES, [(0, 1), (1, 0)])
    return across, sibling


def on_device(right_sides, recycle, medium, shift_table, shift_index):
    med = medium[0]
    u = jnp.transpose(recycle.reshape(2 * K, NX, NY), (1, 0, 2))
    b = jnp.transpose(right_sides.reshape(2 * B, NX, NY), (1, 0, 2))
    u_sides = beside(u)
    b_sides = beside(b)
    (f,) = call(apply_kernel, [(NX, 2 * K, NY)], 2, shift_table, shift_index, u, *u_sides, med)
    f, b_sides = lax.optimization_barrier((f, b_sides))
    f_sides = beside(f)
    b1, first = call(first_gram_kernel, [(NX, 2 * B, NY), (K, 128)], 0, f, b, *b_sides, med)
    fields, gram = call(
        second_gram_kernel, [(NX, 80, NY), (2 * K, 128)], 0, f, *f_sides, b1, first, med
    )
    field_sides = beside(fields)
    q, last, coef, shift = call(
        krylov_kernel,
        [(NX, 96, NY), (NX, 2 * B, NY), (2, 96, 128), (16, 128)],
        0,
        everyone(gram),
        f,
        b,
        fields,
        *field_sides,
        med,
    )
    last_sides = beside(last)
    (basis_gram,) = call(basis_gram_kernel, [(2, 48, 128)], 0, q, fields)
    t, gram = call(
        moment_kernel, [(NX, 2 * B, NY), (K, 128)], 0, last, *last_sides, basis_gram, med, shift
    )
    solution, residue = call(
        finish_kernel,
        [(2 * B, NX, NY)] * 2,
        2,
        shift_table,
        shift_index,
        everyone(gram),
        coef,
        shift,
        u,
        f,
        q,
        t,
        final=True,
    )
    return solution.reshape(right_sides.shape), residue.reshape(right_sides.shape)


def solution(mesh):
    torus = Mesh(mesh.devices.reshape(4, 4, 8, 2), GRID)
    in_specs = (
        P(None, GRID, None, None),
        P(None, None, GRID, None, None),
        P(GRID, None, None),
        P(),
        P(),
    )
    out_specs = (P(None, GRID, None, None), P(None, GRID, None, None))
    return jax.shard_map(
        on_device, mesh=torus, in_specs=in_specs, out_specs=out_specs, check_vma=False
    )
```

```python
import jax
import jax.numpy as jnp
from jax import lax
from jax.experimental import pallas as pl
from jax.experimental.pallas import tpu as pltpu
from jax.sharding import Mesh
from jax.sharding import PartitionSpec as P

GRID = ("grid_0", "grid_1", "grid_2", "grid_3")
CORES = "grid_3"
STAGES = ("grid_2", ("grid_0", "grid_1"))
NX = 48
NY = 128
K = 24
B = 16
SHIFT = 0.5
HIGH = lax.Precision.HIGHEST
F32 = jnp.float32
BF16 = jnp.bfloat16
VMEM = pl.BlockSpec(memory_space=pltpu.VMEM)
SMEM = pl.BlockSpec(memory_space=pltpu.SMEM)
ANY = pl.BlockSpec(memory_space=pl.ANY)
CHUNK = 8


def iota(shape, dim):
    return lax.broadcasted_iota(jnp.int32, shape, dim)


def small(left, right):
    return jnp.dot(left, right, precision=HIGH, preferred_element_type=F32)


def halves(values):
    top = values.astype(BF16)
    return top, (values - top.astype(F32)).astype(BF16)


def row_products(left, right):
    dims = (((1,), (1,)), ((), ()))
    n = left.shape[0]
    l_top, l_rest = halves(left)
    r_top, r_rest = halves(right)
    both = lax.dot_general(
        jnp.concatenate([l_top, l_rest], axis=0), r_top, dims, preferred_element_type=F32
    )
    last = lax.dot_general(l_top, r_rest, dims, preferred_element_type=F32)
    return both[:n] + both[n:] + last


def combination(coeffs, fields):
    c_both, c_top = coeffs
    n = c_top.shape[0]
    f_top, f_rest = halves(fields)
    both = jnp.dot(c_both, f_top, preferred_element_type=F32)
    last = jnp.dot(c_top, f_rest, preferred_element_type=F32)
    return both[:n] + both[n:] + last


def split_coeffs(coeffs):
    top, rest = halves(coeffs)
    return jnp.concatenate([top, rest], axis=0), top


def neighbours(x, read, before, after):
    f = read(x)
    total = before + after
    if x > 0:
        total = total + read(x - 1)
    if x < NX - 1:
        total = total + read(x + 1)
    lane = iota(f.shape, 1)
    total = total + jnp.where(lane == 0, 0.0, pltpu.roll(f, 1, 1))
    return total + jnp.where(lane == NY - 1, 0.0, pltpu.roll(f, NY - 1, 1))


def transposed(values):
    rows = values.shape[0]
    return jnp.concatenate([values, jnp.zeros((128 - rows, 128), F32)], axis=0).T


def eliminate(system, count, meanwhile=None):
    lane = iota((1, 128), 1)
    row = iota(system.shape, 0)

    def column(k):
        return jnp.where(lane < 64, system[:, k : k + 1], system[:, 64 + k : 65 + k])

    for k in range(0, count, 2):
        if meanwhile is not None:
            meanwhile(k // 2)
        one = system[k : k + 1]
        two = system[k + 1 : k + 2]
        left = column(k)
        right = column(k + 1)
        a, b = left[k : k + 1], right[k : k + 1]
        c, d = left[k + 1 : k + 2], right[k + 1 : k + 2]
        inverse = 1.0 / (a * d - b * c)
        new_one = (d * inverse) * one - (b * inverse) * two
        new_two = (a * inverse) * two - (c * inverse) * one
        changed = system - left * new_one - right * new_two
        system = jnp.where(row == k, new_one, jnp.where(row == k + 1, new_two, changed))
    return system


def over_copies(parts):
    total = parts[0]
    for i in range(1, parts.shape[0]):
        total = total + parts[i]
    return total


def planes(ref, start, count):
    return lambda x: ref[start : start + count, x, :]


def stencil(diagonal, own, across, sibling):
    def at(x):
        return diagonal(x) * own(x) - neighbours(x, own, across(x), sibling(x))

    return at


def applied(g, table, index, medium, own, across, sibling):
    base = 6.0 + table[index[g]]
    return stencil(lambda x: medium[x : x + 1, :] + base, own, across, sibling)


def front_kernel(table, index, u, across, sibling, medium, f_out):
    made = applied(
        0, table, index, medium, planes(u, 0, K), planes(across, 0, K), planes(sibling, 0, K)
    )
    for x in range(NX):
        f_out[x] = made(x)


def back_kernel(table, index, ub, across, sibling, medium, f_out, b_out, b1_out):
    made = applied(
        1, table, index, medium, planes(ub, 0, K), planes(across, 0, K), planes(sibling, 0, K)
    )
    own = planes(ub, K, 2 * B)
    shifted = stencil(
        lambda x: medium[x : x + 1, :] - SHIFT,
        own,
        planes(across, K, 2 * B),
        planes(sibling, K, 2 * B),
    )
    for x in range(NX):
        f_out[x] = made(x)
        b_out[x] = own(x)
        b1_out[x] = shifted(x)


def pair(ref, x, rows=slice(None)):
    return jnp.concatenate([ref[x, rows], ref[x + 1, rows]], axis=1)


def first_gram_kernel(f0, f1, b, b1, gram_out):
    total = jnp.zeros((2 * K, 128), F32)
    zeros = jnp.zeros((8, 2 * NY), F32)
    tops = [jnp.zeros((B, NY), F32) for _ in range(2)]
    squares = [jnp.zeros((B, NY), F32) for _ in range(2)]
    for x in range(0, NX, 2):
        fields = [pair(f0, x), pair(f1, x)]
        b_pair = pair(b, x)
        b1_pair = pair(b1, x)
        right = []
        for g in range(2):
            bg = b_pair[B * g : B * g + B]
            b1g = b1_pair[B * g : B * g + B]
            right += [fields[g], bg, b1g, zeros]
            top = bg * b1g
            square = bg * bg
            tops[g] = tops[g] + top[:, :NY] + top[:, NY:]
            squares[g] = squares[g] + square[:, :NY] + square[:, NY:]
        total = total + row_products(
            jnp.concatenate(fields, axis=0), jnp.concatenate(right, axis=0)
        )
    lane = iota((K, 128), 1)
    row = iota((K, 128), 0)
    packed = jnp.where(lane < 64, total[:K], total[K:])
    for g in range(2):
        here = (row == 0) & (lane == 64 * g + 56)
        packed = jnp.where(here, jnp.sum(tops[g], keepdims=True), packed)
        here = (row == 0) & (lane == 64 * g + 57)
        packed = jnp.where(here, jnp.sum(squares[g], keepdims=True), packed)
    gram_out[...] = packed


def rows_of(ref):
    return lambda x: ref[x]


def second_gram_kernel(
    f0, f0_across, f0_sibling, f1, f1_across, f1_sibling, b1, first, medium, fields_out, gram_out
):
    total = jnp.zeros((2 * K, 128), F32)
    made = [
        stencil(
            lambda x: medium[x : x + 1, :] - SHIFT, rows_of(own), rows_of(across), rows_of(sibling)
        )
        for own, across, sibling in ((f0, f0_across, f0_sibling), (f1, f1_across, f1_sibling))
    ]
    for x in range(0, NX, 2):
        nexts = []
        for g in range(2):
            ends = [made[g](x), made[g](x + 1)]
            for i in range(2):
                fields_out[x + i, K * g : K * g + K] = ends[i]
            nexts.append(jnp.concatenate(ends, axis=1))
        b1_pair = pair(b1, x)
        right = [
            pair(f0, x),
            nexts[0],
            b1_pair[:B],
            pair(f1, x),
            nexts[1],
            b1_pair[B:],
        ]
        total = total + row_products(
            jnp.concatenate(nexts, axis=0), jnp.concatenate(right, axis=0)
        )
    lane = iota((K, 128), 1)
    gram_out[:K] = first[...]
    gram_out[K:] = jnp.where(lane < 64, total[:K], total[K:])


def krylov_kernel(
    grams,
    f0,
    f1,
    b,
    b1,
    b1_across,
    b1_sibling,
    fields,
    fields_across,
    fields_sibling,
    medium,
    q_out,
    last_out,
    coef_out,
    shift_out,
    f_next,
    b_next,
):
    def plain(x):
        return medium[x : x + 1, :] - SHIFT

    next_f = stencil(plain, rows_of(fields), rows_of(fields_across), rows_of(fields_sibling))
    next_b = stencil(plain, rows_of(b1), rows_of(b1_across), rows_of(b1_sibling))

    def meanwhile(step):
        for x in range(4 * step, 4 * step + 4):
            f_next[x] = next_f(x)
            b_next[x] = next_b(x)

    gram = over_copies(grams)
    first = gram[:K]
    lane = iota((K, 128), 1)
    row = iota((K, 128), 0)
    place = lane & 63
    unit = jnp.where(place == row + K, 1.0, 0.0)
    inverse_t = transposed(eliminate(jnp.where(place < K, first, unit), K, meanwhile))
    first_t = transposed(first)
    second_t = transposed(gram[K:])
    coeffs = []
    thetas = []
    for g in range(2):
        at = 64 * g
        ginv = inverse_t[at + K : at + 2 * K, :K]
        fb = first_t[at + K : at + K + B, :K]
        fb1 = first_t[at + K + B : at + K + 2 * B, :K]
        ff1 = second_t[at : at + K, :K]
        f1f1 = second_t[at + K : at + 2 * K, :K]
        f1b1 = second_t[at + 2 * K : at + 2 * K + B, :K]
        theta = first_t[at + 56 : at + 57, :1] / first_t[at + 57 : at + 58, :1]
        z0 = small(fb, ginv)
        z1 = small(fb1 - small(z0, ff1), ginv)
        z2 = small(f1b1 - small(z0, f1f1) - small(z1, ff1), ginv)
        z2 = z2 - theta * z1
        mixed = z1 - theta * z0
        zero = jnp.zeros((B, K), F32)
        pad = jnp.zeros((B, 8), F32)
        table = jnp.concatenate(
            [
                jnp.concatenate([z0, zero, zero, pad], axis=1),
                jnp.concatenate([mixed, z0, zero, pad], axis=1),
                jnp.concatenate([z2 - theta * mixed, mixed - theta * z0, z0, pad], axis=1),
            ],
            axis=0,
        )
        coeffs.append(split_coeffs(-table))
        thetas.append(theta)
        for i, z in enumerate((z0, z1, z2, ginv)):
            coef_out[g, 24 * i : 24 * i + z.shape[0], :K] = z
        shift_out[8 * g : 8 * g + 8, :] = jnp.broadcast_to(theta, (8, 128))
    zeros = jnp.zeros((8, 2 * NY), F32)
    for x in range(0, NX, 2):
        for g in range(2):
            frows = slice(K * g, K * g + K)
            brows = slice(B * g, B * g + B)
            theta = thetas[g]
            made = combination(
                coeffs[g],
                jnp.concatenate(
                    [pair((f0, f1)[g], x), pair(fields, x, frows), pair(f_next, x, frows), zeros],
                    axis=0,
                ),
            )
            b_own = pair(b, x, brows)
            b_one = pair(b1, x, brows)
            q1 = b_one - theta * b_own
            q2 = (pair(b_next, x, brows) - theta * b_one) - theta * q1
            made = made + jnp.concatenate([b_own, q1, q2], axis=0)
            for i in range(2):
                part = made[:, NY * i : NY * i + NY]
                q_out[x + i, 48 * g : 48 * g + 48] = part
                last_out[x + i, brows] = part[2 * B :]


def basis_gram_kernel(q, fields, gram_out):
    for g in range(2):
        qrows = slice(48 * g, 48 * g + 48)
        frows = slice(K * g, K * g + K)
        total = jnp.zeros((48, 128), F32)
        none = jnp.zeros((B, 2 * NY), F32)
        pad = jnp.zeros((40, 2 * NY), F32)
        for x in range(0, NX, 2):
            left = jnp.concatenate([q[x, qrows], q[x + 1, qrows]], axis=1)
            f1 = jnp.concatenate([fields[x, frows], fields[x + 1, frows]], axis=1)
            total = total + row_products(left, jnp.concatenate([left, none, f1, pad], axis=0))
        gram_out[g] = total


def moment_kernel(last, last_before, last_after, basis_gram, medium, shift, t_out, gram_out):
    def next_field(x, g):
        theta = shift[8 * g : 8 * g + 1, :]
        brows = slice(B * g, B * g + B)
        out = (medium[x : x + 1, :] - SHIFT - theta) * last[x, brows] - neighbours(
            x, lambda i: last[i, brows], last_before[x, brows], last_after[x, brows]
        )
        t_out[x, brows] = out
        return out

    total = jnp.zeros((2 * B, 128), F32)
    pad = jnp.zeros((64, 2 * NY), F32)
    for x in range(0, NX, 2):
        left = []
        right = []
        for g in range(2):
            brows = slice(B * g, B * g + B)
            made = jnp.concatenate([next_field(x, g), next_field(x + 1, g)], axis=1)
            left.append(made)
            right.append(jnp.concatenate([last[x, brows], last[x + 1, brows]], axis=1))
            right.append(made)
        total = total + row_products(
            jnp.concatenate(left, axis=0), jnp.concatenate(right + [pad], axis=0)
        )
    grams = [basis_gram[0], basis_gram[1]]
    ends = [pltpu.roll(total[:B], 80, 1), pltpu.roll(total[B:], 48, 1)]
    lane = iota((B, 128), 1)
    row = iota((B, 128), 0)
    column = lane & 15
    strips = []
    for gram, end in zip(grams, ends):
        middle = jnp.where(lane < 64, pltpu.roll(gram[16:32], 16, 1), pltpu.roll(gram[32:48], 32, 1))
        strips.append(jnp.where(lane < 32, gram[:16], jnp.where(lane < 80, middle, end)))
    packed = jnp.where(row <= column, strips[0], strips[1])
    packed = jnp.where(lane < 112, packed, 0.0)
    on_diagonal = jnp.where((row == column) & (lane < 112), strips[1], 0.0)
    for k in range(7):
        inside = (lane >= 16 * k) & (lane < 16 * k + 16)
        own = jnp.sum(jnp.where(inside, on_diagonal, 0.0), axis=1, keepdims=True)
        packed = jnp.where(lane == 112 + k, own, packed)
    low = jnp.zeros((8, 128), F32)
    lane8 = iota((8, 128), 1)
    for g in range(2):
        for half in range(2):
            at = 24 * (2 * g + half)
            piece = pltpu.roll(grams[g][32 + 8 * half : 40 + 8 * half], (at - 64) % 128, 1)
            low = jnp.where((lane8 >= at) & (lane8 < at + K), piece, low)
    gram_out[:B] = packed
    gram_out[B:] = low


def finish_kernel(
    table,
    index,
    moments,
    coef,
    shift,
    f0,
    f1,
    t,
    u_far,
    q_far,
    solution_far,
    residue_far,
    u,
    q,
    solution_out,
    residue_out,
    arrived,
    left,
):
    copies = [
        pltpu.make_async_copy(u_far, u, arrived.at[0]),
        pltpu.make_async_copy(q_far, q, arrived.at[1]),
    ]
    for copy in copies:
        copy.start()
    summed = over_copies(moments)
    packed = summed[:B]
    turned = transposed(packed)
    lane = iota((B, 128), 1)
    row = iota((B, 128), 0)
    column = lane & 15
    flipped = turned[:B]
    for k in range(1, 7):
        flipped = flipped + pltpu.roll(turned[16 * k : 16 * k + 16], 16 * k, 1)
    diagonal = packed
    for k in range(7):
        diagonal = jnp.where(
            (lane >= 16 * k) & (lane < 16 * k + 16), packed[:, 112 + k : 113 + k], diagonal
        )
    strips = [
        jnp.where(row <= column, packed, flipped),
        jnp.where(row == column, diagonal, jnp.where(row > column, packed, flipped)),
    ]
    shifts = []
    thirds = []
    blocks = [[], [], []]
    parts = []
    for g in range(2):
        c = 6.0 + SHIFT + table[index[g]] + shift[8 * g : 8 * g + 1, :]
        shifts.append(c)
        at = 48 * g
        f1q2 = jnp.concatenate(
            [summed[B:, at : at + K], summed[B:, at + K : at + 2 * K]], axis=0
        )
        z3 = small(f1q2, coef[g, 72 : 72 + K, :K])
        thirds.append(z3)
        taken = lax.dot_general(
            z3, f1q2, (((1,), (1,)), ((), ())), precision=HIGH, preferred_element_type=F32
        )
        wide = jnp.concatenate([taken, jnp.zeros((B, 112), F32)], axis=1)
        strip = strips[g] - pltpu.roll(wide, 96, 1)
        once = pltpu.roll(strip, 16, 1)
        twice = pltpu.roll(strip, 32, 1)
        squared = strip + 2.0 * c * once + c * c * twice
        right = strip + c * once
        parts.append(
            [
                jnp.where(
                    lane < 48,
                    pltpu.roll(squared, 128 - 16 * (i + 1), 1),
                    pltpu.roll(right, 48 - 16 * i, 1),
                )
                for i in (1, 2, 3)
            ]
        )
    system = jnp.concatenate(
        [jnp.where(lane < 64, parts[0][i], pltpu.roll(parts[1][i], 64, 1)) for i in range(3)],
        axis=0,
    )
    solved = transposed(eliminate(system, 48))
    coeffs = []
    for g in range(2):
        c = shifts[g][:, :1]
        ys = solved[64 * g + 48 : 64 * g + 64]
        y1, y2, y3 = (ys[:, 16 * i : 16 * i + 16] for i in range(3))
        z0, z1, z2 = (coef[g, 24 * i : 24 * i + B, :K] for i in range(3))
        on_f = small(y3, thirds[g])
        on_u = z0 - small(y1, z1) - small(y2, z2) - on_f
        none = jnp.zeros((B, K), F32)
        rows = jnp.concatenate(
            [
                jnp.concatenate([on_u, none, y1, y2, y3, jnp.zeros((B, B), F32)], axis=1),
                jnp.concatenate(
                    [none, on_f, -c * y1, -y1 - c * y2, -y2 - c * y3, -y3], axis=1
                ),
            ],
            axis=0,
        )
        coeffs.append(split_coeffs(rows))
    for copy in copies:
        copy.wait()
    leaving = []
    for x in range(0, NX, 2):
        for g in range(2):
            brows = slice(B * g, B * g + B)
            qrows = slice(48 * g, 48 * g + 48)
            us = jnp.concatenate([u[g, :, x, :], u[g, :, x + 1, :]], axis=1)
            made = combination(
                coeffs[g],
                jnp.concatenate(
                    [us, pair((f0, f1)[g], x), pair(q, x, qrows), pair(t, x, brows)], axis=0
                ),
            )
            for i in range(2):
                part = made[:, NY * i : NY * i + NY]
                solution_out[brows, x + i, :] = part[:B]
                residue_out[brows, x + i, :] = part[B:] + q[x + i, 48 * g : 48 * g + B]
        if (x + 2) % CHUNK == 0:
            rows = pl.ds(x + 2 - CHUNK, CHUNK)
            for near, far in ((solution_out, solution_far), (residue_out, residue_far)):
                copy = pltpu.make_async_copy(
                    near.at[:, rows, :], far.at[:, rows, :], left.at[len(leaving)]
                )
                copy.start()
                leaving.append(copy)
    for copy in leaving:
        copy.wait()


def here(values):
    return pltpu.with_memory_space_constraint(values, pltpu.VMEM)


def call(kernel, shapes, scalars, *arrays, scratch=(), limit=8):
    count = len(arrays) - scalars
    return pl.pallas_call(
        kernel,
        out_shape=[pltpu.VMEM(s, F32) for s in shapes],
        in_specs=[SMEM] * scalars + [VMEM] * count,
        out_specs=[VMEM] * len(shapes),
        scratch_shapes=[pltpu.VMEM(s, F32) for s in scratch],
        compiler_params=pltpu.CompilerParams(vmem_limit_bytes=limit << 20),
        name=kernel.__name__,
    )(*arrays[:scalars], *(here(a) for a in arrays[scalars:]))


def finish(scalars, near, far, shape):
    copies = 2 * NX // CHUNK
    return pl.pallas_call(
        finish_kernel,
        out_shape=[jax.ShapeDtypeStruct(shape, F32)] * 2,
        in_specs=[SMEM] * len(scalars) + [VMEM] * len(near) + [ANY] * len(far),
        out_specs=[ANY] * 2,
        scratch_shapes=[pltpu.VMEM(a.shape, F32) for a in far]
        + [pltpu.VMEM(shape, F32)] * 2
        + [pltpu.SemaphoreType.DMA((len(far),)), pltpu.SemaphoreType.DMA((copies,))],
        compiler_params=pltpu.CompilerParams(vmem_limit_bytes=14 << 20),
        name="finish_kernel",
    )(*scalars, *(here(a) for a in near), *far)


def add_kernel(one, two, out):
    total = one[...] + two[...]
    for i in range(out.shape[0]):
        out[i] = total


def respread_kernel(parts, out):
    total = over_copies(parts)
    for i in range(out.shape[0]):
        out[i] = total


def everyone(values):
    far, near = STAGES
    other = lax.ppermute(values, CORES, [(0, 1), (1, 0)])
    (spread,) = call(add_kernel, [(lax.axis_size(far), *values.shape)], 0, values, other)
    parts = lax.all_to_all(spread, far, 0, 0, tiled=True)
    (spread,) = call(respread_kernel, [(lax.axis_size(near), *values.shape)], 0, parts)
    return lax.all_to_all(spread, near, 0, 0, tiled=True)


def beside(values):
    count = lax.axis_size(GRID)
    edges = [(i, i + 1) for i in range(1, count - 1, 2)]
    across = lax.ppermute(values, GRID, edges + [(j, i) for i, j in edges])
    sibling = lax.ppermute(values, CORES, [(0, 1), (1, 0)])
    return across, sibling


def on_device(right_sides, recycle, medium, shift_table, shift_index):
    med = medium[0]
    u = recycle.reshape(2, K, NX, NY)
    b = right_sides.reshape(2 * B, NX, NY)
    scalars = (shift_table, shift_index)
    back = jnp.concatenate([u[1], b], axis=0)
    back_sides = beside(back)
    front = u[0]
    front_across, front_sibling = beside(front)
    f1, b, b1 = call(
        back_kernel,
        [(NX, K, NY), (NX, 2 * B, NY), (NX, 2 * B, NY)],
        2,
        *scalars,
        back,
        *back_sides,
        med,
    )
    f1_sides = beside(f1)
    front_across, b1 = lax.optimization_barrier((front_across, b1))
    (f0,) = call(
        front_kernel, [(NX, K, NY)], 2, *scalars, front, front_across, front_sibling, med
    )
    f0_sides = beside(f0)
    b1_sides = beside(b1)
    (first,) = call(first_gram_kernel, [(K, 128)], 0, f0, f1, b, b1)
    fields, gram = call(
        second_gram_kernel,
        [(NX, 2 * K, NY), (2 * K, 128)],
        0,
        f0,
        *f0_sides,
        f1,
        *f1_sides,
        b1,
        first,
        med,
    )
    field_sides = beside(fields)
    q, last, coef, shift = call(
        krylov_kernel,
        [(NX, 96, NY), (NX, 2 * B, NY), (2, 96, 128), (16, 128)],
        0,
        everyone(gram),
        f0,
        f1,
        b,
        b1,
        *b1_sides,
        fields,
        *field_sides,
        med,
        scratch=[(NX, 2 * K, NY), (NX, 2 * B, NY)],
    )
    last_sides = beside(last)
    (basis_gram,) = call(basis_gram_kernel, [(2, 48, 128)], 0, q, fields)
    t, gram = call(
        moment_kernel, [(NX, 2 * B, NY), (K, 128)], 0, last, *last_sides, basis_gram, med, shift
    )
    solution, residue = finish(
        scalars, (everyone(gram), coef, shift, f0, f1, t), (u, q), (2 * B, NX, NY)
    )
    return solution.reshape(right_sides.shape), residue.reshape(right_sides.shape)


def solution(mesh):
    torus = Mesh(mesh.devices.reshape(4, 4, 8, 2), GRID)
    in_specs = (
        P(None, GRID, None, None),
        P(None, None, GRID, None, None),
        P(GRID, None, None),
        P(),
        P(),
    )
    out_specs = (P(None, GRID, None, None), P(None, GRID, None, None))
    return jax.shard_map(
        on_device, mesh=torus, in_specs=in_specs, out_specs=out_specs, check_vma=False
    )
```

```python
import jax
import jax.numpy as jnp
from jax import lax
from jax.experimental import pallas as pl
from jax.experimental.pallas import tpu as pltpu
from jax.sharding import Mesh
from jax.sharding import PartitionSpec as P

GRID = ("grid_0", "grid_1", "grid_2", "grid_3")
CORES = "grid_3"
STAGES = ("grid_2", ("grid_0", "grid_1"))
NX = 48
NY = 128
K = 24
B = 16
SHIFT = 0.5
HIGH = lax.Precision.HIGHEST
F32 = jnp.float32
BF16 = jnp.bfloat16
VMEM = pl.BlockSpec(memory_space=pltpu.VMEM)
SMEM = pl.BlockSpec(memory_space=pltpu.SMEM)
ANY = pl.BlockSpec(memory_space=pl.ANY)
CHUNK = 8


def iota(shape, dim):
    return lax.broadcasted_iota(jnp.int32, shape, dim)


def small(left, right):
    return jnp.dot(left, right, precision=HIGH, preferred_element_type=F32)


def halves(values):
    top = values.astype(BF16)
    return top, (values - top.astype(F32)).astype(BF16)


def row_products(left, right):
    dims = (((1,), (1,)), ((), ()))
    n = left.shape[0]
    l_top, l_rest = halves(left)
    r_top, r_rest = halves(right)
    both = lax.dot_general(
        jnp.concatenate([l_top, l_rest], axis=0), r_top, dims, preferred_element_type=F32
    )
    last = lax.dot_general(l_top, r_rest, dims, preferred_element_type=F32)
    return both[:n] + both[n:] + last


def combination(coeffs, fields):
    c_both, c_top = coeffs
    n = c_top.shape[0]
    f_top, f_rest = halves(fields)
    both = jnp.dot(c_both, f_top, preferred_element_type=F32)
    last = jnp.dot(c_top, f_rest, preferred_element_type=F32)
    return both[:n] + both[n:] + last


def split_coeffs(coeffs):
    top, rest = halves(coeffs)
    return jnp.concatenate([top, rest], axis=0), top


def neighbours(x, read, before, after):
    f = read(x)
    total = before + after
    if x > 0:
        total = total + read(x - 1)
    if x < NX - 1:
        total = total + read(x + 1)
    lane = iota(f.shape, 1)
    total = total + jnp.where(lane == 0, 0.0, pltpu.roll(f, 1, 1))
    return total + jnp.where(lane == NY - 1, 0.0, pltpu.roll(f, NY - 1, 1))


def transposed(values):
    rows = values.shape[0]
    return jnp.concatenate([values, jnp.zeros((128 - rows, 128), F32)], axis=0).T


def eliminate(system, count, meanwhile=None):
    lane = iota((1, 128), 1)
    row = iota(system.shape, 0)

    def column(k):
        return jnp.where(lane < 64, system[:, k : k + 1], system[:, 64 + k : 65 + k])

    for k in range(0, count, 2):
        if meanwhile is not None:
            meanwhile(k // 2)
        one = system[k : k + 1]
        two = system[k + 1 : k + 2]
        left = column(k)
        right = column(k + 1)
        a, b = left[k : k + 1], right[k : k + 1]
        c, d = left[k + 1 : k + 2], right[k + 1 : k + 2]
        inverse = 1.0 / (a * d - b * c)
        new_one = (d * inverse) * one - (b * inverse) * two
        new_two = (a * inverse) * two - (c * inverse) * one
        changed = system - left * new_one - right * new_two
        system = jnp.where(row == k, new_one, jnp.where(row == k + 1, new_two, changed))
    return system


def over_copies(parts):
    total = parts[0]
    for i in range(1, parts.shape[0]):
        total = total + parts[i]
    return total


def planes(ref, start, count):
    return lambda x: ref[x, start : start + count]


def stencil(diagonal, own, across, sibling):
    def at(x):
        return diagonal(x) * own(x) - neighbours(x, own, across(x), sibling(x))

    return at


def applied(g, table, index, medium, own, across, sibling):
    base = 6.0 + table[index[g]]
    return stencil(lambda x: medium[x : x + 1, :] + base, own, across, sibling)


def front_kernel(table, index, u, across, sibling, medium, f_out):
    made = applied(
        0, table, index, medium, planes(u, 0, K), planes(across, 0, K), planes(sibling, 0, K)
    )
    for x in range(NX):
        f_out[x] = made(x)


def back_kernel(table, index, ub, across, sibling, medium, f_out, b_out, b1_out):
    made = applied(
        1, table, index, medium, planes(ub, 0, K), planes(across, 0, K), planes(sibling, 0, K)
    )
    own = planes(ub, K, 2 * B)
    shifted = stencil(
        lambda x: medium[x : x + 1, :] - SHIFT,
        own,
        planes(across, K, 2 * B),
        planes(sibling, K, 2 * B),
    )
    for x in range(NX):
        f_out[x] = made(x)
        b_out[x] = own(x)
        b1_out[x] = shifted(x)


def pair(ref, x, rows=slice(None)):
    return jnp.concatenate([ref[x, rows], ref[x + 1, rows]], axis=1)


def first_gram_kernel(f0, f1, b, b1, gram_out):
    total = jnp.zeros((2 * K, 128), F32)
    zeros = jnp.zeros((8, 2 * NY), F32)
    tops = [jnp.zeros((B, NY), F32) for _ in range(2)]
    squares = [jnp.zeros((B, NY), F32) for _ in range(2)]
    for x in range(0, NX, 2):
        fields = [pair(f0, x), pair(f1, x)]
        b_pair = pair(b, x)
        b1_pair = pair(b1, x)
        right = []
        for g in range(2):
            bg = b_pair[B * g : B * g + B]
            b1g = b1_pair[B * g : B * g + B]
            right += [fields[g], bg, b1g, zeros]
            top = bg * b1g
            square = bg * bg
            tops[g] = tops[g] + top[:, :NY] + top[:, NY:]
            squares[g] = squares[g] + square[:, :NY] + square[:, NY:]
        total = total + row_products(
            jnp.concatenate(fields, axis=0), jnp.concatenate(right, axis=0)
        )
    lane = iota((K, 128), 1)
    row = iota((K, 128), 0)
    packed = jnp.where(lane < 64, total[:K], total[K:])
    for g in range(2):
        here = (row == 0) & (lane == 64 * g + 56)
        packed = jnp.where(here, jnp.sum(tops[g], keepdims=True), packed)
        here = (row == 0) & (lane == 64 * g + 57)
        packed = jnp.where(here, jnp.sum(squares[g], keepdims=True), packed)
    gram_out[...] = packed


def rows_of(ref):
    return lambda x: ref[x]


def second_gram_kernel(
    f0, f0_across, f0_sibling, f1, f1_across, f1_sibling, b1, first, medium, fields_out, gram_out
):
    total = jnp.zeros((2 * K, 128), F32)
    made = [
        stencil(
            lambda x: medium[x : x + 1, :] - SHIFT, rows_of(own), rows_of(across), rows_of(sibling)
        )
        for own, across, sibling in ((f0, f0_across, f0_sibling), (f1, f1_across, f1_sibling))
    ]
    for x in range(0, NX, 2):
        nexts = []
        for g in range(2):
            ends = [made[g](x), made[g](x + 1)]
            for i in range(2):
                fields_out[x + i, K * g : K * g + K] = ends[i]
            nexts.append(jnp.concatenate(ends, axis=1))
        b1_pair = pair(b1, x)
        right = [
            pair(f0, x),
            nexts[0],
            b1_pair[:B],
            pair(f1, x),
            nexts[1],
            b1_pair[B:],
        ]
        total = total + row_products(
            jnp.concatenate(nexts, axis=0), jnp.concatenate(right, axis=0)
        )
    lane = iota((K, 128), 1)
    gram_out[:K] = first[...]
    gram_out[K:] = jnp.where(lane < 64, total[:K], total[K:])


def krylov_kernel(
    grams,
    f0,
    f1,
    b,
    b1,
    b1_across,
    b1_sibling,
    fields,
    fields_across,
    fields_sibling,
    medium,
    q_out,
    last_out,
    coef_out,
    shift_out,
    f_next,
    b_next,
):
    def plain(x):
        return medium[x : x + 1, :] - SHIFT

    next_f = stencil(plain, rows_of(fields), rows_of(fields_across), rows_of(fields_sibling))
    next_b = stencil(plain, rows_of(b1), rows_of(b1_across), rows_of(b1_sibling))

    def meanwhile(step):
        for x in range(4 * step, 4 * step + 4):
            f_next[x] = next_f(x)
            b_next[x] = next_b(x)

    gram = over_copies(grams)
    first = gram[:K]
    lane = iota((K, 128), 1)
    row = iota((K, 128), 0)
    place = lane & 63
    unit = jnp.where(place == row + K, 1.0, 0.0)
    inverse_t = transposed(eliminate(jnp.where(place < K, first, unit), K, meanwhile))
    first_t = transposed(first)
    second_t = transposed(gram[K:])
    coeffs = []
    thetas = []
    for g in range(2):
        at = 64 * g
        ginv = inverse_t[at + K : at + 2 * K, :K]
        fb = first_t[at + K : at + K + B, :K]
        fb1 = first_t[at + K + B : at + K + 2 * B, :K]
        ff1 = second_t[at : at + K, :K]
        f1f1 = second_t[at + K : at + 2 * K, :K]
        f1b1 = second_t[at + 2 * K : at + 2 * K + B, :K]
        theta = first_t[at + 56 : at + 57, :1] / first_t[at + 57 : at + 58, :1]
        z0 = small(fb, ginv)
        z1 = small(fb1 - small(z0, ff1), ginv)
        z2 = small(f1b1 - small(z0, f1f1) - small(z1, ff1), ginv)
        z2 = z2 - theta * z1
        mixed = z1 - theta * z0
        zero = jnp.zeros((B, K), F32)
        pad = jnp.zeros((B, 8), F32)
        table = jnp.concatenate(
            [
                jnp.concatenate([z0, zero, zero, pad], axis=1),
                jnp.concatenate([mixed, z0, zero, pad], axis=1),
                jnp.concatenate([z2 - theta * mixed, mixed - theta * z0, z0, pad], axis=1),
            ],
            axis=0,
        )
        coeffs.append(split_coeffs(-table))
        thetas.append(theta)
        for i, z in enumerate((z0, z1, z2, ginv)):
            coef_out[g, 24 * i : 24 * i + z.shape[0], :K] = z
        shift_out[8 * g : 8 * g + 8, :] = jnp.broadcast_to(theta, (8, 128))
    zeros = jnp.zeros((8, 2 * NY), F32)
    for x in range(0, NX, 2):
        for g in range(2):
            frows = slice(K * g, K * g + K)
            brows = slice(B * g, B * g + B)
            theta = thetas[g]
            made = combination(
                coeffs[g],
                jnp.concatenate(
                    [pair((f0, f1)[g], x), pair(fields, x, frows), pair(f_next, x, frows), zeros],
                    axis=0,
                ),
            )
            b_own = pair(b, x, brows)
            b_one = pair(b1, x, brows)
            q1 = b_one - theta * b_own
            q2 = (pair(b_next, x, brows) - theta * b_one) - theta * q1
            made = made + jnp.concatenate([b_own, q1, q2], axis=0)
            for i in range(2):
                part = made[:, NY * i : NY * i + NY]
                q_out[x + i, 48 * g : 48 * g + 48] = part
                last_out[x + i, brows] = part[2 * B :]


def basis_gram_kernel(q, fields, gram_out):
    for g in range(2):
        qrows = slice(48 * g, 48 * g + 48)
        frows = slice(K * g, K * g + K)
        total = jnp.zeros((48, 128), F32)
        none = jnp.zeros((B, 2 * NY), F32)
        pad = jnp.zeros((40, 2 * NY), F32)
        for x in range(0, NX, 2):
            left = jnp.concatenate([q[x, qrows], q[x + 1, qrows]], axis=1)
            f1 = jnp.concatenate([fields[x, frows], fields[x + 1, frows]], axis=1)
            total = total + row_products(left, jnp.concatenate([left, none, f1, pad], axis=0))
        gram_out[g] = total


def moment_kernel(last, last_before, last_after, basis_gram, medium, shift, t_out, gram_out):
    def next_field(x, g):
        theta = shift[8 * g : 8 * g + 1, :]
        brows = slice(B * g, B * g + B)
        out = (medium[x : x + 1, :] - SHIFT - theta) * last[x, brows] - neighbours(
            x, lambda i: last[i, brows], last_before[x, brows], last_after[x, brows]
        )
        t_out[x, brows] = out
        return out

    total = jnp.zeros((2 * B, 128), F32)
    pad = jnp.zeros((64, 2 * NY), F32)
    for x in range(0, NX, 2):
        left = []
        right = []
        for g in range(2):
            brows = slice(B * g, B * g + B)
            made = jnp.concatenate([next_field(x, g), next_field(x + 1, g)], axis=1)
            left.append(made)
            right.append(jnp.concatenate([last[x, brows], last[x + 1, brows]], axis=1))
            right.append(made)
        total = total + row_products(
            jnp.concatenate(left, axis=0), jnp.concatenate(right + [pad], axis=0)
        )
    grams = [basis_gram[0], basis_gram[1]]
    ends = [pltpu.roll(total[:B], 80, 1), pltpu.roll(total[B:], 48, 1)]
    lane = iota((B, 128), 1)
    row = iota((B, 128), 0)
    column = lane & 15
    strips = []
    for gram, end in zip(grams, ends):
        middle = jnp.where(lane < 64, pltpu.roll(gram[16:32], 16, 1), pltpu.roll(gram[32:48], 32, 1))
        strips.append(jnp.where(lane < 32, gram[:16], jnp.where(lane < 80, middle, end)))
    packed = jnp.where(row <= column, strips[0], strips[1])
    packed = jnp.where(lane < 112, packed, 0.0)
    on_diagonal = jnp.where((row == column) & (lane < 112), strips[1], 0.0)
    for k in range(7):
        inside = (lane >= 16 * k) & (lane < 16 * k + 16)
        own = jnp.sum(jnp.where(inside, on_diagonal, 0.0), axis=1, keepdims=True)
        packed = jnp.where(lane == 112 + k, own, packed)
    low = jnp.zeros((8, 128), F32)
    lane8 = iota((8, 128), 1)
    for g in range(2):
        for half in range(2):
            at = 24 * (2 * g + half)
            piece = pltpu.roll(grams[g][32 + 8 * half : 40 + 8 * half], (at - 64) % 128, 1)
            low = jnp.where((lane8 >= at) & (lane8 < at + K), piece, low)
    gram_out[:B] = packed
    gram_out[B:] = low


def finish_kernel(
    table,
    index,
    moments,
    coef,
    shift,
    f0,
    f1,
    t,
    u0_far,
    u1_far,
    q_far,
    solution_far,
    residue_far,
    u0,
    u1,
    q,
    solution_out,
    residue_out,
    arrived,
    left,
):
    copies = [
        pltpu.make_async_copy(u0_far, u0, arrived.at[0]),
        pltpu.make_async_copy(u1_far, u1, arrived.at[1]),
        pltpu.make_async_copy(q_far, q, arrived.at[2]),
    ]
    for copy in copies:
        copy.start()
    summed = over_copies(moments)
    packed = summed[:B]
    turned = transposed(packed)
    lane = iota((B, 128), 1)
    row = iota((B, 128), 0)
    column = lane & 15
    flipped = turned[:B]
    for k in range(1, 7):
        flipped = flipped + pltpu.roll(turned[16 * k : 16 * k + 16], 16 * k, 1)
    diagonal = packed
    for k in range(7):
        diagonal = jnp.where(
            (lane >= 16 * k) & (lane < 16 * k + 16), packed[:, 112 + k : 113 + k], diagonal
        )
    strips = [
        jnp.where(row <= column, packed, flipped),
        jnp.where(row == column, diagonal, jnp.where(row > column, packed, flipped)),
    ]
    shifts = []
    thirds = []
    blocks = [[], [], []]
    parts = []
    for g in range(2):
        c = 6.0 + SHIFT + table[index[g]] + shift[8 * g : 8 * g + 1, :]
        shifts.append(c)
        at = 48 * g
        f1q2 = jnp.concatenate(
            [summed[B:, at : at + K], summed[B:, at + K : at + 2 * K]], axis=0
        )
        z3 = small(f1q2, coef[g, 72 : 72 + K, :K])
        thirds.append(z3)
        taken = lax.dot_general(
            z3, f1q2, (((1,), (1,)), ((), ())), precision=HIGH, preferred_element_type=F32
        )
        wide = jnp.concatenate([taken, jnp.zeros((B, 112), F32)], axis=1)
        strip = strips[g] - pltpu.roll(wide, 96, 1)
        once = pltpu.roll(strip, 16, 1)
        twice = pltpu.roll(strip, 32, 1)
        squared = strip + 2.0 * c * once + c * c * twice
        right = strip + c * once
        parts.append(
            [
                jnp.where(
                    lane < 48,
                    pltpu.roll(squared, 128 - 16 * (i + 1), 1),
                    pltpu.roll(right, 48 - 16 * i, 1),
                )
                for i in (1, 2, 3)
            ]
        )
    system = jnp.concatenate(
        [jnp.where(lane < 64, parts[0][i], pltpu.roll(parts[1][i], 64, 1)) for i in range(3)],
        axis=0,
    )
    solved = transposed(eliminate(system, 48))
    coeffs = []
    for g in range(2):
        c = shifts[g][:, :1]
        ys = solved[64 * g + 48 : 64 * g + 64]
        y1, y2, y3 = (ys[:, 16 * i : 16 * i + 16] for i in range(3))
        z0, z1, z2 = (coef[g, 24 * i : 24 * i + B, :K] for i in range(3))
        on_f = small(y3, thirds[g])
        on_u = z0 - small(y1, z1) - small(y2, z2) - on_f
        none = jnp.zeros((B, K), F32)
        rows = jnp.concatenate(
            [
                jnp.concatenate([on_u, none, y1, y2, y3, jnp.zeros((B, B), F32)], axis=1),
                jnp.concatenate(
                    [none, on_f, -c * y1, -y1 - c * y2, -y2 - c * y3, -y3], axis=1
                ),
            ],
            axis=0,
        )
        coeffs.append(split_coeffs(rows))
    for copy in copies:
        copy.wait()
    leaving = []
    for x in range(0, NX, 2):
        for g in range(2):
            brows = slice(B * g, B * g + B)
            qrows = slice(48 * g, 48 * g + 48)
            made = combination(
                coeffs[g],
                jnp.concatenate(
                    [pair((u0, u1)[g], x, slice(0, K)), pair((f0, f1)[g], x), pair(q, x, qrows), pair(t, x, brows)], axis=0
                ),
            )
            for i in range(2):
                part = made[:, NY * i : NY * i + NY]
                solution_out[brows, x + i, :] = part[:B]
                residue_out[brows, x + i, :] = part[B:] + q[x + i, 48 * g : 48 * g + B]
        if (x + 2) % CHUNK == 0:
            rows = pl.ds(x + 2 - CHUNK, CHUNK)
            for near, far in ((solution_out, solution_far), (residue_out, residue_far)):
                copy = pltpu.make_async_copy(
                    near.at[:, rows, :], far.at[:, rows, :], left.at[len(leaving)]
                )
                copy.start()
                leaving.append(copy)
    for copy in leaving:
        copy.wait()


def here(values):
    return pltpu.with_memory_space_constraint(values, pltpu.VMEM)


def call(kernel, shapes, scalars, *arrays, scratch=(), limit=8):
    count = len(arrays) - scalars
    return pl.pallas_call(
        kernel,
        out_shape=[pltpu.VMEM(s, F32) for s in shapes],
        in_specs=[SMEM] * scalars + [VMEM] * count,
        out_specs=[VMEM] * len(shapes),
        scratch_shapes=[pltpu.VMEM(s, F32) for s in scratch],
        compiler_params=pltpu.CompilerParams(vmem_limit_bytes=limit << 20),
        name=kernel.__name__,
    )(*arrays[:scalars], *(here(a) for a in arrays[scalars:]))


def finish(scalars, near, far, shape):
    copies = 2 * NX // CHUNK
    return pl.pallas_call(
        finish_kernel,
        out_shape=[jax.ShapeDtypeStruct(shape, F32)] * 2,
        in_specs=[SMEM] * len(scalars) + [VMEM] * len(near) + [ANY] * len(far),
        out_specs=[ANY] * 2,
        scratch_shapes=[pltpu.VMEM(a.shape, F32) for a in far]
        + [pltpu.VMEM(shape, F32)] * 2
        + [pltpu.SemaphoreType.DMA((len(far),)), pltpu.SemaphoreType.DMA((copies,))],
        compiler_params=pltpu.CompilerParams(vmem_limit_bytes=14 << 20),
        name="finish_kernel",
    )(*scalars, *(here(a) for a in near), *far)


def add_kernel(one, two, out):
    total = one[...] + two[...]
    for i in range(out.shape[0]):
        out[i] = total


def respread_kernel(parts, out):
    total = over_copies(parts)
    for i in range(out.shape[0]):
        out[i] = total


def everyone(values):
    far, near = STAGES
    other = lax.ppermute(values, CORES, [(0, 1), (1, 0)])
    (spread,) = call(add_kernel, [(lax.axis_size(far), *values.shape)], 0, values, other)
    parts = lax.all_to_all(spread, far, 0, 0, tiled=True)
    (spread,) = call(respread_kernel, [(lax.axis_size(near), *values.shape)], 0, parts)
    return lax.all_to_all(spread, near, 0, 0, tiled=True)


def beside(values):
    count = lax.axis_size(GRID)
    edges = [(i, i + 1) for i in range(1, count - 1, 2)]
    across = lax.ppermute(values, GRID, edges + [(j, i) for i, j in edges])
    sibling = lax.ppermute(values, CORES, [(0, 1), (1, 0)])
    return across, sibling


def on_device(right_sides, recycle, medium, shift_table, shift_index):
    med = medium[0]
    u = recycle.reshape(2, K, NX, NY)
    b = right_sides.reshape(2 * B, NX, NY)
    scalars = (shift_table, shift_index)
    back = jnp.transpose(jnp.concatenate([u[1], b], axis=0), (1, 0, 2))
    back_sides = beside(back)
    front = jnp.transpose(u[0], (1, 0, 2))
    front_across, front_sibling = beside(front)
    f1, b, b1 = call(
        back_kernel,
        [(NX, K, NY), (NX, 2 * B, NY), (NX, 2 * B, NY)],
        2,
        *scalars,
        back,
        *back_sides,
        med,
    )
    f1_sides = beside(f1)
    front_across, f1, f1_sibling = lax.optimization_barrier((front_across, f1, f1_sides[1]))
    f1_sides = (f1_sides[0], f1_sibling)
    (f0,) = call(
        front_kernel, [(NX, K, NY)], 2, *scalars, front, front_across, front_sibling, med
    )
    f0_sides = beside(f0)
    b1_sides = beside(b1)
    (first,) = call(first_gram_kernel, [(K, 128)], 0, f0, f1, b, b1)
    fields, gram = call(
        second_gram_kernel,
        [(NX, 2 * K, NY), (2 * K, 128)],
        0,
        f0,
        *f0_sides,
        f1,
        *f1_sides,
        b1,
        first,
        med,
    )
    field_sides = beside(fields)
    gram, b1_sides = lax.optimization_barrier((gram, b1_sides))
    q, last, coef, shift = call(
        krylov_kernel,
        [(NX, 96, NY), (NX, 2 * B, NY), (2, 96, 128), (16, 128)],
        0,
        everyone(gram),
        f0,
        f1,
        b,
        b1,
        *b1_sides,
        fields,
        *field_sides,
        med,
        scratch=[(NX, 2 * K, NY), (NX, 2 * B, NY)],
    )
    last_sides = beside(last)
    (basis_gram,) = call(basis_gram_kernel, [(2, 48, 128)], 0, q, fields)
    t, gram = call(
        moment_kernel, [(NX, 2 * B, NY), (K, 128)], 0, last, *last_sides, basis_gram, med, shift
    )
    solution, residue = finish(
        scalars, (everyone(gram), coef, shift, f0, f1, t), (front, back, q), (2 * B, NX, NY)
    )
    return solution.reshape(right_sides.shape), residue.reshape(right_sides.shape)


def solution(mesh):
    torus = Mesh(mesh.devices.reshape(4, 4, 8, 2), GRID)
    in_specs = (
        P(None, GRID, None, None),
        P(None, None, GRID, None, None),
        P(GRID, None, None),
        P(),
        P(),
    )
    out_specs = (P(None, GRID, None, None), P(None, GRID, None, None))
    return jax.shard_map(
        on_device, mesh=torus, in_specs=in_specs, out_specs=out_specs, check_vma=False
    )
```

```python
import jax
import jax.numpy as jnp
from jax import lax
from jax.experimental import pallas as pl
from jax.experimental.pallas import tpu as pltpu
from jax.sharding import Mesh
from jax.sharding import PartitionSpec as P

GRID = ("grid_0", "grid_1", "grid_2", "grid_3")
CORES = "grid_3"
STAGES = ("grid_2", ("grid_0", "grid_1"))
NX = 48
NY = 128
K = 24
B = 16
SHIFT = 0.5
HIGH = lax.Precision.HIGHEST
F32 = jnp.float32
BF16 = jnp.bfloat16
VMEM = pl.BlockSpec(memory_space=pltpu.VMEM)
SMEM = pl.BlockSpec(memory_space=pltpu.SMEM)
ANY = pl.BlockSpec(memory_space=pl.ANY)
CHUNK = 8


def iota(shape, dim):
    return lax.broadcasted_iota(jnp.int32, shape, dim)


def small(left, right):
    return jnp.dot(left, right, precision=HIGH, preferred_element_type=F32)


def halves(values):
    top = values.astype(BF16)
    return top, (values - top.astype(F32)).astype(BF16)


def row_products(left, right):
    dims = (((1,), (1,)), ((), ()))
    n = left.shape[0]
    l_top, l_rest = halves(left)
    r_top, r_rest = halves(right)
    both = lax.dot_general(
        jnp.concatenate([l_top, l_rest], axis=0), r_top, dims, preferred_element_type=F32
    )
    last = lax.dot_general(l_top, r_rest, dims, preferred_element_type=F32)
    return both[:n] + both[n:] + last


def combination(coeffs, fields):
    c_both, c_top = coeffs
    n = c_top.shape[0]
    f_top, f_rest = halves(fields)
    both = jnp.dot(c_both, f_top, preferred_element_type=F32)
    last = jnp.dot(c_top, f_rest, preferred_element_type=F32)
    return both[:n] + both[n:] + last


def split_coeffs(coeffs):
    top, rest = halves(coeffs)
    return jnp.concatenate([top, rest], axis=0), top


def neighbours(x, read, before, after):
    f = read(x)
    total = before + after
    if x > 0:
        total = total + read(x - 1)
    if x < NX - 1:
        total = total + read(x + 1)
    lane = iota(f.shape, 1)
    total = total + jnp.where(lane == 0, 0.0, pltpu.roll(f, 1, 1))
    return total + jnp.where(lane == NY - 1, 0.0, pltpu.roll(f, NY - 1, 1))


def transposed(values):
    rows = values.shape[0]
    return jnp.concatenate([values, jnp.zeros((128 - rows, 128), F32)], axis=0).T


def eliminate(system, count, meanwhile=None):
    lane = iota((1, 128), 1)
    row = iota(system.shape, 0)

    def column(k):
        return jnp.where(lane < 64, system[:, k : k + 1], system[:, 64 + k : 65 + k])

    for k in range(0, count, 2):
        if meanwhile is not None:
            meanwhile(k // 2)
        one = system[k : k + 1]
        two = system[k + 1 : k + 2]
        left = column(k)
        right = column(k + 1)
        a, b = left[k : k + 1], right[k : k + 1]
        c, d = left[k + 1 : k + 2], right[k + 1 : k + 2]
        inverse = 1.0 / (a * d - b * c)
        new_one = (d * inverse) * one - (b * inverse) * two
        new_two = (a * inverse) * two - (c * inverse) * one
        changed = system - left * new_one - right * new_two
        system = jnp.where(row == k, new_one, jnp.where(row == k + 1, new_two, changed))
    return system


def over_copies(parts):
    total = parts[0]
    for i in range(1, parts.shape[0]):
        total = total + parts[i]
    return total


def planes(ref, start, count):
    return lambda x: ref[x, start : start + count]


def stencil(diagonal, own, across, sibling):
    def at(x):
        return diagonal(x) * own(x) - neighbours(x, own, across(x), sibling(x))

    return at


def applied(g, table, index, medium, own, across, sibling):
    base = 6.0 + table[index[g]]
    return stencil(lambda x: medium[x : x + 1, :] + base, own, across, sibling)


def front_kernel(table, index, u, across, sibling, medium, f_out):
    made = applied(
        0, table, index, medium, planes(u, 0, K), planes(across, 0, K), planes(sibling, 0, K)
    )
    for x in range(NX):
        f_out[x] = made(x)


def back_kernel(table, index, ub, across, sibling, medium, f_out, b_out, b1_out):
    made = applied(
        1, table, index, medium, planes(ub, 0, K), planes(across, 0, K), planes(sibling, 0, K)
    )
    own = planes(ub, K, 2 * B)
    shifted = stencil(
        lambda x: medium[x : x + 1, :] - SHIFT,
        own,
        planes(across, K, 2 * B),
        planes(sibling, K, 2 * B),
    )
    for x in range(NX):
        f_out[x] = made(x)
        b_out[x] = own(x)
        b1_out[x] = shifted(x)


def pair(ref, x, rows=slice(None)):
    return jnp.concatenate([ref[x, rows], ref[x + 1, rows]], axis=1)


def first_gram_kernel(f0, f1, b, b1, gram_out):
    total = jnp.zeros((2 * K, 128), F32)
    zeros = jnp.zeros((8, 2 * NY), F32)
    tops = [jnp.zeros((B, NY), F32) for _ in range(2)]
    squares = [jnp.zeros((B, NY), F32) for _ in range(2)]
    for x in range(0, NX, 2):
        fields = [pair(f0, x), pair(f1, x)]
        b_pair = pair(b, x)
        b1_pair = pair(b1, x)
        right = []
        for g in range(2):
            bg = b_pair[B * g : B * g + B]
            b1g = b1_pair[B * g : B * g + B]
            right += [fields[g], bg, b1g, zeros]
            top = bg * b1g
            square = bg * bg
            tops[g] = tops[g] + top[:, :NY] + top[:, NY:]
            squares[g] = squares[g] + square[:, :NY] + square[:, NY:]
        total = total + row_products(
            jnp.concatenate(fields, axis=0), jnp.concatenate(right, axis=0)
        )
    lane = iota((K, 128), 1)
    row = iota((K, 128), 0)
    packed = jnp.where(lane < 64, total[:K], total[K:])
    for g in range(2):
        here = (row == 0) & (lane == 64 * g + 56)
        packed = jnp.where(here, jnp.sum(tops[g], keepdims=True), packed)
        here = (row == 0) & (lane == 64 * g + 57)
        packed = jnp.where(here, jnp.sum(squares[g], keepdims=True), packed)
    gram_out[...] = packed


def rows_of(ref):
    return lambda x: ref[x]


def next_kernel(f0, f0_across, f0_sibling, f1, f1_across, f1_sibling, medium, fields_out):
    for g, (own, across, sibling) in enumerate(
        ((f0, f0_across, f0_sibling), (f1, f1_across, f1_sibling))
    ):
        made = stencil(
            lambda x: medium[x : x + 1, :] - SHIFT, rows_of(own), rows_of(across), rows_of(sibling)
        )
        for x in range(NX):
            fields_out[x, K * g : K * g + K] = made(x)


def second_gram_kernel(f0, f1, fields, b1, first, gram_out):
    total = jnp.zeros((2 * K, 128), F32)
    for x in range(0, NX, 2):
        nexts = pair(fields, x)
        b1_pair = pair(b1, x)
        right = [pair(f0, x), nexts[:K], b1_pair[:B], pair(f1, x), nexts[K:], b1_pair[B:]]
        total = total + row_products(nexts, jnp.concatenate(right, axis=0))
    lane = iota((K, 128), 1)
    gram_out[:K] = first[...]
    gram_out[K:] = jnp.where(lane < 64, total[:K], total[K:])


def krylov_kernel(
    grams,
    f0,
    f1,
    b,
    b1,
    b1_across,
    b1_sibling,
    fields,
    fields_across,
    fields_sibling,
    medium,
    q_out,
    last_out,
    coef_out,
    shift_out,
    f_next,
    b_next,
):
    def plain(x):
        return medium[x : x + 1, :] - SHIFT

    next_f = stencil(plain, rows_of(fields), rows_of(fields_across), rows_of(fields_sibling))
    next_b = stencil(plain, rows_of(b1), rows_of(b1_across), rows_of(b1_sibling))

    def meanwhile(step):
        for x in range(4 * step, 4 * step + 4):
            f_next[x] = next_f(x)
            b_next[x] = next_b(x)

    gram = over_copies(grams)
    first = gram[:K]
    lane = iota((K, 128), 1)
    row = iota((K, 128), 0)
    place = lane & 63
    unit = jnp.where(place == row + K, 1.0, 0.0)
    inverse_t = transposed(eliminate(jnp.where(place < K, first, unit), K, meanwhile))
    first_t = transposed(first)
    second_t = transposed(gram[K:])
    coeffs = []
    thetas = []
    for g in range(2):
        at = 64 * g
        ginv = inverse_t[at + K : at + 2 * K, :K]
        fb = first_t[at + K : at + K + B, :K]
        fb1 = first_t[at + K + B : at + K + 2 * B, :K]
        ff1 = second_t[at : at + K, :K]
        f1f1 = second_t[at + K : at + 2 * K, :K]
        f1b1 = second_t[at + 2 * K : at + 2 * K + B, :K]
        theta = first_t[at + 56 : at + 57, :1] / first_t[at + 57 : at + 58, :1]
        z0 = small(fb, ginv)
        z1 = small(fb1 - small(z0, ff1), ginv)
        z2 = small(f1b1 - small(z0, f1f1) - small(z1, ff1), ginv)
        z2 = z2 - theta * z1
        mixed = z1 - theta * z0
        zero = jnp.zeros((B, K), F32)
        pad = jnp.zeros((B, 8), F32)
        table = jnp.concatenate(
            [
                jnp.concatenate([z0, zero, zero, pad], axis=1),
                jnp.concatenate([mixed, z0, zero, pad], axis=1),
                jnp.concatenate([z2 - theta * mixed, mixed - theta * z0, z0, pad], axis=1),
            ],
            axis=0,
        )
        coeffs.append(split_coeffs(-table))
        thetas.append(theta)
        for i, z in enumerate((z0, z1, z2, ginv)):
            coef_out[g, 24 * i : 24 * i + z.shape[0], :K] = z
        shift_out[8 * g : 8 * g + 8, :] = jnp.broadcast_to(theta, (8, 128))
    zeros = jnp.zeros((8, 2 * NY), F32)
    for x in range(0, NX, 2):
        for g in range(2):
            frows = slice(K * g, K * g + K)
            brows = slice(B * g, B * g + B)
            theta = thetas[g]
            made = combination(
                coeffs[g],
                jnp.concatenate(
                    [pair((f0, f1)[g], x), pair(fields, x, frows), pair(f_next, x, frows), zeros],
                    axis=0,
                ),
            )
            b_own = pair(b, x, brows)
            b_one = pair(b1, x, brows)
            q1 = b_one - theta * b_own
            q2 = (pair(b_next, x, brows) - theta * b_one) - theta * q1
            made = made + jnp.concatenate([b_own, q1, q2], axis=0)
            for i in range(2):
                part = made[:, NY * i : NY * i + NY]
                q_out[x + i, 48 * g : 48 * g + 48] = part
                last_out[x + i, brows] = part[2 * B :]


def basis_gram_kernel(q, fields, gram_out):
    for g in range(2):
        qrows = slice(48 * g, 48 * g + 48)
        frows = slice(K * g, K * g + K)
        total = jnp.zeros((48, 128), F32)
        none = jnp.zeros((B, 2 * NY), F32)
        pad = jnp.zeros((40, 2 * NY), F32)
        for x in range(0, NX, 2):
            left = jnp.concatenate([q[x, qrows], q[x + 1, qrows]], axis=1)
            f1 = jnp.concatenate([fields[x, frows], fields[x + 1, frows]], axis=1)
            total = total + row_products(left, jnp.concatenate([left, none, f1, pad], axis=0))
        gram_out[g] = total


def moment_kernel(last, last_before, last_after, basis_gram, medium, shift, t_out, gram_out):
    def next_field(x, g):
        theta = shift[8 * g : 8 * g + 1, :]
        brows = slice(B * g, B * g + B)
        out = (medium[x : x + 1, :] - SHIFT - theta) * last[x, brows] - neighbours(
            x, lambda i: last[i, brows], last_before[x, brows], last_after[x, brows]
        )
        t_out[x, brows] = out
        return out

    total = jnp.zeros((2 * B, 128), F32)
    pad = jnp.zeros((64, 2 * NY), F32)
    for x in range(0, NX, 2):
        left = []
        right = []
        for g in range(2):
            brows = slice(B * g, B * g + B)
            made = jnp.concatenate([next_field(x, g), next_field(x + 1, g)], axis=1)
            left.append(made)
            right.append(jnp.concatenate([last[x, brows], last[x + 1, brows]], axis=1))
            right.append(made)
        total = total + row_products(
            jnp.concatenate(left, axis=0), jnp.concatenate(right + [pad], axis=0)
        )
    grams = [basis_gram[0], basis_gram[1]]
    ends = [pltpu.roll(total[:B], 80, 1), pltpu.roll(total[B:], 48, 1)]
    lane = iota((B, 128), 1)
    row = iota((B, 128), 0)
    column = lane & 15
    strips = []
    for gram, end in zip(grams, ends):
        middle = jnp.where(lane < 64, pltpu.roll(gram[16:32], 16, 1), pltpu.roll(gram[32:48], 32, 1))
        strips.append(jnp.where(lane < 32, gram[:16], jnp.where(lane < 80, middle, end)))
    packed = jnp.where(row <= column, strips[0], strips[1])
    packed = jnp.where(lane < 112, packed, 0.0)
    on_diagonal = jnp.where((row == column) & (lane < 112), strips[1], 0.0)
    for k in range(7):
        inside = (lane >= 16 * k) & (lane < 16 * k + 16)
        own = jnp.sum(jnp.where(inside, on_diagonal, 0.0), axis=1, keepdims=True)
        packed = jnp.where(lane == 112 + k, own, packed)
    low = jnp.zeros((8, 128), F32)
    lane8 = iota((8, 128), 1)
    for g in range(2):
        for half in range(2):
            at = 24 * (2 * g + half)
            piece = pltpu.roll(grams[g][32 + 8 * half : 40 + 8 * half], (at - 64) % 128, 1)
            low = jnp.where((lane8 >= at) & (lane8 < at + K), piece, low)
    gram_out[:B] = packed
    gram_out[B:] = low


def finish_kernel(
    table,
    index,
    moments,
    coef,
    shift,
    f0,
    f1,
    t,
    u0_far,
    u1_far,
    q_far,
    solution_far,
    residue_far,
    u0,
    u1,
    q,
    solution_out,
    residue_out,
    arrived,
    left,
):
    copies = [
        pltpu.make_async_copy(u0_far, u0, arrived.at[0]),
        pltpu.make_async_copy(u1_far, u1, arrived.at[1]),
        pltpu.make_async_copy(q_far, q, arrived.at[2]),
    ]
    for copy in copies:
        copy.start()
    summed = over_copies(moments)
    packed = summed[:B]
    turned = transposed(packed)
    lane = iota((B, 128), 1)
    row = iota((B, 128), 0)
    column = lane & 15
    flipped = turned[:B]
    for k in range(1, 7):
        flipped = flipped + pltpu.roll(turned[16 * k : 16 * k + 16], 16 * k, 1)
    diagonal = packed
    for k in range(7):
        diagonal = jnp.where(
            (lane >= 16 * k) & (lane < 16 * k + 16), packed[:, 112 + k : 113 + k], diagonal
        )
    strips = [
        jnp.where(row <= column, packed, flipped),
        jnp.where(row == column, diagonal, jnp.where(row > column, packed, flipped)),
    ]
    shifts = []
    thirds = []
    blocks = [[], [], []]
    parts = []
    for g in range(2):
        c = 6.0 + SHIFT + table[index[g]] + shift[8 * g : 8 * g + 1, :]
        shifts.append(c)
        at = 48 * g
        f1q2 = jnp.concatenate(
            [summed[B:, at : at + K], summed[B:, at + K : at + 2 * K]], axis=0
        )
        z3 = small(f1q2, coef[g, 72 : 72 + K, :K])
        thirds.append(z3)
        taken = lax.dot_general(
            z3, f1q2, (((1,), (1,)), ((), ())), precision=HIGH, preferred_element_type=F32
        )
        wide = jnp.concatenate([taken, jnp.zeros((B, 112), F32)], axis=1)
        strip = strips[g] - pltpu.roll(wide, 96, 1)
        once = pltpu.roll(strip, 16, 1)
        twice = pltpu.roll(strip, 32, 1)
        squared = strip + 2.0 * c * once + c * c * twice
        right = strip + c * once
        parts.append(
            [
                jnp.where(
                    lane < 48,
                    pltpu.roll(squared, 128 - 16 * (i + 1), 1),
                    pltpu.roll(right, 48 - 16 * i, 1),
                )
                for i in (1, 2, 3)
            ]
        )
    system = jnp.concatenate(
        [jnp.where(lane < 64, parts[0][i], pltpu.roll(parts[1][i], 64, 1)) for i in range(3)],
        axis=0,
    )
    solved = transposed(eliminate(system, 48))
    coeffs = []
    for g in range(2):
        c = shifts[g][:, :1]
        ys = solved[64 * g + 48 : 64 * g + 64]
        y1, y2, y3 = (ys[:, 16 * i : 16 * i + 16] for i in range(3))
        z0, z1, z2 = (coef[g, 24 * i : 24 * i + B, :K] for i in range(3))
        on_f = small(y3, thirds[g])
        on_u = z0 - small(y1, z1) - small(y2, z2) - on_f
        none = jnp.zeros((B, K), F32)
        rows = jnp.concatenate(
            [
                jnp.concatenate([on_u, none, y1, y2, y3, jnp.zeros((B, B), F32)], axis=1),
                jnp.concatenate(
                    [none, on_f, -c * y1, -y1 - c * y2, -y2 - c * y3, -y3], axis=1
                ),
            ],
            axis=0,
        )
        coeffs.append(split_coeffs(rows))
    for copy in copies:
        copy.wait()
    leaving = []
    for x in range(0, NX, 2):
        for g in range(2):
            brows = slice(B * g, B * g + B)
            qrows = slice(48 * g, 48 * g + 48)
            made = combination(
                coeffs[g],
                jnp.concatenate(
                    [pair((u0, u1)[g], x, slice(0, K)), pair((f0, f1)[g], x), pair(q, x, qrows), pair(t, x, brows)], axis=0
                ),
            )
            for i in range(2):
                part = made[:, NY * i : NY * i + NY]
                solution_out[brows, x + i, :] = part[:B]
                residue_out[brows, x + i, :] = part[B:] + q[x + i, 48 * g : 48 * g + B]
        if (x + 2) % CHUNK == 0:
            rows = pl.ds(x + 2 - CHUNK, CHUNK)
            for near, far in ((solution_out, solution_far), (residue_out, residue_far)):
                copy = pltpu.make_async_copy(
                    near.at[:, rows, :], far.at[:, rows, :], left.at[len(leaving)]
                )
                copy.start()
                leaving.append(copy)
    for copy in leaving:
        copy.wait()


def here(values):
    return pltpu.with_memory_space_constraint(values, pltpu.VMEM)


def call(kernel, shapes, scalars, *arrays, scratch=(), limit=8):
    count = len(arrays) - scalars
    return pl.pallas_call(
        kernel,
        out_shape=[pltpu.VMEM(s, F32) for s in shapes],
        in_specs=[SMEM] * scalars + [VMEM] * count,
        out_specs=[VMEM] * len(shapes),
        scratch_shapes=[pltpu.VMEM(s, F32) for s in scratch],
        compiler_params=pltpu.CompilerParams(vmem_limit_bytes=limit << 20),
        name=kernel.__name__,
    )(*arrays[:scalars], *(here(a) for a in arrays[scalars:]))


def finish(scalars, near, far, shape):
    copies = 2 * NX // CHUNK
    return pl.pallas_call(
        finish_kernel,
        out_shape=[jax.ShapeDtypeStruct(shape, F32)] * 2,
        in_specs=[SMEM] * len(scalars) + [VMEM] * len(near) + [ANY] * len(far),
        out_specs=[ANY] * 2,
        scratch_shapes=[pltpu.VMEM(a.shape, F32) for a in far]
        + [pltpu.VMEM(shape, F32)] * 2
        + [pltpu.SemaphoreType.DMA((len(far),)), pltpu.SemaphoreType.DMA((copies,))],
        compiler_params=pltpu.CompilerParams(vmem_limit_bytes=14 << 20),
        name="finish_kernel",
    )(*scalars, *(here(a) for a in near), *far)


def add_kernel(one, two, out):
    total = one[...] + two[...]
    for i in range(out.shape[0]):
        out[i] = total


def respread_kernel(parts, out):
    total = over_copies(parts)
    for i in range(out.shape[0]):
        out[i] = total


def everyone(values):
    far, near = STAGES
    other = lax.ppermute(values, CORES, [(0, 1), (1, 0)])
    (spread,) = call(add_kernel, [(lax.axis_size(far), *values.shape)], 0, values, other)
    parts = lax.all_to_all(spread, far, 0, 0, tiled=True)
    (spread,) = call(respread_kernel, [(lax.axis_size(near), *values.shape)], 0, parts)
    return lax.all_to_all(spread, near, 0, 0, tiled=True)


def beside(values):
    count = lax.axis_size(GRID)
    edges = [(i, i + 1) for i in range(1, count - 1, 2)]
    across = lax.ppermute(values, GRID, edges + [(j, i) for i, j in edges])
    sibling = lax.ppermute(values, CORES, [(0, 1), (1, 0)])
    return across, sibling


def on_device(right_sides, recycle, medium, shift_table, shift_index):
    med = medium[0]
    u = recycle.reshape(2, K, NX, NY)
    b = right_sides.reshape(2 * B, NX, NY)
    scalars = (shift_table, shift_index)
    back = jnp.transpose(jnp.concatenate([u[1], b], axis=0), (1, 0, 2))
    back_sides = beside(back)
    front = jnp.transpose(u[0], (1, 0, 2))
    front_across, front_sibling = beside(front)
    f1, b, b1 = call(
        back_kernel,
        [(NX, K, NY), (NX, 2 * B, NY), (NX, 2 * B, NY)],
        2,
        *scalars,
        back,
        *back_sides,
        med,
    )
    f1_sides = beside(f1)
    front_across, f1, f1_sibling = lax.optimization_barrier((front_across, f1, f1_sides[1]))
    f1_sides = (f1_sides[0], f1_sibling)
    (f0,) = call(
        front_kernel, [(NX, K, NY)], 2, *scalars, front, front_across, front_sibling, med
    )
    f0_sides = beside(f0)
    b1_sides = beside(b1)
    (first,) = call(first_gram_kernel, [(K, 128)], 0, f0, f1, b, b1)
    (fields,) = call(next_kernel, [(NX, 2 * K, NY)], 0, f0, *f0_sides, f1, *f1_sides, med)
    field_sides = beside(fields)
    (gram,) = call(second_gram_kernel, [(2 * K, 128)], 0, f0, f1, fields, b1, first)
    gram, b1_sides = lax.optimization_barrier((gram, b1_sides))
    q, last, coef, shift = call(
        krylov_kernel,
        [(NX, 96, NY), (NX, 2 * B, NY), (2, 96, 128), (16, 128)],
        0,
        everyone(gram),
        f0,
        f1,
        b,
        b1,
        *b1_sides,
        fields,
        *field_sides,
        med,
        scratch=[(NX, 2 * K, NY), (NX, 2 * B, NY)],
    )
    last_sides = beside(last)
    (basis_gram,) = call(basis_gram_kernel, [(2, 48, 128)], 0, q, fields)
    t, gram = call(
        moment_kernel, [(NX, 2 * B, NY), (K, 128)], 0, last, *last_sides, basis_gram, med, shift
    )
    solution, residue = finish(
        scalars, (everyone(gram), coef, shift, f0, f1, t), (front, back, q), (2 * B, NX, NY)
    )
    return solution.reshape(right_sides.shape), residue.reshape(right_sides.shape)


def solution(mesh):
    torus = Mesh(mesh.devices.reshape(4, 4, 8, 2), GRID)
    in_specs = (
        P(None, GRID, None, None),
        P(None, None, GRID, None, None),
        P(GRID, None, None),
        P(),
        P(),
    )
    out_specs = (P(None, GRID, None, None), P(None, GRID, None, None))
    return jax.shard_map(
        on_device, mesh=torus, in_specs=in_specs, out_specs=out_specs, check_vma=False
    )
```

```python
import jax
import jax.numpy as jnp
from jax import lax
from jax.experimental import pallas as pl
from jax.experimental.pallas import tpu as pltpu
from jax.sharding import Mesh
from jax.sharding import PartitionSpec as P

GRID = ("grid_0", "grid_1", "grid_2", "grid_3")
CORES = "grid_3"
STAGES = ("grid_2", ("grid_0", "grid_1"))
NX = 48
NY = 128
K = 24
B = 16
SHIFT = 0.5
HIGH = lax.Precision.HIGHEST
F32 = jnp.float32
BF16 = jnp.bfloat16
VMEM = pl.BlockSpec(memory_space=pltpu.VMEM)
SMEM = pl.BlockSpec(memory_space=pltpu.SMEM)
ANY = pl.BlockSpec(memory_space=pl.ANY)
CHUNK = 8


def iota(shape, dim):
    return lax.broadcasted_iota(jnp.int32, shape, dim)


def small(left, right):
    return jnp.dot(left, right, precision=HIGH, preferred_element_type=F32)


def halves(values):
    top = values.astype(BF16)
    return top, (values - top.astype(F32)).astype(BF16)


def row_products(left, right):
    dims = (((1,), (1,)), ((), ()))
    n = left.shape[0]
    l_top, l_rest = halves(left)
    r_top, r_rest = halves(right)
    both = lax.dot_general(
        jnp.concatenate([l_top, l_rest], axis=0), r_top, dims, preferred_element_type=F32
    )
    last = lax.dot_general(l_top, r_rest, dims, preferred_element_type=F32)
    return both[:n] + both[n:] + last


def combination(coeffs, fields):
    c_both, c_top = coeffs
    n = c_top.shape[0]
    f_top, f_rest = halves(fields)
    both = jnp.dot(c_both, f_top, preferred_element_type=F32)
    last = jnp.dot(c_top, f_rest, preferred_element_type=F32)
    return both[:n] + both[n:] + last


def split_coeffs(coeffs):
    top, rest = halves(coeffs)
    return jnp.concatenate([top, rest], axis=0), top


def neighbours(x, read, before, after):
    f = read(x)
    total = before + after
    if x > 0:
        total = total + read(x - 1)
    if x < NX - 1:
        total = total + read(x + 1)
    lane = iota(f.shape, 1)
    total = total + jnp.where(lane == 0, 0.0, pltpu.roll(f, 1, 1))
    return total + jnp.where(lane == NY - 1, 0.0, pltpu.roll(f, NY - 1, 1))


def transposed(values):
    rows = values.shape[0]
    return jnp.concatenate([values, jnp.zeros((128 - rows, 128), F32)], axis=0).T


def eliminate(system, count, meanwhile=None):
    lane = iota((1, 128), 1)
    row = iota(system.shape, 0)

    def column(k):
        return jnp.where(lane < 64, system[:, k : k + 1], system[:, 64 + k : 65 + k])

    for k in range(0, count, 2):
        if meanwhile is not None:
            meanwhile(k // 2)
        one = system[k : k + 1]
        two = system[k + 1 : k + 2]
        left = column(k)
        right = column(k + 1)
        a, b = left[k : k + 1], right[k : k + 1]
        c, d = left[k + 1 : k + 2], right[k + 1 : k + 2]
        inverse = 1.0 / (a * d - b * c)
        new_one = (d * inverse) * one - (b * inverse) * two
        new_two = (a * inverse) * two - (c * inverse) * one
        changed = system - left * new_one - right * new_two
        system = jnp.where(row == k, new_one, jnp.where(row == k + 1, new_two, changed))
    return system


def over_copies(parts):
    total = parts[0]
    for i in range(1, parts.shape[0]):
        total = total + parts[i]
    return total


def planes(ref, start, count):
    return lambda x: ref[x, start : start + count]


def stencil(diagonal, own, across, sibling, inside):
    def at(x):
        return diagonal(x) * own(x) - neighbours(x, own, across(x) * inside[0], sibling(x))

    return at


def applied(g, table, index, inside, medium, own, across, sibling):
    base = 6.0 + table[index[g]]
    return stencil(lambda x: medium[x : x + 1, :] + base, own, across, sibling, inside)


def front_kernel(table, index, inside, u, across, sibling, medium, f_out):
    made = applied(
        0, table, index, inside, medium, planes(u, 0, K), planes(across, 0, K), planes(sibling, 0, K)
    )
    for x in range(NX):
        f_out[x] = made(x)


def back_kernel(table, index, inside, ub, across, sibling, medium, f_out, b_out, b1_out):
    made = applied(
        1, table, index, inside, medium, planes(ub, 0, K), planes(across, 0, K), planes(sibling, 0, K)
    )
    own = planes(ub, K, 2 * B)
    shifted = stencil(
        lambda x: medium[x : x + 1, :] - SHIFT,
        own,
        planes(across, K, 2 * B),
        planes(sibling, K, 2 * B),
        inside,
    )
    for x in range(NX):
        f_out[x] = made(x)
        b_out[x] = own(x)
        b1_out[x] = shifted(x)


def pair(ref, x, rows=slice(None)):
    return jnp.concatenate([ref[x, rows], ref[x + 1, rows]], axis=1)


def first_gram_kernel(f0, f1, b, b1, gram_out):
    total = jnp.zeros((2 * K, 128), F32)
    zeros = jnp.zeros((8, 2 * NY), F32)
    tops = [jnp.zeros((B, NY), F32) for _ in range(2)]
    squares = [jnp.zeros((B, NY), F32) for _ in range(2)]
    for x in range(0, NX, 2):
        fields = [pair(f0, x), pair(f1, x)]
        b_pair = pair(b, x)
        b1_pair = pair(b1, x)
        right = []
        for g in range(2):
            bg = b_pair[B * g : B * g + B]
            b1g = b1_pair[B * g : B * g + B]
            right += [fields[g], bg, b1g, zeros]
            top = bg * b1g
            square = bg * bg
            tops[g] = tops[g] + top[:, :NY] + top[:, NY:]
            squares[g] = squares[g] + square[:, :NY] + square[:, NY:]
        total = total + row_products(
            jnp.concatenate(fields, axis=0), jnp.concatenate(right, axis=0)
        )
    lane = iota((K, 128), 1)
    row = iota((K, 128), 0)
    packed = jnp.where(lane < 64, total[:K], total[K:])
    for g in range(2):
        here = (row == 0) & (lane == 64 * g + 56)
        packed = jnp.where(here, jnp.sum(tops[g], keepdims=True), packed)
        here = (row == 0) & (lane == 64 * g + 57)
        packed = jnp.where(here, jnp.sum(squares[g], keepdims=True), packed)
    gram_out[...] = packed


def rows_of(ref):
    return lambda x: ref[x]


def next_kernel(inside, f0, f0_across, f0_sibling, f1, f1_across, f1_sibling, medium, fields_out):
    for g, (own, across, sibling) in enumerate(
        ((f0, f0_across, f0_sibling), (f1, f1_across, f1_sibling))
    ):
        made = stencil(
            lambda x: medium[x : x + 1, :] - SHIFT,
            rows_of(own),
            rows_of(across),
            rows_of(sibling),
            inside,
        )
        for x in range(NX):
            fields_out[x, K * g : K * g + K] = made(x)


def second_gram_kernel(f0, f1, fields, b1, first, gram_out):
    total = jnp.zeros((2 * K, 128), F32)
    for x in range(0, NX, 2):
        nexts = pair(fields, x)
        b1_pair = pair(b1, x)
        right = [pair(f0, x), nexts[:K], b1_pair[:B], pair(f1, x), nexts[K:], b1_pair[B:]]
        total = total + row_products(nexts, jnp.concatenate(right, axis=0))
    lane = iota((K, 128), 1)
    gram_out[:K] = first[...]
    gram_out[K:] = jnp.where(lane < 64, total[:K], total[K:])


def krylov_kernel(
    inside,
    grams,
    f0,
    f1,
    b,
    b1,
    b1_across,
    b1_sibling,
    fields,
    fields_across,
    fields_sibling,
    medium,
    q_out,
    last_out,
    coef_out,
    shift_out,
    f_next,
    b_next,
):
    def plain(x):
        return medium[x : x + 1, :] - SHIFT

    next_f = stencil(
        plain, rows_of(fields), rows_of(fields_across), rows_of(fields_sibling), inside
    )
    next_b = stencil(plain, rows_of(b1), rows_of(b1_across), rows_of(b1_sibling), inside)

    def meanwhile(step):
        for x in range(4 * step, 4 * step + 4):
            f_next[x] = next_f(x)
            b_next[x] = next_b(x)

    gram = over_copies(grams)
    first = gram[:K]
    lane = iota((K, 128), 1)
    row = iota((K, 128), 0)
    place = lane & 63
    unit = jnp.where(place == row + K, 1.0, 0.0)
    inverse_t = transposed(eliminate(jnp.where(place < K, first, unit), K, meanwhile))
    first_t = transposed(first)
    second_t = transposed(gram[K:])
    coeffs = []
    thetas = []
    for g in range(2):
        at = 64 * g
        ginv = inverse_t[at + K : at + 2 * K, :K]
        fb = first_t[at + K : at + K + B, :K]
        fb1 = first_t[at + K + B : at + K + 2 * B, :K]
        ff1 = second_t[at : at + K, :K]
        f1f1 = second_t[at + K : at + 2 * K, :K]
        f1b1 = second_t[at + 2 * K : at + 2 * K + B, :K]
        theta = first_t[at + 56 : at + 57, :1] / first_t[at + 57 : at + 58, :1]
        z0 = small(fb, ginv)
        z1 = small(fb1 - small(z0, ff1), ginv)
        z2 = small(f1b1 - small(z0, f1f1) - small(z1, ff1), ginv)
        z2 = z2 - theta * z1
        mixed = z1 - theta * z0
        zero = jnp.zeros((B, K), F32)
        pad = jnp.zeros((B, 8), F32)
        table = jnp.concatenate(
            [
                jnp.concatenate([z0, zero, zero, pad], axis=1),
                jnp.concatenate([mixed, z0, zero, pad], axis=1),
                jnp.concatenate([z2 - theta * mixed, mixed - theta * z0, z0, pad], axis=1),
            ],
            axis=0,
        )
        coeffs.append(split_coeffs(-table))
        thetas.append(theta)
        for i, z in enumerate((z0, z1, z2, ginv)):
            coef_out[g, 24 * i : 24 * i + z.shape[0], :K] = z
        shift_out[8 * g : 8 * g + 8, :] = jnp.broadcast_to(theta, (8, 128))
    zeros = jnp.zeros((8, 2 * NY), F32)
    for x in range(0, NX, 2):
        for g in range(2):
            frows = slice(K * g, K * g + K)
            brows = slice(B * g, B * g + B)
            theta = thetas[g]
            made = combination(
                coeffs[g],
                jnp.concatenate(
                    [pair((f0, f1)[g], x), pair(fields, x, frows), pair(f_next, x, frows), zeros],
                    axis=0,
                ),
            )
            b_own = pair(b, x, brows)
            b_one = pair(b1, x, brows)
            q1 = b_one - theta * b_own
            q2 = (pair(b_next, x, brows) - theta * b_one) - theta * q1
            made = made + jnp.concatenate([b_own, q1, q2], axis=0)
            for i in range(2):
                part = made[:, NY * i : NY * i + NY]
                q_out[x + i, 48 * g : 48 * g + 48] = part
                last_out[x + i, brows] = part[2 * B :]


def basis_gram_kernel(q, fields, gram_out):
    for g in range(2):
        qrows = slice(48 * g, 48 * g + 48)
        frows = slice(K * g, K * g + K)
        total = jnp.zeros((48, 128), F32)
        none = jnp.zeros((B, 2 * NY), F32)
        pad = jnp.zeros((40, 2 * NY), F32)
        for x in range(0, NX, 2):
            left = jnp.concatenate([q[x, qrows], q[x + 1, qrows]], axis=1)
            f1 = jnp.concatenate([fields[x, frows], fields[x + 1, frows]], axis=1)
            total = total + row_products(left, jnp.concatenate([left, none, f1, pad], axis=0))
        gram_out[g] = total


def moment_kernel(inside, last, last_across, last_sibling, basis_gram, medium, shift, t_out, gram_out):
    def next_field(x, g):
        theta = shift[8 * g : 8 * g + 1, :]
        brows = slice(B * g, B * g + B)
        out = (medium[x : x + 1, :] - SHIFT - theta) * last[x, brows] - neighbours(
            x, lambda i: last[i, brows], last_across[x, brows] * inside[0], last_sibling[x, brows]
        )
        t_out[x, brows] = out
        return out

    total = jnp.zeros((2 * B, 128), F32)
    pad = jnp.zeros((64, 2 * NY), F32)
    for x in range(0, NX, 2):
        left = []
        right = []
        for g in range(2):
            brows = slice(B * g, B * g + B)
            made = jnp.concatenate([next_field(x, g), next_field(x + 1, g)], axis=1)
            left.append(made)
            right.append(jnp.concatenate([last[x, brows], last[x + 1, brows]], axis=1))
            right.append(made)
        total = total + row_products(
            jnp.concatenate(left, axis=0), jnp.concatenate(right + [pad], axis=0)
        )
    grams = [basis_gram[0], basis_gram[1]]
    ends = [pltpu.roll(total[:B], 80, 1), pltpu.roll(total[B:], 48, 1)]
    lane = iota((B, 128), 1)
    row = iota((B, 128), 0)
    column = lane & 15
    strips = []
    for gram, end in zip(grams, ends):
        middle = jnp.where(lane < 64, pltpu.roll(gram[16:32], 16, 1), pltpu.roll(gram[32:48], 32, 1))
        strips.append(jnp.where(lane < 32, gram[:16], jnp.where(lane < 80, middle, end)))
    packed = jnp.where(row <= column, strips[0], strips[1])
    packed = jnp.where(lane < 112, packed, 0.0)
    on_diagonal = jnp.where((row == column) & (lane < 112), strips[1], 0.0)
    for k in range(7):
        inside = (lane >= 16 * k) & (lane < 16 * k + 16)
        own = jnp.sum(jnp.where(inside, on_diagonal, 0.0), axis=1, keepdims=True)
        packed = jnp.where(lane == 112 + k, own, packed)
    low = jnp.zeros((8, 128), F32)
    lane8 = iota((8, 128), 1)
    for g in range(2):
        for half in range(2):
            at = 24 * (2 * g + half)
            piece = pltpu.roll(grams[g][32 + 8 * half : 40 + 8 * half], (at - 64) % 128, 1)
            low = jnp.where((lane8 >= at) & (lane8 < at + K), piece, low)
    gram_out[:B] = packed
    gram_out[B:] = low


def finish_kernel(
    table,
    index,
    moments,
    coef,
    shift,
    f0,
    f1,
    t,
    u0_far,
    u1_far,
    q_far,
    solution_far,
    residue_far,
    u0,
    u1,
    q,
    solution_out,
    residue_out,
    arrived,
    left,
):
    copies = [
        pltpu.make_async_copy(u0_far, u0, arrived.at[0]),
        pltpu.make_async_copy(u1_far, u1, arrived.at[1]),
        pltpu.make_async_copy(q_far, q, arrived.at[2]),
    ]
    for copy in copies:
        copy.start()
    summed = over_copies(moments)
    packed = summed[:B]
    turned = transposed(packed)
    lane = iota((B, 128), 1)
    row = iota((B, 128), 0)
    column = lane & 15
    flipped = turned[:B]
    for k in range(1, 7):
        flipped = flipped + pltpu.roll(turned[16 * k : 16 * k + 16], 16 * k, 1)
    diagonal = packed
    for k in range(7):
        diagonal = jnp.where(
            (lane >= 16 * k) & (lane < 16 * k + 16), packed[:, 112 + k : 113 + k], diagonal
        )
    strips = [
        jnp.where(row <= column, packed, flipped),
        jnp.where(row == column, diagonal, jnp.where(row > column, packed, flipped)),
    ]
    shifts = []
    thirds = []
    blocks = [[], [], []]
    parts = []
    for g in range(2):
        c = 6.0 + SHIFT + table[index[g]] + shift[8 * g : 8 * g + 1, :]
        shifts.append(c)
        at = 48 * g
        f1q2 = jnp.concatenate(
            [summed[B:, at : at + K], summed[B:, at + K : at + 2 * K]], axis=0
        )
        z3 = small(f1q2, coef[g, 72 : 72 + K, :K])
        thirds.append(z3)
        taken = lax.dot_general(
            z3, f1q2, (((1,), (1,)), ((), ())), precision=HIGH, preferred_element_type=F32
        )
        wide = jnp.concatenate([taken, jnp.zeros((B, 112), F32)], axis=1)
        strip = strips[g] - pltpu.roll(wide, 96, 1)
        once = pltpu.roll(strip, 16, 1)
        twice = pltpu.roll(strip, 32, 1)
        squared = strip + 2.0 * c * once + c * c * twice
        right = strip + c * once
        parts.append(
            [
                jnp.where(
                    lane < 48,
                    pltpu.roll(squared, 128 - 16 * (i + 1), 1),
                    pltpu.roll(right, 48 - 16 * i, 1),
                )
                for i in (1, 2, 3)
            ]
        )
    system = jnp.concatenate(
        [jnp.where(lane < 64, parts[0][i], pltpu.roll(parts[1][i], 64, 1)) for i in range(3)],
        axis=0,
    )
    solved = transposed(eliminate(system, 48))
    coeffs = []
    for g in range(2):
        c = shifts[g][:, :1]
        ys = solved[64 * g + 48 : 64 * g + 64]
        y1, y2, y3 = (ys[:, 16 * i : 16 * i + 16] for i in range(3))
        z0, z1, z2 = (coef[g, 24 * i : 24 * i + B, :K] for i in range(3))
        on_f = small(y3, thirds[g])
        on_u = z0 - small(y1, z1) - small(y2, z2) - on_f
        none = jnp.zeros((B, K), F32)
        rows = jnp.concatenate(
            [
                jnp.concatenate([on_u, none, y1, y2, y3, jnp.zeros((B, B), F32)], axis=1),
                jnp.concatenate(
                    [none, on_f, -c * y1, -y1 - c * y2, -y2 - c * y3, -y3], axis=1
                ),
            ],
            axis=0,
        )
        coeffs.append(split_coeffs(rows))
    for copy in copies:
        copy.wait()
    leaving = []
    for x in range(0, NX, 2):
        for g in range(2):
            brows = slice(B * g, B * g + B)
            qrows = slice(48 * g, 48 * g + 48)
            made = combination(
                coeffs[g],
                jnp.concatenate(
                    [pair((u0, u1)[g], x, slice(0, K)), pair((f0, f1)[g], x), pair(q, x, qrows), pair(t, x, brows)], axis=0
                ),
            )
            for i in range(2):
                part = made[:, NY * i : NY * i + NY]
                solution_out[brows, x + i, :] = part[:B]
                residue_out[brows, x + i, :] = part[B:] + q[x + i, 48 * g : 48 * g + B]
        if (x + 2) % CHUNK == 0:
            rows = pl.ds(x + 2 - CHUNK, CHUNK)
            for near, far in ((solution_out, solution_far), (residue_out, residue_far)):
                copy = pltpu.make_async_copy(
                    near.at[:, rows, :], far.at[:, rows, :], left.at[len(leaving)]
                )
                copy.start()
                leaving.append(copy)
    for copy in leaving:
        copy.wait()


def here(values):
    return pltpu.with_memory_space_constraint(values, pltpu.VMEM)


def call(kernel, shapes, scalars, *arrays, scratch=(), limit=8):
    count = len(arrays) - scalars
    return pl.pallas_call(
        kernel,
        out_shape=[pltpu.VMEM(s, F32) for s in shapes],
        in_specs=[SMEM] * scalars + [VMEM] * count,
        out_specs=[VMEM] * len(shapes),
        scratch_shapes=[pltpu.VMEM(s, F32) for s in scratch],
        compiler_params=pltpu.CompilerParams(vmem_limit_bytes=limit << 20),
        name=kernel.__name__,
    )(*arrays[:scalars], *(here(a) for a in arrays[scalars:]))


def finish(scalars, near, far, shape):
    copies = 2 * NX // CHUNK
    return pl.pallas_call(
        finish_kernel,
        out_shape=[jax.ShapeDtypeStruct(shape, F32)] * 2,
        in_specs=[SMEM] * len(scalars) + [VMEM] * len(near) + [ANY] * len(far),
        out_specs=[ANY] * 2,
        scratch_shapes=[pltpu.VMEM(a.shape, F32) for a in far]
        + [pltpu.VMEM(shape, F32)] * 2
        + [pltpu.SemaphoreType.DMA((len(far),)), pltpu.SemaphoreType.DMA((copies,))],
        compiler_params=pltpu.CompilerParams(vmem_limit_bytes=14 << 20),
        name="finish_kernel",
    )(*scalars, *(here(a) for a in near), *far)


def add_kernel(one, two, out):
    total = one[...] + two[...]
    for i in range(out.shape[0]):
        out[i] = total


def respread_kernel(parts, out):
    total = over_copies(parts)
    for i in range(out.shape[0]):
        out[i] = total


def everyone(values):
    far, near = STAGES
    other = lax.ppermute(values, CORES, [(0, 1), (1, 0)])
    (spread,) = call(add_kernel, [(lax.axis_size(far), *values.shape)], 0, values, other)
    parts = lax.all_to_all(spread, far, 0, 0, tiled=True)
    (spread,) = call(respread_kernel, [(lax.axis_size(near), *values.shape)], 0, parts)
    return lax.all_to_all(spread, near, 0, 0, tiled=True)


def beside(values):
    count = lax.axis_size(GRID)
    edges = [(i, (i + 1) % count) for i in range(1, count, 2)]
    across = lax.ppermute(values, GRID, edges + [(j, i) for i, j in edges])
    sibling = lax.ppermute(values, CORES, [(0, 1), (1, 0)])
    return across, sibling


def on_device(right_sides, recycle, medium, shift_table, shift_index):
    med = medium[0]
    u = recycle.reshape(2, K, NX, NY)
    b = right_sides.reshape(2 * B, NX, NY)
    scalars = (shift_table, shift_index)
    place = lax.axis_index(GRID)
    at_end = (place == 0) | (place == lax.axis_size(GRID) - 1)
    inside = jnp.where(at_end, 0.0, 1.0).astype(F32).reshape(1)
    back = jnp.transpose(jnp.concatenate([u[1], b], axis=0), (1, 0, 2))
    back_sides = beside(back)
    front = jnp.transpose(u[0], (1, 0, 2))
    front_across, front_sibling = beside(front)
    f1, b, b1 = call(
        back_kernel,
        [(NX, K, NY), (NX, 2 * B, NY), (NX, 2 * B, NY)],
        3,
        *scalars,
        inside,
        back,
        *back_sides,
        med,
    )
    f1_sides = beside(f1)
    front_across, f1, f1_sibling = lax.optimization_barrier((front_across, f1, f1_sides[1]))
    f1_sides = (f1_sides[0], f1_sibling)
    (f0,) = call(
        front_kernel, [(NX, K, NY)], 3, *scalars, inside, front, front_across, front_sibling, med
    )
    f0_sides = beside(f0)
    b1_sides = beside(b1)
    (first,) = call(first_gram_kernel, [(K, 128)], 0, f0, f1, b, b1)
    (fields,) = call(next_kernel, [(NX, 2 * K, NY)], 1, inside, f0, *f0_sides, f1, *f1_sides, med)
    field_sides = beside(fields)
    (gram,) = call(second_gram_kernel, [(2 * K, 128)], 0, f0, f1, fields, b1, first)
    gram, b1_sides = lax.optimization_barrier((gram, b1_sides))
    q, last, coef, shift = call(
        krylov_kernel,
        [(NX, 96, NY), (NX, 2 * B, NY), (2, 96, 128), (16, 128)],
        1,
        inside,
        everyone(gram),
        f0,
        f1,
        b,
        b1,
        *b1_sides,
        fields,
        *field_sides,
        med,
        scratch=[(NX, 2 * K, NY), (NX, 2 * B, NY)],
    )
    last_sides = beside(last)
    (basis_gram,) = call(basis_gram_kernel, [(2, 48, 128)], 0, q, fields)
    t, gram = call(
        moment_kernel,
        [(NX, 2 * B, NY), (K, 128)],
        1,
        inside,
        last,
        *last_sides,
        basis_gram,
        med,
        shift,
    )
    solution, residue = finish(
        scalars, (everyone(gram), coef, shift, f0, f1, t), (front, back, q), (2 * B, NX, NY)
    )
    return solution.reshape(right_sides.shape), residue.reshape(right_sides.shape)


def solution(mesh):
    torus = Mesh(mesh.devices.reshape(4, 4, 8, 2), GRID)
    in_specs = (
        P(None, GRID, None, None),
        P(None, None, GRID, None, None),
        P(GRID, None, None),
        P(),
        P(),
    )
    out_specs = (P(None, GRID, None, None), P(None, GRID, None, None))
    return jax.shard_map(
        on_device, mesh=torus, in_specs=in_specs, out_specs=out_specs, check_vma=False
    )
```

```python
import jax
import jax.numpy as jnp
from jax import lax
from jax.experimental import pallas as pl
from jax.experimental.pallas import tpu as pltpu
from jax.sharding import Mesh
from jax.sharding import PartitionSpec as P

GRID = ("grid_0", "grid_1", "grid_2", "grid_3")
CORES = "grid_3"
STAGES = ("grid_2", ("grid_0", "grid_1"))
NX = 48
NY = 128
K = 24
B = 16
SHIFT = 0.5
HIGH = lax.Precision.HIGHEST
F32 = jnp.float32
BF16 = jnp.bfloat16
VMEM = pl.BlockSpec(memory_space=pltpu.VMEM)
SMEM = pl.BlockSpec(memory_space=pltpu.SMEM)
ANY = pl.BlockSpec(memory_space=pl.ANY)
CHUNK = 8


def iota(shape, dim):
    return lax.broadcasted_iota(jnp.int32, shape, dim)


def small(left, right):
    return jnp.dot(left, right, precision=HIGH, preferred_element_type=F32)


def halves(values):
    top = values.astype(BF16)
    return top, (values - top.astype(F32)).astype(BF16)


def row_products(left, right):
    dims = (((1,), (1,)), ((), ()))
    n = left.shape[0]
    l_top, l_rest = halves(left)
    r_top, r_rest = halves(right)
    both = lax.dot_general(
        jnp.concatenate([l_top, l_rest], axis=0), r_top, dims, preferred_element_type=F32
    )
    last = lax.dot_general(l_top, r_rest, dims, preferred_element_type=F32)
    return both[:n] + both[n:] + last


def combination(coeffs, fields):
    c_both, c_top = coeffs
    n = c_top.shape[0]
    f_top, f_rest = halves(fields)
    both = jnp.dot(c_both, f_top, preferred_element_type=F32)
    last = jnp.dot(c_top, f_rest, preferred_element_type=F32)
    return both[:n] + both[n:] + last


def split_coeffs(coeffs):
    top, rest = halves(coeffs)
    return jnp.concatenate([top, rest], axis=0), top


def neighbours(x, read, before, after):
    f = read(x)
    total = before + after
    if x > 0:
        total = total + read(x - 1)
    if x < NX - 1:
        total = total + read(x + 1)
    lane = iota(f.shape, 1)
    total = total + jnp.where(lane == 0, 0.0, pltpu.roll(f, 1, 1))
    return total + jnp.where(lane == NY - 1, 0.0, pltpu.roll(f, NY - 1, 1))


def transposed(values):
    rows = values.shape[0]
    return jnp.concatenate([values, jnp.zeros((128 - rows, 128), F32)], axis=0).T


def eliminate(system, count):
    lane = iota((1, 128), 1)
    row = iota(system.shape, 0)

    def column(k):
        return jnp.where(lane < 64, system[:, k : k + 1], system[:, 64 + k : 65 + k])

    for k in range(0, count, 2):
        one = system[k : k + 1]
        two = system[k + 1 : k + 2]
        left = column(k)
        right = column(k + 1)
        a, b = left[k : k + 1], right[k : k + 1]
        c, d = left[k + 1 : k + 2], right[k + 1 : k + 2]
        inverse = 1.0 / (a * d - b * c)
        new_one = (d * inverse) * one - (b * inverse) * two
        new_two = (a * inverse) * two - (c * inverse) * one
        changed = system - left * new_one - right * new_two
        system = jnp.where(row == k, new_one, jnp.where(row == k + 1, new_two, changed))
    return system


def over_copies(parts):
    total = parts[0]
    for i in range(1, parts.shape[0]):
        total = total + parts[i]
    return total


def planes(ref, start, count):
    return lambda x: ref[x, start : start + count]


def stencil(diagonal, own, across, sibling, inside):
    def at(x):
        return diagonal(x) * own(x) - neighbours(x, own, across(x) * inside[0], sibling(x))

    return at


def applied(g, table, index, inside, medium, own, across, sibling):
    base = 6.0 + table[index[g]]
    return stencil(lambda x: medium[x : x + 1, :] + base, own, across, sibling, inside)


def front_kernel(table, index, inside, u, across, sibling, medium, f_out):
    made = applied(
        0, table, index, inside, medium, planes(u, 0, K), planes(across, 0, K), planes(sibling, 0, K)
    )
    for x in range(NX):
        f_out[x] = made(x)


def back_kernel(table, index, inside, ub, across, sibling, medium, f_out, b_out, b1_out):
    made = applied(
        1, table, index, inside, medium, planes(ub, 0, K), planes(across, 0, K), planes(sibling, 0, K)
    )
    own = planes(ub, K, 2 * B)
    shifted = stencil(
        lambda x: medium[x : x + 1, :] - SHIFT,
        own,
        planes(across, K, 2 * B),
        planes(sibling, K, 2 * B),
        inside,
    )
    for x in range(NX):
        f_out[x] = made(x)
        b_out[x] = own(x)
        b1_out[x] = shifted(x)


def pair(ref, x, rows=slice(None)):
    return jnp.concatenate([ref[x, rows], ref[x + 1, rows]], axis=1)


def first_gram_kernel(f0, f1, b, b1, gram_out):
    total = jnp.zeros((2 * K, 128), F32)
    zeros = jnp.zeros((8, 2 * NY), F32)
    tops = [jnp.zeros((B, NY), F32) for _ in range(2)]
    squares = [jnp.zeros((B, NY), F32) for _ in range(2)]
    for x in range(0, NX, 2):
        fields = [pair(f0, x), pair(f1, x)]
        b_pair = pair(b, x)
        b1_pair = pair(b1, x)
        right = []
        for g in range(2):
            bg = b_pair[B * g : B * g + B]
            b1g = b1_pair[B * g : B * g + B]
            right += [fields[g], bg, b1g, zeros]
            top = bg * b1g
            square = bg * bg
            tops[g] = tops[g] + top[:, :NY] + top[:, NY:]
            squares[g] = squares[g] + square[:, :NY] + square[:, NY:]
        total = total + row_products(
            jnp.concatenate(fields, axis=0), jnp.concatenate(right, axis=0)
        )
    lane = iota((K, 128), 1)
    row = iota((K, 128), 0)
    packed = jnp.where(lane < 64, total[:K], total[K:])
    for g in range(2):
        here = (row == 0) & (lane == 64 * g + 56)
        packed = jnp.where(here, jnp.sum(tops[g], keepdims=True), packed)
        here = (row == 0) & (lane == 64 * g + 57)
        packed = jnp.where(here, jnp.sum(squares[g], keepdims=True), packed)
    gram_out[...] = packed


def rows_of(ref, rows=slice(None)):
    return lambda x: ref[x, rows]


def next_kernel(inside, f0, f0_across, f0_sibling, f1, f1_across, f1_sibling, medium, fields_out):
    for g, (own, across, sibling) in enumerate(
        ((f0, f0_across, f0_sibling), (f1, f1_across, f1_sibling))
    ):
        made = stencil(
            lambda x: medium[x : x + 1, :] - SHIFT,
            rows_of(own),
            rows_of(across),
            rows_of(sibling),
            inside,
        )
        for x in range(NX):
            fields_out[x, K * g : K * g + K] = made(x)


def second_gram_kernel(f0, f1, fields, b1, first, gram_out):
    total = jnp.zeros((2 * K, 128), F32)
    for x in range(0, NX, 2):
        nexts = pair(fields, x)
        b1_pair = pair(b1, x)
        right = [pair(f0, x), nexts[:K], b1_pair[:B], pair(f1, x), nexts[K:], b1_pair[B:]]
        total = total + row_products(nexts, jnp.concatenate(right, axis=0))
    lane = iota((K, 128), 1)
    gram_out[:K] = first[...]
    gram_out[K:] = jnp.where(lane < 64, total[:K], total[K:])


def krylov_kernel(grams, f0, f1, b, b1, fields, q_out, last_out, coef_out, shift_out):
    gram = over_copies(grams)
    first = gram[:K]
    lane = iota((K, 128), 1)
    row = iota((K, 128), 0)
    place = lane & 63
    unit = jnp.where(place == row + K, 1.0, 0.0)
    inverse_t = transposed(eliminate(jnp.where(place < K, first, unit), K))
    first_t = transposed(first)
    second_t = transposed(gram[K:])
    coeffs = []
    thetas = []
    for g in range(2):
        at = 64 * g
        ginv = inverse_t[at + K : at + 2 * K, :K]
        fb = first_t[at + K : at + K + B, :K]
        fb1 = first_t[at + K + B : at + K + 2 * B, :K]
        ff1 = second_t[at : at + K, :K]
        f1f1 = second_t[at + K : at + 2 * K, :K]
        f1b1 = second_t[at + 2 * K : at + 2 * K + B, :K]
        theta = first_t[at + 56 : at + 57, :1] / first_t[at + 57 : at + 58, :1]
        z0 = small(fb, ginv)
        z1 = small(fb1 - small(z0, ff1), ginv)
        z2 = small(f1b1 - small(z0, f1f1) - small(z1, ff1), ginv)
        z2 = z2 - theta * z1
        mixed = z1 - theta * z0
        table = jnp.concatenate(
            [
                jnp.concatenate([z0, jnp.zeros((B, K), F32)], axis=1),
                jnp.concatenate([mixed, z0], axis=1),
            ],
            axis=0,
        )
        coeffs.append(split_coeffs(-table))
        thetas.append(theta)
        for i, z in enumerate((z0, z1, z2, ginv)):
            coef_out[g, 24 * i : 24 * i + z.shape[0], :K] = z
        shift_out[8 * g : 8 * g + 8, :] = jnp.broadcast_to(theta, (8, 128))
    for x in range(0, NX, 2):
        for g in range(2):
            frows = slice(K * g, K * g + K)
            brows = slice(B * g, B * g + B)
            made = combination(
                coeffs[g],
                jnp.concatenate([pair((f0, f1)[g], x), pair(fields, x, frows)], axis=0),
            )
            b_own = pair(b, x, brows)
            made = made + jnp.concatenate([b_own, pair(b1, x, brows) - thetas[g] * b_own], axis=0)
            for i in range(2):
                part = made[:, NY * i : NY * i + NY]
                q_out[x + i, 32 * g : 32 * g + 32] = part
                last_out[x + i, brows] = part[B:]


def basis_gram_kernel(q, gram_out):
    pad = jnp.zeros((96, 2 * NY), F32)
    for g in range(2):
        rows = slice(32 * g, 32 * g + 32)
        total = jnp.zeros((32, 128), F32)
        for x in range(0, NX, 2):
            left = pair(q, x, rows)
            total = total + row_products(left, jnp.concatenate([left, pad], axis=0))
        gram_out[g] = total


def moment_kernel(
    inside,
    q,
    last,
    across,
    sibling,
    past_across,
    past_sibling,
    f0,
    f0_across,
    f0_sibling,
    f1,
    f1_across,
    f1_sibling,
    fields,
    medium,
    medium_across,
    medium_sibling,
    coef,
    shift,
    basis_gram,
    q2_out,
    t_out,
    gram_out,
    aside,
):
    zeros = jnp.zeros((8, 6 * NY), F32)
    ones = (1.0, 1.0)
    grams = []
    for g in range(2):
        theta = shift[8 * g : 8 * g + 1, :]
        brows = slice(B * g, B * g + B)
        coeffs = split_coeffs(
            jnp.concatenate([-coef[g, 48 : 48 + B, :K], jnp.zeros((B, 8), F32)], axis=1)
        )

        def shifted(field):
            return lambda x: field[x : x + 1, :] - SHIFT - theta

        own, over, near, past_over, past_near = (
            rows_of(a, brows) for a in (last, across, sibling, past_across, past_sibling)
        )
        here_q2 = stencil(shifted(medium), own, over, near, inside)
        near_q2 = stencil(shifted(medium_sibling), near, past_near, own, (inside[1],))
        over_q2 = stencil(shifted(medium_across), over, past_over, own, ones)
        slabs = ((f0, f0_sibling, f0_across), (f1, f1_sibling, f1_across))[g]
        for x in range(0, NX, 2):
            fs = jnp.concatenate([pair(a, x) for a in slabs], axis=1)
            made = combination(coeffs, jnp.concatenate([fs, zeros], axis=0))
            for i in range(2):
                at = [made[:, NY * (2 * k + i) : NY * (2 * k + i + 1)] for k in range(3)]
                q2_out[x + i, brows] = here_q2(x + i) + at[0]
                beyond = (over_q2(x + i) + at[2]) * inside[0]
                aside[x + i, brows] = near_q2(x + i) + at[1] + beyond
        made_t = stencil(
            shifted(medium), rows_of(q2_out, brows), rows_of(aside, brows), lambda x: 0.0, ones
        )
        total = jnp.zeros((2 * B, 128), F32)
        pad = jnp.zeros((40, 2 * NY), F32)
        for x in range(0, NX, 2):
            ends = [made_t(x), made_t(x + 1)]
            for i in range(2):
                t_out[x + i, brows] = ends[i]
            left = jnp.concatenate(
                [pair(q2_out, x, brows), jnp.concatenate(ends, axis=1)], axis=0
            )
            f1_pair = pair(fields, x, slice(K * g, K * g + K))
            right = [pair(q, x, slice(32 * g, 32 * g + 32)), left, f1_pair, pad]
            total = total + row_products(left, jnp.concatenate(right, axis=0))
        grams.append(total)
    lane = iota((B, 128), 1)
    row = iota((B, 128), 0)
    column = lane & 15
    strips = []
    for g in range(2):
        low, high = basis_gram[g, :B], basis_gram[g, B:]
        ends = jnp.where(lane < 96, pltpu.roll(grams[g][:B], 32, 1), pltpu.roll(grams[g][B:], 48, 1))
        strips.append(
            jnp.where(lane < 32, low, jnp.where(lane < 48, pltpu.roll(high, 16, 1), ends))
        )
    packed = jnp.where(row <= column, strips[0], strips[1])
    packed = jnp.where(lane < 112, packed, 0.0)
    on_diagonal = jnp.where((row == column) & (lane < 112), strips[1], 0.0)
    for k in range(7):
        inside = (lane >= 16 * k) & (lane < 16 * k + 16)
        own = jnp.sum(jnp.where(inside, on_diagonal, 0.0), axis=1, keepdims=True)
        packed = jnp.where(lane == 112 + k, own, packed)
    low = jnp.zeros((8, 128), F32)
    lane8 = iota((8, 128), 1)
    for g in range(2):
        for half in range(2):
            at = 24 * (2 * g + half)
            piece = pltpu.roll(grams[g][8 * half : 8 * half + 8], (at - 64) % 128, 1)
            low = jnp.where((lane8 >= at) & (lane8 < at + K), piece, low)
    gram_out[:B] = packed
    gram_out[B:] = low


def finish_kernel(
    table,
    index,
    moments,
    coef,
    shift,
    f0,
    f1,
    q2,
    t,
    u0_far,
    u1_far,
    q_far,
    solution_far,
    residue_far,
    u0,
    u1,
    q,
    solution_out,
    residue_out,
    arrived,
    left,
):
    copies = [
        pltpu.make_async_copy(u0_far, u0, arrived.at[0]),
        pltpu.make_async_copy(u1_far, u1, arrived.at[1]),
        pltpu.make_async_copy(q_far, q, arrived.at[2]),
    ]
    for copy in copies:
        copy.start()
    summed = over_copies(moments)
    packed = summed[:B]
    turned = transposed(packed)
    lane = iota((B, 128), 1)
    row = iota((B, 128), 0)
    column = lane & 15
    flipped = turned[:B]
    for k in range(1, 7):
        flipped = flipped + pltpu.roll(turned[16 * k : 16 * k + 16], 16 * k, 1)
    diagonal = packed
    for k in range(7):
        diagonal = jnp.where(
            (lane >= 16 * k) & (lane < 16 * k + 16), packed[:, 112 + k : 113 + k], diagonal
        )
    strips = [
        jnp.where(row <= column, packed, flipped),
        jnp.where(row == column, diagonal, jnp.where(row > column, packed, flipped)),
    ]
    shifts = []
    thirds = []
    blocks = [[], [], []]
    parts = []
    for g in range(2):
        c = 6.0 + SHIFT + table[index[g]] + shift[8 * g : 8 * g + 1, :]
        shifts.append(c)
        at = 48 * g
        f1q2 = jnp.concatenate(
            [summed[B:, at : at + K], summed[B:, at + K : at + 2 * K]], axis=0
        )
        z3 = small(f1q2, coef[g, 72 : 72 + K, :K])
        thirds.append(z3)
        taken = lax.dot_general(
            z3, f1q2, (((1,), (1,)), ((), ())), precision=HIGH, preferred_element_type=F32
        )
        wide = jnp.concatenate([taken, jnp.zeros((B, 112), F32)], axis=1)
        strip = strips[g] - pltpu.roll(wide, 96, 1)
        once = pltpu.roll(strip, 16, 1)
        twice = pltpu.roll(strip, 32, 1)
        squared = strip + 2.0 * c * once + c * c * twice
        right = strip + c * once
        parts.append(
            [
                jnp.where(
                    lane < 48,
                    pltpu.roll(squared, 128 - 16 * (i + 1), 1),
                    pltpu.roll(right, 48 - 16 * i, 1),
                )
                for i in (1, 2, 3)
            ]
        )
    system = jnp.concatenate(
        [jnp.where(lane < 64, parts[0][i], pltpu.roll(parts[1][i], 64, 1)) for i in range(3)],
        axis=0,
    )
    solved = transposed(eliminate(system, 48))
    coeffs = []
    for g in range(2):
        c = shifts[g][:, :1]
        ys = solved[64 * g + 48 : 64 * g + 64]
        y1, y2, y3 = (ys[:, 16 * i : 16 * i + 16] for i in range(3))
        z0, z1, z2 = (coef[g, 24 * i : 24 * i + B, :K] for i in range(3))
        on_f = small(y3, thirds[g])
        on_u = z0 - small(y1, z1) - small(y2, z2) - on_f
        none = jnp.zeros((B, K), F32)
        rows = jnp.concatenate(
            [
                jnp.concatenate([on_u, none, y1, y2, y3, jnp.zeros((B, B), F32)], axis=1),
                jnp.concatenate(
                    [none, on_f, -c * y1, -y1 - c * y2, -y2 - c * y3, -y3], axis=1
                ),
            ],
            axis=0,
        )
        coeffs.append(split_coeffs(rows))
    for copy in copies:
        copy.wait()
    leaving = []
    for x in range(0, NX, 2):
        for g in range(2):
            brows = slice(B * g, B * g + B)
            qrows = slice(32 * g, 32 * g + 32)
            made = combination(
                coeffs[g],
                jnp.concatenate(
                    [pair((u0, u1)[g], x, slice(0, K)), pair((f0, f1)[g], x), pair(q, x, qrows), pair(q2, x, brows), pair(t, x, brows)], axis=0
                ),
            )
            for i in range(2):
                part = made[:, NY * i : NY * i + NY]
                solution_out[brows, x + i, :] = part[:B]
                residue_out[brows, x + i, :] = part[B:] + q[x + i, 32 * g : 32 * g + B]
        if (x + 2) % CHUNK == 0:
            rows = pl.ds(x + 2 - CHUNK, CHUNK)
            for near, far in ((solution_out, solution_far), (residue_out, residue_far)):
                copy = pltpu.make_async_copy(
                    near.at[:, rows, :], far.at[:, rows, :], left.at[len(leaving)]
                )
                copy.start()
                leaving.append(copy)
    for copy in leaving:
        copy.wait()


def here(values):
    return pltpu.with_memory_space_constraint(values, pltpu.VMEM)


def call(kernel, shapes, scalars, *arrays, scratch=(), limit=8):
    count = len(arrays) - scalars
    return pl.pallas_call(
        kernel,
        out_shape=[pltpu.VMEM(s, F32) for s in shapes],
        in_specs=[SMEM] * scalars + [VMEM] * count,
        out_specs=[VMEM] * len(shapes),
        scratch_shapes=[pltpu.VMEM(s, F32) for s in scratch],
        compiler_params=pltpu.CompilerParams(vmem_limit_bytes=limit << 20),
        name=kernel.__name__,
    )(*arrays[:scalars], *(here(a) for a in arrays[scalars:]))


def finish(scalars, near, far, shape):
    copies = 2 * NX // CHUNK
    return pl.pallas_call(
        finish_kernel,
        out_shape=[jax.ShapeDtypeStruct(shape, F32)] * 2,
        in_specs=[SMEM] * len(scalars) + [VMEM] * len(near) + [ANY] * len(far),
        out_specs=[ANY] * 2,
        scratch_shapes=[pltpu.VMEM(a.shape, F32) for a in far]
        + [pltpu.VMEM(shape, F32)] * 2
        + [pltpu.SemaphoreType.DMA((len(far),)), pltpu.SemaphoreType.DMA((copies,))],
        compiler_params=pltpu.CompilerParams(vmem_limit_bytes=14 << 20),
        name="finish_kernel",
    )(*scalars, *(here(a) for a in near), *far)


def add_kernel(one, two, out):
    total = one[...] + two[...]
    for i in range(out.shape[0]):
        out[i] = total


def respread_kernel(parts, out):
    total = over_copies(parts)
    for i in range(out.shape[0]):
        out[i] = total


def everyone(values):
    far, near = STAGES
    other = lax.ppermute(values, CORES, [(0, 1), (1, 0)])
    (spread,) = call(add_kernel, [(lax.axis_size(far), *values.shape)], 0, values, other)
    parts = lax.all_to_all(spread, far, 0, 0, tiled=True)
    (spread,) = call(respread_kernel, [(lax.axis_size(near), *values.shape)], 0, parts)
    return lax.all_to_all(spread, near, 0, 0, tiled=True)


def beside(values):
    count = lax.axis_size(GRID)
    edges = [(i, (i + 1) % count) for i in range(1, count, 2)]
    across = lax.ppermute(values, GRID, edges + [(j, i) for i, j in edges])
    sibling = lax.ppermute(values, CORES, [(0, 1), (1, 0)])
    return across, sibling


def past_edge(values):
    count = lax.axis_size(GRID)
    return lax.ppermute(
        values, GRID, [(i, (i - 2 if i % 2 else i + 2) % count) for i in range(count)]
    )


def on_device(right_sides, recycle, medium, shift_table, shift_index):
    med = medium[0]
    u = recycle.reshape(2, K, NX, NY)
    b = right_sides.reshape(2 * B, NX, NY)
    scalars = (shift_table, shift_index)
    place = lax.axis_index(GRID)
    at_end = (place == 0) | (place == lax.axis_size(GRID) - 1)
    near_end = (place == 1) | (place == lax.axis_size(GRID) - 2)
    inside = jnp.where(jnp.stack([at_end, near_end]), 0.0, 1.0).astype(F32)
    back = jnp.transpose(jnp.concatenate([u[1], b], axis=0), (1, 0, 2))
    back_sides = beside(back)
    front = jnp.transpose(u[0], (1, 0, 2))
    front_across, front_sibling = beside(front)
    f1, b, b1 = call(
        back_kernel,
        [(NX, K, NY), (NX, 2 * B, NY), (NX, 2 * B, NY)],
        3,
        *scalars,
        inside,
        back,
        *back_sides,
        med,
    )
    f1_sides = beside(f1)
    front_across, f1, f1_sibling = lax.optimization_barrier((front_across, f1, f1_sides[1]))
    f1_sides = (f1_sides[0], f1_sibling)
    (f0,) = call(
        front_kernel, [(NX, K, NY)], 3, *scalars, inside, front, front_across, front_sibling, med
    )
    f0_sides = beside(f0)
    med_sides = beside(med)
    (first,) = call(first_gram_kernel, [(K, 128)], 0, f0, f1, b, b1)
    (fields,) = call(next_kernel, [(NX, 2 * K, NY)], 1, inside, f0, *f0_sides, f1, *f1_sides, med)
    (gram,) = call(second_gram_kernel, [(2 * K, 128)], 0, f0, f1, fields, b1, first)
    q, last, coef, shift = call(
        krylov_kernel,
        [(NX, 64, NY), (NX, 2 * B, NY), (2, 96, 128), (16, 128)],
        0,
        everyone(gram),
        f0,
        f1,
        b,
        b1,
        fields,
    )
    last_across, last_sibling = beside(last)
    past_across = past_edge(last)
    past_sibling = lax.ppermute(last_across, CORES, [(0, 1), (1, 0)])
    (basis_gram,) = call(basis_gram_kernel, [(2, 32, 128)], 0, q)
    q2, t, gram = call(
        moment_kernel,
        [(NX, 2 * B, NY), (NX, 2 * B, NY), (K, 128)],
        1,
        inside,
        q,
        last,
        last_across,
        last_sibling,
        past_across,
        past_sibling,
        f0,
        *f0_sides,
        f1,
        *f1_sides,
        fields,
        med,
        *med_sides,
        coef,
        shift,
        basis_gram,
        scratch=[(NX, 2 * B, NY)],
    )
    solution, residue = finish(
        scalars, (everyone(gram), coef, shift, f0, f1, q2, t), (front, back, q), (2 * B, NX, NY)
    )
    return solution.reshape(right_sides.shape), residue.reshape(right_sides.shape)


def solution(mesh):
    torus = Mesh(mesh.devices.reshape(4, 4, 8, 2), GRID)
    in_specs = (
        P(None, GRID, None, None),
        P(None, None, GRID, None, None),
        P(GRID, None, None),
        P(),
        P(),
    )
    out_specs = (P(None, GRID, None, None), P(None, GRID, None, None))
    return jax.shard_map(
        on_device, mesh=torus, in_specs=in_specs, out_specs=out_specs, check_vma=False
    )
```

```python
import jax
import jax.numpy as jnp
from jax import lax
from jax.experimental import pallas as pl
from jax.experimental.pallas import tpu as pltpu
from jax.sharding import Mesh
from jax.sharding import PartitionSpec as P

GRID = ("grid_0", "grid_1", "grid_2", "grid_3")
CORES = "grid_3"
STAGES = ("grid_2", ("grid_0", "grid_1"))
NX = 48
NY = 128
K = 24
B = 16
SHIFT = 0.5
HIGH = lax.Precision.HIGHEST
F32 = jnp.float32
BF16 = jnp.bfloat16
VMEM = pl.BlockSpec(memory_space=pltpu.VMEM)
SMEM = pl.BlockSpec(memory_space=pltpu.SMEM)
ANY = pl.BlockSpec(memory_space=pl.ANY)
CHUNK = 8


def iota(shape, dim):
    return lax.broadcasted_iota(jnp.int32, shape, dim)


def small(left, right):
    return jnp.dot(left, right, precision=HIGH, preferred_element_type=F32)


def halves(values):
    top = values.astype(BF16)
    return top, (values - top.astype(F32)).astype(BF16)


def row_products(left, right):
    dims = (((1,), (1,)), ((), ()))
    n = left.shape[0]
    l_top, l_rest = halves(left)
    r_top, r_rest = halves(right)
    both = lax.dot_general(
        jnp.concatenate([l_top, l_rest], axis=0), r_top, dims, preferred_element_type=F32
    )
    last = lax.dot_general(l_top, r_rest, dims, preferred_element_type=F32)
    return both[:n] + both[n:] + last


def combination(coeffs, fields):
    c_both, c_top = coeffs
    n = c_top.shape[0]
    f_top, f_rest = halves(fields)
    both = jnp.dot(c_both, f_top, preferred_element_type=F32)
    last = jnp.dot(c_top, f_rest, preferred_element_type=F32)
    return both[:n] + both[n:] + last


def split_coeffs(coeffs):
    top, rest = halves(coeffs)
    return jnp.concatenate([top, rest], axis=0), top


def neighbours(x, read, before, after):
    f = read(x)
    total = before + after
    if x > 0:
        total = total + read(x - 1)
    if x < NX - 1:
        total = total + read(x + 1)
    lane = iota(f.shape, 1)
    total = total + jnp.where(lane == 0, 0.0, pltpu.roll(f, 1, 1))
    return total + jnp.where(lane == NY - 1, 0.0, pltpu.roll(f, NY - 1, 1))


def transposed(values):
    rows = values.shape[0]
    return jnp.concatenate([values, jnp.zeros((128 - rows, 128), F32)], axis=0).T


def eliminate(system, count, meanwhile=None):
    lane = iota((1, 128), 1)
    row = iota(system.shape, 0)

    def column(k):
        return jnp.where(lane < 64, system[:, k : k + 1], system[:, 64 + k : 65 + k])

    for k in range(0, count, 4):
        if meanwhile is not None:
            meanwhile(k // 4)
        rows = [system[k + i : k + i + 1] for i in range(4)]
        columns = [column(k + i) for i in range(4)]
        p = [[c[k + i : k + i + 1] for c in columns] for i in range(4)]
        inverse = 1.0 / (p[0][0] * p[1][1] - p[0][1] * p[1][0])
        a, b = p[1][1] * inverse, p[0][1] * inverse
        c, d = p[1][0] * inverse, p[0][0] * inverse
        one = a * rows[0] - b * rows[1]
        two = d * rows[1] - c * rows[0]
        three, four = (rows[i] - p[i][0] * one - p[i][1] * two for i in (2, 3))
        over = [[a * p[0][i] - b * p[1][i], d * p[1][i] - c * p[0][i]] for i in (2, 3)]
        (e, f), (g, h) = (
            [p[i][m + 2] - p[i][0] * over[m][0] - p[i][1] * over[m][1] for m in range(2)]
            for i in (2, 3)
        )
        inverse = 1.0 / (e * h - f * g)
        three, four = (
            (h * inverse) * three - (f * inverse) * four,
            (e * inverse) * four - (g * inverse) * three,
        )
        one = one - over[0][0] * three - over[1][0] * four
        two = two - over[0][1] * three - over[1][1] * four
        made = (one, two, three, four)
        for i in range(4):
            system = system - columns[i] * made[i]
        for i in range(4):
            system = jnp.where(row == k + i, made[i], system)
    return system


def over_copies(parts):
    total = parts[0]
    for i in range(1, parts.shape[0]):
        total = total + parts[i]
    return total


def planes(ref, start, count):
    return lambda x: ref[x, start : start + count]


def stencil(diagonal, own, across, sibling, inside):
    def at(x):
        return diagonal(x) * own(x) - neighbours(x, own, across(x) * inside[0], sibling(x))

    return at


def applied(g, table, index, inside, medium, own, across, sibling):
    base = 6.0 + table[index[g]]
    return stencil(lambda x: medium[x : x + 1, :] + base, own, across, sibling, inside)


def front_kernel(table, index, inside, u, across, sibling, medium, f_out):
    made = applied(
        0, table, index, inside, medium, planes(u, 0, K), planes(across, 0, K), planes(sibling, 0, K)
    )
    for x in range(NX):
        f_out[x] = made(x)


def back_kernel(table, index, inside, ub, across, sibling, medium, f_out, b_out, b1_out):
    made = applied(
        1, table, index, inside, medium, planes(ub, 0, K), planes(across, 0, K), planes(sibling, 0, K)
    )
    own = planes(ub, K, 2 * B)
    shifted = stencil(
        lambda x: medium[x : x + 1, :] - SHIFT,
        own,
        planes(across, K, 2 * B),
        planes(sibling, K, 2 * B),
        inside,
    )
    for x in range(NX):
        f_out[x] = made(x)
        b_out[x] = own(x)
        b1_out[x] = shifted(x)


def pair(ref, x, rows=slice(None)):
    return jnp.concatenate([ref[x, rows], ref[x + 1, rows]], axis=1)


def first_gram_kernel(f0, f1, b, b1, gram_out):
    total = jnp.zeros((2 * K, 128), F32)
    zeros = jnp.zeros((8, 2 * NY), F32)
    tops = [jnp.zeros((B, NY), F32) for _ in range(2)]
    squares = [jnp.zeros((B, NY), F32) for _ in range(2)]
    for x in range(0, NX, 2):
        fields = [pair(f0, x), pair(f1, x)]
        b_pair = pair(b, x)
        b1_pair = pair(b1, x)
        right = []
        for g in range(2):
            bg = b_pair[B * g : B * g + B]
            b1g = b1_pair[B * g : B * g + B]
            right += [fields[g], bg, b1g, zeros]
            top = bg * b1g
            square = bg * bg
            tops[g] = tops[g] + top[:, :NY] + top[:, NY:]
            squares[g] = squares[g] + square[:, :NY] + square[:, NY:]
        total = total + row_products(
            jnp.concatenate(fields, axis=0), jnp.concatenate(right, axis=0)
        )
    lane = iota((K, 128), 1)
    row = iota((K, 128), 0)
    packed = jnp.where(lane < 64, total[:K], total[K:])
    for g in range(2):
        here = (row == 0) & (lane == 64 * g + 56)
        packed = jnp.where(here, jnp.sum(tops[g], keepdims=True), packed)
        here = (row == 0) & (lane == 64 * g + 57)
        packed = jnp.where(here, jnp.sum(squares[g], keepdims=True), packed)
    gram_out[...] = packed


def rows_of(ref):
    return lambda x: ref[x]


def next_kernel(
    inside, f0, f0_across, f0_sibling, f1, f1_across, f1_sibling, medium, first, fields_out
):
    for g, (own, across, sibling) in enumerate(
        ((f0, f0_across, f0_sibling), (f1, f1_across, f1_sibling))
    ):
        made = stencil(
            lambda x: medium[x : x + 1, :] - SHIFT,
            rows_of(own),
            rows_of(across),
            rows_of(sibling),
            inside,
        )
        for x in range(NX):
            fields_out[x, K * g : K * g + K] = made(x)


def second_gram_kernel(f0, f1, fields, b1, first, gram_out):
    total = jnp.zeros((2 * K, 128), F32)
    for x in range(0, NX, 2):
        nexts = pair(fields, x)
        b1_pair = pair(b1, x)
        right = [pair(f0, x), nexts[:K], b1_pair[:B], pair(f1, x), nexts[K:], b1_pair[B:]]
        total = total + row_products(nexts, jnp.concatenate(right, axis=0))
    lane = iota((K, 128), 1)
    gram_out[:K] = first[...]
    gram_out[K:] = jnp.where(lane < 64, total[:K], total[K:])


def krylov_kernel(
    inside,
    grams,
    f0,
    f1,
    b,
    b1,
    b1_across,
    b1_sibling,
    fields,
    fields_across,
    fields_sibling,
    medium,
    q_out,
    last_out,
    coef_out,
    shift_out,
    f_next,
    b_next,
):
    def plain(x):
        return medium[x : x + 1, :] - SHIFT

    next_f = stencil(
        plain, rows_of(fields), rows_of(fields_across), rows_of(fields_sibling), inside
    )
    next_b = stencil(plain, rows_of(b1), rows_of(b1_across), rows_of(b1_sibling), inside)

    def meanwhile(step):
        for x in range(8 * step, 8 * step + 8):
            f_next[x] = next_f(x)
            b_next[x] = next_b(x)

    gram = over_copies(grams)
    first = gram[:K]
    lane = iota((K, 128), 1)
    row = iota((K, 128), 0)
    place = lane & 63
    unit = jnp.where(place == row + K, 1.0, 0.0)
    inverse_t = transposed(eliminate(jnp.where(place < K, first, unit), K, meanwhile))
    first_t = transposed(first)
    second_t = transposed(gram[K:])
    coeffs = []
    thetas = []
    for g in range(2):
        at = 64 * g
        ginv = inverse_t[at + K : at + 2 * K, :K]
        fb = first_t[at + K : at + K + B, :K]
        fb1 = first_t[at + K + B : at + K + 2 * B, :K]
        ff1 = second_t[at : at + K, :K]
        f1f1 = second_t[at + K : at + 2 * K, :K]
        f1b1 = second_t[at + 2 * K : at + 2 * K + B, :K]
        theta = first_t[at + 56 : at + 57, :1] / first_t[at + 57 : at + 58, :1]
        z0 = small(fb, ginv)
        z1 = small(fb1 - small(z0, ff1), ginv)
        z2 = small(f1b1 - small(z0, f1f1) - small(z1, ff1), ginv)
        z2 = z2 - theta * z1
        mixed = z1 - theta * z0
        zero = jnp.zeros((B, K), F32)
        pad = jnp.zeros((B, 8), F32)
        table = jnp.concatenate(
            [
                jnp.concatenate([z0, zero, zero, pad], axis=1),
                jnp.concatenate([mixed, z0, zero, pad], axis=1),
                jnp.concatenate([z2 - theta * mixed, mixed - theta * z0, z0, pad], axis=1),
            ],
            axis=0,
        )
        coeffs.append(split_coeffs(-table))
        thetas.append(theta)
        for i, z in enumerate((z0, z1, z2, ginv)):
            coef_out[g, 24 * i : 24 * i + z.shape[0], :K] = z
        shift_out[8 * g : 8 * g + 8, :] = jnp.broadcast_to(theta, (8, 128))
    zeros = jnp.zeros((8, 2 * NY), F32)
    for x in range(0, NX, 2):
        for g in range(2):
            frows = slice(K * g, K * g + K)
            brows = slice(B * g, B * g + B)
            theta = thetas[g]
            made = combination(
                coeffs[g],
                jnp.concatenate(
                    [pair((f0, f1)[g], x), pair(fields, x, frows), pair(f_next, x, frows), zeros],
                    axis=0,
                ),
            )
            b_own = pair(b, x, brows)
            b_one = pair(b1, x, brows)
            q1 = b_one - theta * b_own
            q2 = (pair(b_next, x, brows) - theta * b_one) - theta * q1
            made = made + jnp.concatenate([b_own, q1, q2], axis=0)
            for i in range(2):
                part = made[:, NY * i : NY * i + NY]
                q_out[x + i, 48 * g : 48 * g + 48] = part
                last_out[x + i, brows] = part[2 * B :]


def basis_gram_kernel(q, fields, gram_out):
    for g in range(2):
        qrows = slice(48 * g, 48 * g + 48)
        frows = slice(K * g, K * g + K)
        total = jnp.zeros((48, 128), F32)
        none = jnp.zeros((B, 2 * NY), F32)
        pad = jnp.zeros((40, 2 * NY), F32)
        for x in range(0, NX, 2):
            left = jnp.concatenate([q[x, qrows], q[x + 1, qrows]], axis=1)
            f1 = jnp.concatenate([fields[x, frows], fields[x + 1, frows]], axis=1)
            total = total + row_products(left, jnp.concatenate([left, none, f1, pad], axis=0))
        gram_out[g] = total


def moment_kernel(inside, last, last_across, last_sibling, basis_gram, medium, shift, t_out, gram_out):
    def next_field(x, g):
        theta = shift[8 * g : 8 * g + 1, :]
        brows = slice(B * g, B * g + B)
        out = (medium[x : x + 1, :] - SHIFT - theta) * last[x, brows] - neighbours(
            x, lambda i: last[i, brows], last_across[x, brows] * inside[0], last_sibling[x, brows]
        )
        t_out[x, brows] = out
        return out

    total = jnp.zeros((2 * B, 128), F32)
    pad = jnp.zeros((64, 2 * NY), F32)
    for x in range(0, NX, 2):
        left = []
        right = []
        for g in range(2):
            brows = slice(B * g, B * g + B)
            made = jnp.concatenate([next_field(x, g), next_field(x + 1, g)], axis=1)
            left.append(made)
            right.append(jnp.concatenate([last[x, brows], last[x + 1, brows]], axis=1))
            right.append(made)
        total = total + row_products(
            jnp.concatenate(left, axis=0), jnp.concatenate(right + [pad], axis=0)
        )
    grams = [basis_gram[0], basis_gram[1]]
    ends = [pltpu.roll(total[:B], 80, 1), pltpu.roll(total[B:], 48, 1)]
    lane = iota((B, 128), 1)
    row = iota((B, 128), 0)
    column = lane & 15
    strips = []
    for gram, end in zip(grams, ends):
        middle = jnp.where(lane < 64, pltpu.roll(gram[16:32], 16, 1), pltpu.roll(gram[32:48], 32, 1))
        strips.append(jnp.where(lane < 32, gram[:16], jnp.where(lane < 80, middle, end)))
    packed = jnp.where(row <= column, strips[0], strips[1])
    packed = jnp.where(lane < 112, packed, 0.0)
    on_diagonal = jnp.where((row == column) & (lane < 112), strips[1], 0.0)
    for k in range(7):
        inside = (lane >= 16 * k) & (lane < 16 * k + 16)
        own = jnp.sum(jnp.where(inside, on_diagonal, 0.0), axis=1, keepdims=True)
        packed = jnp.where(lane == 112 + k, own, packed)
    low = jnp.zeros((8, 128), F32)
    lane8 = iota((8, 128), 1)
    for g in range(2):
        for half in range(2):
            at = 24 * (2 * g + half)
            piece = pltpu.roll(grams[g][32 + 8 * half : 40 + 8 * half], (at - 64) % 128, 1)
            low = jnp.where((lane8 >= at) & (lane8 < at + K), piece, low)
    gram_out[:B] = packed
    gram_out[B:] = low


def finish_kernel(
    table,
    index,
    moments,
    coef,
    shift,
    f0,
    f1,
    t,
    u0_far,
    u1_far,
    q_far,
    solution_far,
    residue_far,
    u0,
    u1,
    q,
    solution_out,
    residue_out,
    arrived,
    left,
):
    copies = [
        pltpu.make_async_copy(u0_far, u0, arrived.at[0]),
        pltpu.make_async_copy(u1_far, u1, arrived.at[1]),
        pltpu.make_async_copy(q_far, q, arrived.at[2]),
    ]
    for copy in copies:
        copy.start()
    summed = over_copies(moments)
    packed = summed[:B]
    turned = transposed(packed)
    lane = iota((B, 128), 1)
    row = iota((B, 128), 0)
    column = lane & 15
    flipped = turned[:B]
    for k in range(1, 7):
        flipped = flipped + pltpu.roll(turned[16 * k : 16 * k + 16], 16 * k, 1)
    diagonal = packed
    for k in range(7):
        diagonal = jnp.where(
            (lane >= 16 * k) & (lane < 16 * k + 16), packed[:, 112 + k : 113 + k], diagonal
        )
    strips = [
        jnp.where(row <= column, packed, flipped),
        jnp.where(row == column, diagonal, jnp.where(row > column, packed, flipped)),
    ]
    shifts = []
    thirds = []
    blocks = [[], [], []]
    parts = []
    for g in range(2):
        c = 6.0 + SHIFT + table[index[g]] + shift[8 * g : 8 * g + 1, :]
        shifts.append(c)
        at = 48 * g
        f1q2 = jnp.concatenate(
            [summed[B:, at : at + K], summed[B:, at + K : at + 2 * K]], axis=0
        )
        z3 = small(f1q2, coef[g, 72 : 72 + K, :K])
        thirds.append(z3)
        taken = lax.dot_general(
            z3, f1q2, (((1,), (1,)), ((), ())), precision=HIGH, preferred_element_type=F32
        )
        wide = jnp.concatenate([taken, jnp.zeros((B, 112), F32)], axis=1)
        strip = strips[g] - pltpu.roll(wide, 96, 1)
        once = pltpu.roll(strip, 16, 1)
        twice = pltpu.roll(strip, 32, 1)
        squared = strip + 2.0 * c * once + c * c * twice
        right = strip + c * once
        parts.append(
            [
                jnp.where(
                    lane < 48,
                    pltpu.roll(squared, 128 - 16 * (i + 1), 1),
                    pltpu.roll(right, 48 - 16 * i, 1),
                )
                for i in (1, 2, 3)
            ]
        )
    system = jnp.concatenate(
        [jnp.where(lane < 64, parts[0][i], pltpu.roll(parts[1][i], 64, 1)) for i in range(3)],
        axis=0,
    )
    solved = transposed(eliminate(system, 48))
    coeffs = []
    for g in range(2):
        c = shifts[g][:, :1]
        ys = solved[64 * g + 48 : 64 * g + 64]
        y1, y2, y3 = (ys[:, 16 * i : 16 * i + 16] for i in range(3))
        z0, z1, z2 = (coef[g, 24 * i : 24 * i + B, :K] for i in range(3))
        on_f = small(y3, thirds[g])
        on_u = z0 - small(y1, z1) - small(y2, z2) - on_f
        none = jnp.zeros((B, K), F32)
        rows = jnp.concatenate(
            [
                jnp.concatenate([on_u, none, y1, y2, y3, jnp.zeros((B, B), F32)], axis=1),
                jnp.concatenate(
                    [none, on_f, -c * y1, -y1 - c * y2, -y2 - c * y3, -y3], axis=1
                ),
            ],
            axis=0,
        )
        coeffs.append(split_coeffs(rows))
    for copy in copies:
        copy.wait()
    leaving = []
    for x in range(0, NX, 2):
        for g in range(2):
            brows = slice(B * g, B * g + B)
            qrows = slice(48 * g, 48 * g + 48)
            made = combination(
                coeffs[g],
                jnp.concatenate(
                    [pair((u0, u1)[g], x, slice(0, K)), pair((f0, f1)[g], x), pair(q, x, qrows), pair(t, x, brows)], axis=0
                ),
            )
            for i in range(2):
                part = made[:, NY * i : NY * i + NY]
                solution_out[brows, x + i, :] = part[:B]
                residue_out[brows, x + i, :] = part[B:] + q[x + i, 48 * g : 48 * g + B]
        if (x + 2) % CHUNK == 0:
            rows = pl.ds(x + 2 - CHUNK, CHUNK)
            for near, far in ((solution_out, solution_far), (residue_out, residue_far)):
                copy = pltpu.make_async_copy(
                    near.at[:, rows, :], far.at[:, rows, :], left.at[len(leaving)]
                )
                copy.start()
                leaving.append(copy)
    for copy in leaving:
        copy.wait()


def here(values):
    return pltpu.with_memory_space_constraint(values, pltpu.VMEM)


def call(kernel, shapes, scalars, *arrays, scratch=(), limit=8):
    count = len(arrays) - scalars
    return pl.pallas_call(
        kernel,
        out_shape=[pltpu.VMEM(s, F32) for s in shapes],
        in_specs=[SMEM] * scalars + [VMEM] * count,
        out_specs=[VMEM] * len(shapes),
        scratch_shapes=[pltpu.VMEM(s, F32) for s in scratch],
        compiler_params=pltpu.CompilerParams(vmem_limit_bytes=limit << 20),
        name=kernel.__name__,
    )(*arrays[:scalars], *(here(a) for a in arrays[scalars:]))


def finish(scalars, near, far, shape):
    copies = 2 * NX // CHUNK
    return pl.pallas_call(
        finish_kernel,
        out_shape=[jax.ShapeDtypeStruct(shape, F32)] * 2,
        in_specs=[SMEM] * len(scalars) + [VMEM] * len(near) + [ANY] * len(far),
        out_specs=[ANY] * 2,
        scratch_shapes=[pltpu.VMEM(a.shape, F32) for a in far]
        + [pltpu.VMEM(shape, F32)] * 2
        + [pltpu.SemaphoreType.DMA((len(far),)), pltpu.SemaphoreType.DMA((copies,))],
        compiler_params=pltpu.CompilerParams(vmem_limit_bytes=14 << 20),
        name="finish_kernel",
    )(*scalars, *(here(a) for a in near), *far)


def add_kernel(one, two, out):
    total = one[...] + two[...]
    for i in range(out.shape[0]):
        out[i] = total


def respread_kernel(parts, out):
    total = over_copies(parts)
    for i in range(out.shape[0]):
        out[i] = total


def everyone(values, beside_it=()):
    far, near = STAGES
    other = lax.ppermute(values, CORES, [(0, 1), (1, 0)])
    other, beside_it = lax.optimization_barrier((other, beside_it))
    (spread,) = call(add_kernel, [(lax.axis_size(far), *values.shape)], 0, values, other)
    parts = lax.all_to_all(spread, far, 0, 0, tiled=True)
    (spread,) = call(respread_kernel, [(lax.axis_size(near), *values.shape)], 0, parts)
    return lax.all_to_all(spread, near, 0, 0, tiled=True), beside_it


def beside(values):
    count = lax.axis_size(GRID)
    edges = [(i, (i + 1) % count) for i in range(1, count, 2)]
    across = lax.ppermute(values, GRID, edges + [(j, i) for i, j in edges])
    sibling = lax.ppermute(values, CORES, [(0, 1), (1, 0)])
    return across, sibling


def on_device(right_sides, recycle, medium, shift_table, shift_index):
    med = medium[0]
    u = recycle.reshape(2, K, NX, NY)
    b = right_sides.reshape(2 * B, NX, NY)
    scalars = (shift_table, shift_index)
    place = lax.axis_index(GRID)
    at_end = (place == 0) | (place == lax.axis_size(GRID) - 1)
    inside = jnp.where(at_end, 0.0, 1.0).astype(F32).reshape(1)
    back = jnp.transpose(jnp.concatenate([u[1], b], axis=0), (1, 0, 2))
    back_sides = beside(back)
    front = jnp.transpose(u[0], (1, 0, 2))
    front_across, front_sibling = beside(front)
    f1, b, b1 = call(
        back_kernel,
        [(NX, K, NY), (NX, 2 * B, NY), (NX, 2 * B, NY)],
        3,
        *scalars,
        inside,
        back,
        *back_sides,
        med,
    )
    f1_sides = beside(f1)
    front_across, f1, f1_sibling = lax.optimization_barrier((front_across, f1, f1_sides[1]))
    f1_sides = (f1_sides[0], f1_sibling)
    (f0,) = call(
        front_kernel, [(NX, K, NY)], 3, *scalars, inside, front, front_across, front_sibling, med
    )
    f0_sides = beside(f0)
    b1_sides = beside(b1)
    (first,) = call(first_gram_kernel, [(K, 128)], 0, f0, f1, b, b1)
    (fields,) = call(
        next_kernel, [(NX, 2 * K, NY)], 1, inside, f0, *f0_sides, f1, *f1_sides, med, first
    )
    field_sides = beside(fields)
    (gram,) = call(second_gram_kernel, [(2 * K, 128)], 0, f0, f1, fields, b1, first)
    grams, b1_sides = everyone(gram, b1_sides)
    q, last, coef, shift = call(
        krylov_kernel,
        [(NX, 96, NY), (NX, 2 * B, NY), (2, 96, 128), (16, 128)],
        1,
        inside,
        grams,
        f0,
        f1,
        b,
        b1,
        *b1_sides,
        fields,
        *field_sides,
        med,
        scratch=[(NX, 2 * K, NY), (NX, 2 * B, NY)],
    )
    last_sides = beside(last)
    (basis_gram,) = call(basis_gram_kernel, [(2, 48, 128)], 0, q, fields)
    t, gram = call(
        moment_kernel,
        [(NX, 2 * B, NY), (K, 128)],
        1,
        inside,
        last,
        *last_sides,
        basis_gram,
        med,
        shift,
    )
    solution, residue = finish(
        scalars, (everyone(gram)[0], coef, shift, f0, f1, t), (front, back, q), (2 * B, NX, NY)
    )
    return solution.reshape(right_sides.shape), residue.reshape(right_sides.shape)


def solution(mesh):
    torus = Mesh(mesh.devices.reshape(4, 4, 8, 2), GRID)
    in_specs = (
        P(None, GRID, None, None),
        P(None, None, GRID, None, None),
        P(GRID, None, None),
        P(),
        P(),
    )
    out_specs = (P(None, GRID, None, None), P(None, GRID, None, None))
    return jax.shard_map(
        on_device, mesh=torus, in_specs=in_specs, out_specs=out_specs, check_vma=False
    )
```

```python
import jax
import jax.numpy as jnp
from jax import lax
from jax.experimental import pallas as pl
from jax.experimental.pallas import tpu as pltpu
from jax.sharding import Mesh
from jax.sharding import PartitionSpec as P

GRID = ("grid_0", "grid_1", "grid_2", "grid_3")
CORES = "grid_3"
STAGES = ("grid_2", ("grid_0", "grid_1"))
NX = 48
NY = 128
K = 24
B = 16
SHIFT = 0.5
HIGH = lax.Precision.HIGHEST
F32 = jnp.float32
BF16 = jnp.bfloat16
VMEM = pl.BlockSpec(memory_space=pltpu.VMEM)
SMEM = pl.BlockSpec(memory_space=pltpu.SMEM)
ANY = pl.BlockSpec(memory_space=pl.ANY)
CHUNK = 8


def iota(shape, dim):
    return lax.broadcasted_iota(jnp.int32, shape, dim)


def small(left, right):
    return jnp.dot(left, right, precision=HIGH, preferred_element_type=F32)


def halves(values):
    top = values.astype(BF16)
    return top, (values - top.astype(F32)).astype(BF16)


def row_products(left, right):
    dims = (((1,), (1,)), ((), ()))
    n = left.shape[0]
    l_top, l_rest = halves(left)
    r_top, r_rest = halves(right)
    both = lax.dot_general(
        jnp.concatenate([l_top, l_rest], axis=0), r_top, dims, preferred_element_type=F32
    )
    last = lax.dot_general(l_top, r_rest, dims, preferred_element_type=F32)
    return both[:n] + both[n:] + last


def combination(coeffs, fields):
    c_both, c_top = coeffs
    n = c_top.shape[0]
    f_top, f_rest = halves(fields)
    both = jnp.dot(c_both, f_top, preferred_element_type=F32)
    last = jnp.dot(c_top, f_rest, preferred_element_type=F32)
    return both[:n] + both[n:] + last


def split_coeffs(coeffs):
    top, rest = halves(coeffs)
    return jnp.concatenate([top, rest], axis=0), top


def neighbours(x, read, before, after):
    f = read(x)
    total = before + after
    if x > 0:
        total = total + read(x - 1)
    if x < NX - 1:
        total = total + read(x + 1)
    lane = iota(f.shape, 1)
    total = total + jnp.where(lane == 0, 0.0, pltpu.roll(f, 1, 1))
    return total + jnp.where(lane == NY - 1, 0.0, pltpu.roll(f, NY - 1, 1))


def transposed(values):
    rows = values.shape[0]
    return jnp.concatenate([values, jnp.zeros((128 - rows, 128), F32)], axis=0).T


def eliminate(system, count, meanwhile=None):
    lane = iota((1, 128), 1)
    row = iota(system.shape, 0)

    def column(k):
        return jnp.where(lane < 64, system[:, k : k + 1], system[:, 64 + k : 65 + k])

    for k in range(0, count, 4):
        if meanwhile is not None:
            meanwhile(k // 4)
        rows = [system[k + i : k + i + 1] for i in range(4)]
        columns = [column(k + i) for i in range(4)]
        p = [[c[k + i : k + i + 1] for c in columns] for i in range(4)]
        inverse = 1.0 / (p[0][0] * p[1][1] - p[0][1] * p[1][0])
        a, b = p[1][1] * inverse, p[0][1] * inverse
        c, d = p[1][0] * inverse, p[0][0] * inverse
        one = a * rows[0] - b * rows[1]
        two = d * rows[1] - c * rows[0]
        three, four = (rows[i] - p[i][0] * one - p[i][1] * two for i in (2, 3))
        over = [[a * p[0][i] - b * p[1][i], d * p[1][i] - c * p[0][i]] for i in (2, 3)]
        (e, f), (g, h) = (
            [p[i][m + 2] - p[i][0] * over[m][0] - p[i][1] * over[m][1] for m in range(2)]
            for i in (2, 3)
        )
        inverse = 1.0 / (e * h - f * g)
        three, four = (
            (h * inverse) * three - (f * inverse) * four,
            (e * inverse) * four - (g * inverse) * three,
        )
        one = one - over[0][0] * three - over[1][0] * four
        two = two - over[0][1] * three - over[1][1] * four
        made = (one, two, three, four)
        for i in range(4):
            system = system - columns[i] * made[i]
        for i in range(4):
            system = jnp.where(row == k + i, made[i], system)
    return system


def over_copies(parts):
    total = parts[0]
    for i in range(1, parts.shape[0]):
        total = total + parts[i]
    return total


def planes(ref, start, count):
    return lambda x: ref[x, start : start + count]


def stencil(diagonal, own, across, sibling, inside):
    def at(x):
        return diagonal(x) * own(x) - neighbours(x, own, across(x) * inside[0], sibling(x))

    return at


def applied(g, table, index, inside, medium, own, across, sibling):
    base = 6.0 + table[index[g]]
    return stencil(lambda x: medium[x : x + 1, :] + base, own, across, sibling, inside)


def front_kernel(table, index, inside, u, across, sibling, medium, f_out):
    made = applied(
        0, table, index, inside, medium, planes(u, 0, K), planes(across, 0, K), planes(sibling, 0, K)
    )
    for x in range(NX):
        f_out[x] = made(x)


def back_kernel(table, index, inside, ub, across, sibling, medium, f_out, b_out, b1_out):
    made = applied(
        1, table, index, inside, medium, planes(ub, 0, K), planes(across, 0, K), planes(sibling, 0, K)
    )
    own = planes(ub, K, 2 * B)
    shifted = stencil(
        lambda x: medium[x : x + 1, :] - SHIFT,
        own,
        planes(across, K, 2 * B),
        planes(sibling, K, 2 * B),
        inside,
    )
    for x in range(NX):
        f_out[x] = made(x)
        b_out[x] = own(x)
        b1_out[x] = shifted(x)


def pair(ref, x, rows=slice(None)):
    return jnp.concatenate([ref[x, rows], ref[x + 1, rows]], axis=1)


def first_gram_kernel(f0, f1, b, b1, gram_out):
    total = jnp.zeros((2 * K, 128), F32)
    zeros = jnp.zeros((8, 2 * NY), F32)
    tops = [jnp.zeros((B, NY), F32) for _ in range(2)]
    squares = [jnp.zeros((B, NY), F32) for _ in range(2)]
    for x in range(0, NX, 2):
        fields = [pair(f0, x), pair(f1, x)]
        b_pair = pair(b, x)
        b1_pair = pair(b1, x)
        right = []
        for g in range(2):
            bg = b_pair[B * g : B * g + B]
            b1g = b1_pair[B * g : B * g + B]
            right += [fields[g], bg, b1g, zeros]
            top = bg * b1g
            square = bg * bg
            tops[g] = tops[g] + top[:, :NY] + top[:, NY:]
            squares[g] = squares[g] + square[:, :NY] + square[:, NY:]
        total = total + row_products(
            jnp.concatenate(fields, axis=0), jnp.concatenate(right, axis=0)
        )
    lane = iota((K, 128), 1)
    row = iota((K, 128), 0)
    packed = jnp.where(lane < 64, total[:K], total[K:])
    for g in range(2):
        here = (row == 0) & (lane == 64 * g + 56)
        packed = jnp.where(here, jnp.sum(tops[g], keepdims=True), packed)
        here = (row == 0) & (lane == 64 * g + 57)
        packed = jnp.where(here, jnp.sum(squares[g], keepdims=True), packed)
    gram_out[...] = packed


def rows_of(ref):
    return lambda x: ref[x]


def next_kernel(
    inside, f0, f0_across, f0_sibling, f1, f1_across, f1_sibling, medium, first, fields_out
):
    for g, (own, across, sibling) in enumerate(
        ((f0, f0_across, f0_sibling), (f1, f1_across, f1_sibling))
    ):
        made = stencil(
            lambda x: medium[x : x + 1, :] - SHIFT,
            rows_of(own),
            rows_of(across),
            rows_of(sibling),
            inside,
        )
        for x in range(NX):
            fields_out[x, K * g : K * g + K] = made(x)


def second_gram_kernel(core, f0, f1, fields, b1, first, kept_out, sent_out):
    total = jnp.zeros((2 * K, 128), F32)
    for x in range(0, NX, 2):
        nexts = pair(fields, x)
        b1_pair = pair(b1, x)
        right = [pair(f0, x), nexts[:K], b1_pair[:B], pair(f1, x), nexts[K:], b1_pair[B:]]
        total = total + row_products(nexts, jnp.concatenate(right, axis=0))
    lane = iota((K, 128), 1)
    second = jnp.where(lane < 64, total[:K], total[K:])
    is_first = core[0] == 0
    kept_out[...] = jnp.where(is_first, first[...], second)
    sent_out[...] = jnp.where(is_first, second, first[...])


def krylov_kernel(
    core,
    inside,
    own,
    other,
    f0,
    f1,
    b,
    b1,
    b1_across,
    b1_sibling,
    fields,
    fields_across,
    fields_sibling,
    medium,
    q_out,
    last_out,
    coef_out,
    shift_out,
    f_next,
    b_next,
):
    def plain(x):
        return medium[x : x + 1, :] - SHIFT

    next_f = stencil(
        plain, rows_of(fields), rows_of(fields_across), rows_of(fields_sibling), inside
    )
    next_b = stencil(plain, rows_of(b1), rows_of(b1_across), rows_of(b1_sibling), inside)

    def meanwhile(step):
        for x in range(8 * step, 8 * step + 8):
            f_next[x] = next_f(x)
            b_next[x] = next_b(x)

    is_first = core[0] == 0
    first = jnp.where(is_first, own[...], other[...])
    second = jnp.where(is_first, other[...], own[...])
    lane = iota((K, 128), 1)
    row = iota((K, 128), 0)
    place = lane & 63
    unit = jnp.where(place == row + K, 1.0, 0.0)
    inverse_t = transposed(eliminate(jnp.where(place < K, first, unit), K, meanwhile))
    first_t = transposed(first)
    second_t = transposed(second)
    coeffs = []
    thetas = []
    for g in range(2):
        at = 64 * g
        ginv = inverse_t[at + K : at + 2 * K, :K]
        fb = first_t[at + K : at + K + B, :K]
        fb1 = first_t[at + K + B : at + K + 2 * B, :K]
        ff1 = second_t[at : at + K, :K]
        f1f1 = second_t[at + K : at + 2 * K, :K]
        f1b1 = second_t[at + 2 * K : at + 2 * K + B, :K]
        theta = first_t[at + 56 : at + 57, :1] / first_t[at + 57 : at + 58, :1]
        z0 = small(fb, ginv)
        z1 = small(fb1 - small(z0, ff1), ginv)
        z2 = small(f1b1 - small(z0, f1f1) - small(z1, ff1), ginv)
        z2 = z2 - theta * z1
        mixed = z1 - theta * z0
        zero = jnp.zeros((B, K), F32)
        pad = jnp.zeros((B, 8), F32)
        table = jnp.concatenate(
            [
                jnp.concatenate([z0, zero, zero, pad], axis=1),
                jnp.concatenate([mixed, z0, zero, pad], axis=1),
                jnp.concatenate([z2 - theta * mixed, mixed - theta * z0, z0, pad], axis=1),
            ],
            axis=0,
        )
        coeffs.append(split_coeffs(-table))
        thetas.append(theta)
        for i, z in enumerate((z0, z1, z2, ginv)):
            coef_out[g, 24 * i : 24 * i + z.shape[0], :K] = z
        shift_out[8 * g : 8 * g + 8, :] = jnp.broadcast_to(theta, (8, 128))
    zeros = jnp.zeros((8, 2 * NY), F32)
    for x in range(0, NX, 2):
        for g in range(2):
            frows = slice(K * g, K * g + K)
            brows = slice(B * g, B * g + B)
            theta = thetas[g]
            made = combination(
                coeffs[g],
                jnp.concatenate(
                    [pair((f0, f1)[g], x), pair(fields, x, frows), pair(f_next, x, frows), zeros],
                    axis=0,
                ),
            )
            b_own = pair(b, x, brows)
            b_one = pair(b1, x, brows)
            q1 = b_one - theta * b_own
            q2 = (pair(b_next, x, brows) - theta * b_one) - theta * q1
            made = made + jnp.concatenate([b_own, q1, q2], axis=0)
            for i in range(2):
                part = made[:, NY * i : NY * i + NY]
                q_out[x + i, 48 * g : 48 * g + 48] = part
                last_out[x + i, brows] = part[2 * B :]


def basis_gram_kernel(q, fields, gram_out):
    for g in range(2):
        qrows = slice(48 * g, 48 * g + 48)
        frows = slice(K * g, K * g + K)
        total = jnp.zeros((48, 128), F32)
        none = jnp.zeros((B, 2 * NY), F32)
        pad = jnp.zeros((40, 2 * NY), F32)
        for x in range(0, NX, 2):
            left = jnp.concatenate([q[x, qrows], q[x + 1, qrows]], axis=1)
            f1 = jnp.concatenate([fields[x, frows], fields[x + 1, frows]], axis=1)
            total = total + row_products(left, jnp.concatenate([left, none, f1, pad], axis=0))
        gram_out[g] = total


def moment_kernel(inside, last, last_across, last_sibling, basis_gram, medium, shift, t_out, gram_out):
    def next_field(x, g):
        theta = shift[8 * g : 8 * g + 1, :]
        brows = slice(B * g, B * g + B)
        out = (medium[x : x + 1, :] - SHIFT - theta) * last[x, brows] - neighbours(
            x, lambda i: last[i, brows], last_across[x, brows] * inside[0], last_sibling[x, brows]
        )
        t_out[x, brows] = out
        return out

    total = jnp.zeros((2 * B, 128), F32)
    pad = jnp.zeros((64, 2 * NY), F32)
    for x in range(0, NX, 2):
        left = []
        right = []
        for g in range(2):
            brows = slice(B * g, B * g + B)
            made = jnp.concatenate([next_field(x, g), next_field(x + 1, g)], axis=1)
            left.append(made)
            right.append(jnp.concatenate([last[x, brows], last[x + 1, brows]], axis=1))
            right.append(made)
        total = total + row_products(
            jnp.concatenate(left, axis=0), jnp.concatenate(right + [pad], axis=0)
        )
    grams = [basis_gram[0], basis_gram[1]]
    ends = [pltpu.roll(total[:B], 80, 1), pltpu.roll(total[B:], 48, 1)]
    lane = iota((B, 128), 1)
    row = iota((B, 128), 0)
    column = lane & 15
    strips = []
    for gram, end in zip(grams, ends):
        middle = jnp.where(lane < 64, pltpu.roll(gram[16:32], 16, 1), pltpu.roll(gram[32:48], 32, 1))
        strips.append(jnp.where(lane < 32, gram[:16], jnp.where(lane < 80, middle, end)))
    packed = jnp.where(row <= column, strips[0], strips[1])
    packed = jnp.where(lane < 112, packed, 0.0)
    on_diagonal = jnp.where((row == column) & (lane < 112), strips[1], 0.0)
    for k in range(7):
        inside = (lane >= 16 * k) & (lane < 16 * k + 16)
        own = jnp.sum(jnp.where(inside, on_diagonal, 0.0), axis=1, keepdims=True)
        packed = jnp.where(lane == 112 + k, own, packed)
    low = jnp.zeros((8, 128), F32)
    lane8 = iota((8, 128), 1)
    for g in range(2):
        for half in range(2):
            at = 24 * (2 * g + half)
            piece = pltpu.roll(grams[g][32 + 8 * half : 40 + 8 * half], (at - 64) % 128, 1)
            low = jnp.where((lane8 >= at) & (lane8 < at + K), piece, low)
    gram_out[:B] = packed
    gram_out[B:] = low


def finish_kernel(
    table,
    index,
    moments,
    coef,
    shift,
    f0,
    f1,
    t,
    u0_far,
    u1_far,
    q_far,
    solution_far,
    residue_far,
    u0,
    u1,
    q,
    solution_out,
    residue_out,
    arrived,
    left,
):
    copies = [
        pltpu.make_async_copy(u0_far, u0, arrived.at[0]),
        pltpu.make_async_copy(u1_far, u1, arrived.at[1]),
        pltpu.make_async_copy(q_far, q, arrived.at[2]),
    ]
    for copy in copies:
        copy.start()
    summed = over_copies(moments)
    packed = summed[:B]
    turned = transposed(packed)
    lane = iota((B, 128), 1)
    row = iota((B, 128), 0)
    column = lane & 15
    flipped = turned[:B]
    for k in range(1, 7):
        flipped = flipped + pltpu.roll(turned[16 * k : 16 * k + 16], 16 * k, 1)
    diagonal = packed
    for k in range(7):
        diagonal = jnp.where(
            (lane >= 16 * k) & (lane < 16 * k + 16), packed[:, 112 + k : 113 + k], diagonal
        )
    strips = [
        jnp.where(row <= column, packed, flipped),
        jnp.where(row == column, diagonal, jnp.where(row > column, packed, flipped)),
    ]
    shifts = []
    thirds = []
    blocks = [[], [], []]
    parts = []
    for g in range(2):
        c = 6.0 + SHIFT + table[index[g]] + shift[8 * g : 8 * g + 1, :]
        shifts.append(c)
        at = 48 * g
        f1q2 = jnp.concatenate(
            [summed[B:, at : at + K], summed[B:, at + K : at + 2 * K]], axis=0
        )
        z3 = small(f1q2, coef[g, 72 : 72 + K, :K])
        thirds.append(z3)
        taken = lax.dot_general(
            z3, f1q2, (((1,), (1,)), ((), ())), precision=HIGH, preferred_element_type=F32
        )
        wide = jnp.concatenate([taken, jnp.zeros((B, 112), F32)], axis=1)
        strip = strips[g] - pltpu.roll(wide, 96, 1)
        once = pltpu.roll(strip, 16, 1)
        twice = pltpu.roll(strip, 32, 1)
        squared = strip + 2.0 * c * once + c * c * twice
        right = strip + c * once
        parts.append(
            [
                jnp.where(
                    lane < 48,
                    pltpu.roll(squared, 128 - 16 * (i + 1), 1),
                    pltpu.roll(right, 48 - 16 * i, 1),
                )
                for i in (1, 2, 3)
            ]
        )
    system = jnp.concatenate(
        [jnp.where(lane < 64, parts[0][i], pltpu.roll(parts[1][i], 64, 1)) for i in range(3)],
        axis=0,
    )
    solved = transposed(eliminate(system, 48))
    coeffs = []
    for g in range(2):
        c = shifts[g][:, :1]
        ys = solved[64 * g + 48 : 64 * g + 64]
        y1, y2, y3 = (ys[:, 16 * i : 16 * i + 16] for i in range(3))
        z0, z1, z2 = (coef[g, 24 * i : 24 * i + B, :K] for i in range(3))
        on_f = small(y3, thirds[g])
        on_u = z0 - small(y1, z1) - small(y2, z2) - on_f
        none = jnp.zeros((B, K), F32)
        rows = jnp.concatenate(
            [
                jnp.concatenate([on_u, none, y1, y2, y3, jnp.zeros((B, B), F32)], axis=1),
                jnp.concatenate(
                    [none, on_f, -c * y1, -y1 - c * y2, -y2 - c * y3, -y3], axis=1
                ),
            ],
            axis=0,
        )
        coeffs.append(split_coeffs(rows))
    for copy in copies:
        copy.wait()
    leaving = []
    for x in range(0, NX, 2):
        for g in range(2):
            brows = slice(B * g, B * g + B)
            qrows = slice(48 * g, 48 * g + 48)
            made = combination(
                coeffs[g],
                jnp.concatenate(
                    [pair((u0, u1)[g], x, slice(0, K)), pair((f0, f1)[g], x), pair(q, x, qrows), pair(t, x, brows)], axis=0
                ),
            )
            for i in range(2):
                part = made[:, NY * i : NY * i + NY]
                solution_out[brows, x + i, :] = part[:B]
                residue_out[brows, x + i, :] = part[B:] + q[x + i, 48 * g : 48 * g + B]
        if (x + 2) % CHUNK == 0:
            rows = pl.ds(x + 2 - CHUNK, CHUNK)
            for near, far in ((solution_out, solution_far), (residue_out, residue_far)):
                copy = pltpu.make_async_copy(
                    near.at[:, rows, :], far.at[:, rows, :], left.at[len(leaving)]
                )
                copy.start()
                leaving.append(copy)
    for copy in leaving:
        copy.wait()


def here(values):
    return pltpu.with_memory_space_constraint(values, pltpu.VMEM)


def call(kernel, shapes, scalars, *arrays, scratch=(), limit=8):
    count = len(arrays) - scalars
    return pl.pallas_call(
        kernel,
        out_shape=[pltpu.VMEM(s, F32) for s in shapes],
        in_specs=[SMEM] * scalars + [VMEM] * count,
        out_specs=[VMEM] * len(shapes),
        scratch_shapes=[pltpu.VMEM(s, F32) for s in scratch],
        compiler_params=pltpu.CompilerParams(vmem_limit_bytes=limit << 20),
        name=kernel.__name__,
    )(*arrays[:scalars], *(here(a) for a in arrays[scalars:]))


def finish(scalars, near, far, shape):
    copies = 2 * NX // CHUNK
    return pl.pallas_call(
        finish_kernel,
        out_shape=[jax.ShapeDtypeStruct(shape, F32)] * 2,
        in_specs=[SMEM] * len(scalars) + [VMEM] * len(near) + [ANY] * len(far),
        out_specs=[ANY] * 2,
        scratch_shapes=[pltpu.VMEM(a.shape, F32) for a in far]
        + [pltpu.VMEM(shape, F32)] * 2
        + [pltpu.SemaphoreType.DMA((len(far),)), pltpu.SemaphoreType.DMA((copies,))],
        compiler_params=pltpu.CompilerParams(vmem_limit_bytes=14 << 20),
        name="finish_kernel",
    )(*scalars, *(here(a) for a in near), *far)


def add_kernel(one, two, out):
    total = one[...] + two[...]
    for i in range(out.shape[0]):
        out[i] = total


def respread_kernel(parts, out):
    total = over_copies(parts)
    for i in range(out.shape[0]):
        out[i] = total


def sum_kernel(parts, out):
    out[...] = over_copies(parts)


def swapped(values):
    return lax.ppermute(values, CORES, [(0, 1), (1, 0)])


def everyone(kept, other):
    far, near = STAGES
    (spread,) = call(add_kernel, [(lax.axis_size(far), *kept.shape)], 0, kept, other)
    parts = lax.all_to_all(spread, far, 0, 0, tiled=True)
    (spread,) = call(respread_kernel, [(lax.axis_size(near), *kept.shape)], 0, parts)
    return lax.all_to_all(spread, near, 0, 0, tiled=True)


def beside(values):
    count = lax.axis_size(GRID)
    edges = [(i, (i + 1) % count) for i in range(1, count, 2)]
    across = lax.ppermute(values, GRID, edges + [(j, i) for i, j in edges])
    sibling = lax.ppermute(values, CORES, [(0, 1), (1, 0)])
    return across, sibling


def on_device(right_sides, recycle, medium, shift_table, shift_index):
    med = medium[0]
    u = recycle.reshape(2, K, NX, NY)
    b = right_sides.reshape(2 * B, NX, NY)
    scalars = (shift_table, shift_index)
    place = lax.axis_index(GRID)
    at_end = (place == 0) | (place == lax.axis_size(GRID) - 1)
    inside = jnp.where(at_end, 0.0, 1.0).astype(F32).reshape(1)
    back = jnp.transpose(jnp.concatenate([u[1], b], axis=0), (1, 0, 2))
    back_sides = beside(back)
    front = jnp.transpose(u[0], (1, 0, 2))
    front_across, front_sibling = beside(front)
    f1, b, b1 = call(
        back_kernel,
        [(NX, K, NY), (NX, 2 * B, NY), (NX, 2 * B, NY)],
        3,
        *scalars,
        inside,
        back,
        *back_sides,
        med,
    )
    f1_sides = beside(f1)
    front_across, f1, f1_sibling = lax.optimization_barrier((front_across, f1, f1_sides[1]))
    f1_sides = (f1_sides[0], f1_sibling)
    (f0,) = call(
        front_kernel, [(NX, K, NY)], 3, *scalars, inside, front, front_across, front_sibling, med
    )
    f0_sides = beside(f0)
    b1_sides = beside(b1)
    (first,) = call(first_gram_kernel, [(K, 128)], 0, f0, f1, b, b1)
    (fields,) = call(
        next_kernel, [(NX, 2 * K, NY)], 1, inside, f0, *f0_sides, f1, *f1_sides, med, first
    )
    field_sides = beside(fields)
    core = lax.axis_index(CORES).reshape(1)
    kept, sent = call(
        second_gram_kernel, [(K, 128)] * 2, 1, core, f0, f1, fields, b1, first
    )
    grams = everyone(kept, swapped(sent))
    grams, field_sides, b1_sides = lax.optimization_barrier((grams, field_sides, b1_sides))
    (half,) = call(sum_kernel, [(K, 128)], 0, grams)
    q, last, coef, shift = call(
        krylov_kernel,
        [(NX, 96, NY), (NX, 2 * B, NY), (2, 96, 128), (16, 128)],
        2,
        core,
        inside,
        half,
        swapped(half),
        f0,
        f1,
        b,
        b1,
        *b1_sides,
        fields,
        *field_sides,
        med,
        scratch=[(NX, 2 * K, NY), (NX, 2 * B, NY)],
    )
    last_sides = beside(last)
    (basis_gram,) = call(basis_gram_kernel, [(2, 48, 128)], 0, q, fields)
    t, gram = call(
        moment_kernel,
        [(NX, 2 * B, NY), (K, 128)],
        1,
        inside,
        last,
        *last_sides,
        basis_gram,
        med,
        shift,
    )
    solution, residue = finish(
        scalars, (everyone(gram, swapped(gram)), coef, shift, f0, f1, t), (front, back, q), (2 * B, NX, NY)
    )
    return solution.reshape(right_sides.shape), residue.reshape(right_sides.shape)


def solution(mesh):
    torus = Mesh(mesh.devices.reshape(4, 4, 8, 2), GRID)
    in_specs = (
        P(None, GRID, None, None),
        P(None, None, GRID, None, None),
        P(GRID, None, None),
        P(),
        P(),
    )
    out_specs = (P(None, GRID, None, None), P(None, GRID, None, None))
    return jax.shard_map(
        on_device, mesh=torus, in_specs=in_specs, out_specs=out_specs, check_vma=False
    )
```

```python
import jax
import jax.numpy as jnp
from jax import lax
from jax.experimental import pallas as pl
from jax.experimental.pallas import tpu as pltpu
from jax.sharding import Mesh
from jax.sharding import PartitionSpec as P

GRID = ("grid_0", "grid_1", "grid_2", "grid_3")
CORES = "grid_3"
STAGES = ("grid_2", ("grid_0", "grid_1"))
NX = 48
NY = 128
K = 24
B = 16
SHIFT = 0.5
HIGH = lax.Precision.HIGHEST
F32 = jnp.float32
BF16 = jnp.bfloat16
VMEM = pl.BlockSpec(memory_space=pltpu.VMEM)
SMEM = pl.BlockSpec(memory_space=pltpu.SMEM)
ANY = pl.BlockSpec(memory_space=pl.ANY)
CHUNK = 16


def iota(shape, dim):
    return lax.broadcasted_iota(jnp.int32, shape, dim)


def small(left, right):
    return jnp.dot(left, right, precision=HIGH, preferred_element_type=F32)


def halves(values):
    top = values.astype(BF16)
    return top, (values - top.astype(F32)).astype(BF16)


def row_products(left, right):
    dims = (((1,), (1,)), ((), ()))
    n = left.shape[0]
    l_top, l_rest = halves(left)
    r_top, r_rest = halves(right)
    both = lax.dot_general(
        jnp.concatenate([l_top, l_rest], axis=0), r_top, dims, preferred_element_type=F32
    )
    last = lax.dot_general(l_top, r_rest, dims, preferred_element_type=F32)
    return both[:n] + both[n:] + last


def combination(coeffs, fields):
    c_both, c_top = coeffs
    n = c_top.shape[0]
    f_top, f_rest = halves(fields)
    both = jnp.dot(c_both, f_top, preferred_element_type=F32)
    last = jnp.dot(c_top, f_rest, preferred_element_type=F32)
    return both[:n] + both[n:] + last


def split_coeffs(coeffs):
    top, rest = halves(coeffs)
    return jnp.concatenate([top, rest], axis=0), top


def neighbours(x, read, before, after):
    f = read(x)
    total = before + after
    if x > 0:
        total = total + read(x - 1)
    if x < NX - 1:
        total = total + read(x + 1)
    lane = iota(f.shape, 1)
    total = total + jnp.where(lane == 0, 0.0, pltpu.roll(f, 1, 1))
    return total + jnp.where(lane == NY - 1, 0.0, pltpu.roll(f, NY - 1, 1))


def transposed(values):
    rows = values.shape[0]
    return jnp.concatenate([values, jnp.zeros((128 - rows, 128), F32)], axis=0).T


def eliminate(system, count, meanwhile=None):
    lane = iota((1, 128), 1)
    row = iota(system.shape, 0)

    def column(k):
        return jnp.where(lane < 64, system[:, k : k + 1], system[:, 64 + k : 65 + k])

    for k in range(0, count, 4):
        if meanwhile is not None:
            meanwhile(k // 4)
        rows = [system[k + i : k + i + 1] for i in range(4)]
        columns = [column(k + i) for i in range(4)]
        p = [[c[k + i : k + i + 1] for c in columns] for i in range(4)]
        inverse = 1.0 / (p[0][0] * p[1][1] - p[0][1] * p[1][0])
        a, b = p[1][1] * inverse, p[0][1] * inverse
        c, d = p[1][0] * inverse, p[0][0] * inverse
        one = a * rows[0] - b * rows[1]
        two = d * rows[1] - c * rows[0]
        three, four = (rows[i] - p[i][0] * one - p[i][1] * two for i in (2, 3))
        over = [[a * p[0][i] - b * p[1][i], d * p[1][i] - c * p[0][i]] for i in (2, 3)]
        (e, f), (g, h) = (
            [p[i][m + 2] - p[i][0] * over[m][0] - p[i][1] * over[m][1] for m in range(2)]
            for i in (2, 3)
        )
        inverse = 1.0 / (e * h - f * g)
        three, four = (
            (h * inverse) * three - (f * inverse) * four,
            (e * inverse) * four - (g * inverse) * three,
        )
        one = one - over[0][0] * three - over[1][0] * four
        two = two - over[0][1] * three - over[1][1] * four
        made = (one, two, three, four)
        for i in range(4):
            system = system - columns[i] * made[i]
        for i in range(4):
            system = jnp.where(row == k + i, made[i], system)
    return system


def over_copies(parts):
    total = parts[0]
    for i in range(1, parts.shape[0]):
        total = total + parts[i]
    return total


def planes(ref, start, count):
    return lambda x: ref[x, start : start + count]


def stencil(diagonal, own, across, sibling, inside):
    def at(x):
        return diagonal(x) * own(x) - neighbours(x, own, across(x) * inside[0], sibling(x))

    return at


def applied(g, table, index, inside, medium, own, across, sibling):
    base = 6.0 + table[index[g]]
    return stencil(lambda x: medium[x : x + 1, :] + base, own, across, sibling, inside)


def front_kernel(table, index, inside, u, across, sibling, medium, f_out):
    made = applied(
        0, table, index, inside, medium, planes(u, 0, K), planes(across, 0, K), planes(sibling, 0, K)
    )
    for x in range(NX):
        f_out[x] = made(x)


def back_kernel(table, index, inside, ub, across, sibling, medium, f_out, b_out, b1_out):
    made = applied(
        1, table, index, inside, medium, planes(ub, 0, K), planes(across, 0, K), planes(sibling, 0, K)
    )
    own = planes(ub, K, 2 * B)
    shifted = stencil(
        lambda x: medium[x : x + 1, :] - SHIFT,
        own,
        planes(across, K, 2 * B),
        planes(sibling, K, 2 * B),
        inside,
    )
    for x in range(NX):
        f_out[x] = made(x)
        b_out[x] = own(x)
        b1_out[x] = shifted(x)


def pair(ref, x, rows=slice(None)):
    return jnp.concatenate([ref[x, rows], ref[x + 1, rows]], axis=1)


def first_gram_kernel(f0, f1, b, b1, gram_out):
    total = jnp.zeros((2 * K, 128), F32)
    zeros = jnp.zeros((8, 2 * NY), F32)
    tops = [jnp.zeros((B, NY), F32) for _ in range(2)]
    squares = [jnp.zeros((B, NY), F32) for _ in range(2)]
    for x in range(0, NX, 2):
        fields = [pair(f0, x), pair(f1, x)]
        b_pair = pair(b, x)
        b1_pair = pair(b1, x)
        right = []
        for g in range(2):
            bg = b_pair[B * g : B * g + B]
            b1g = b1_pair[B * g : B * g + B]
            right += [fields[g], bg, b1g, zeros]
            top = bg * b1g
            square = bg * bg
            tops[g] = tops[g] + top[:, :NY] + top[:, NY:]
            squares[g] = squares[g] + square[:, :NY] + square[:, NY:]
        total = total + row_products(
            jnp.concatenate(fields, axis=0), jnp.concatenate(right, axis=0)
        )
    lane = iota((K, 128), 1)
    row = iota((K, 128), 0)
    packed = jnp.where(lane < 64, total[:K], total[K:])
    for g in range(2):
        here = (row == 0) & (lane == 64 * g + 56)
        packed = jnp.where(here, jnp.sum(tops[g], keepdims=True), packed)
        here = (row == 0) & (lane == 64 * g + 57)
        packed = jnp.where(here, jnp.sum(squares[g], keepdims=True), packed)
    gram_out[...] = packed


def rows_of(ref):
    return lambda x: ref[x]


def next_kernel(
    inside, f0, f0_across, f0_sibling, f1, f1_across, f1_sibling, medium, first, fields_out
):
    for g, (own, across, sibling) in enumerate(
        ((f0, f0_across, f0_sibling), (f1, f1_across, f1_sibling))
    ):
        made = stencil(
            lambda x: medium[x : x + 1, :] - SHIFT,
            rows_of(own),
            rows_of(across),
            rows_of(sibling),
            inside,
        )
        for x in range(NX):
            fields_out[x, K * g : K * g + K] = made(x)


def second_gram_kernel(f0, f1, fields, b1, first, gram_out):
    total = jnp.zeros((2 * K, 128), F32)
    for x in range(0, NX, 2):
        nexts = pair(fields, x)
        b1_pair = pair(b1, x)
        right = [pair(f0, x), nexts[:K], b1_pair[:B], pair(f1, x), nexts[K:], b1_pair[B:]]
        total = total + row_products(nexts, jnp.concatenate(right, axis=0))
    lane = iota((K, 128), 1)
    gram_out[:K] = first[...]
    gram_out[K:] = jnp.where(lane < 64, total[:K], total[K:])


def krylov_kernel(
    inside,
    grams,
    f0,
    f1,
    b,
    b1,
    b1_across,
    b1_sibling,
    fields,
    fields_across,
    fields_sibling,
    medium,
    q_out,
    last_out,
    coef_out,
    shift_out,
    f_next,
    b_next,
):
    def plain(x):
        return medium[x : x + 1, :] - SHIFT

    next_f = stencil(
        plain, rows_of(fields), rows_of(fields_across), rows_of(fields_sibling), inside
    )
    next_b = stencil(plain, rows_of(b1), rows_of(b1_across), rows_of(b1_sibling), inside)

    def meanwhile(step):
        for x in range(8 * step, 8 * step + 8):
            f_next[x] = next_f(x)
            b_next[x] = next_b(x)

    gram = over_copies(grams)
    first = gram[:K]
    lane = iota((K, 128), 1)
    row = iota((K, 128), 0)
    place = lane & 63
    unit = jnp.where(place == row + K, 1.0, 0.0)
    inverse_t = transposed(eliminate(jnp.where(place < K, first, unit), K, meanwhile))
    first_t = transposed(first)
    second_t = transposed(gram[K:])
    coeffs = []
    thetas = []
    for g in range(2):
        at = 64 * g
        ginv = inverse_t[at + K : at + 2 * K, :K]
        fb = first_t[at + K : at + K + B, :K]
        fb1 = first_t[at + K + B : at + K + 2 * B, :K]
        ff1 = second_t[at : at + K, :K]
        f1f1 = second_t[at + K : at + 2 * K, :K]
        f1b1 = second_t[at + 2 * K : at + 2 * K + B, :K]
        theta = first_t[at + 56 : at + 57, :1] / first_t[at + 57 : at + 58, :1]
        z0 = small(fb, ginv)
        z1 = small(fb1 - small(z0, ff1), ginv)
        z2 = small(f1b1 - small(z0, f1f1) - small(z1, ff1), ginv)
        z2 = z2 - theta * z1
        mixed = z1 - theta * z0
        zero = jnp.zeros((B, K), F32)
        pad = jnp.zeros((B, 8), F32)
        table = jnp.concatenate(
            [
                jnp.concatenate([z0, zero, zero, pad], axis=1),
                jnp.concatenate([mixed, z0, zero, pad], axis=1),
                jnp.concatenate([z2 - theta * mixed, mixed - theta * z0, z0, pad], axis=1),
            ],
            axis=0,
        )
        coeffs.append(split_coeffs(-table))
        thetas.append(theta)
        for i, z in enumerate((z0, z1, z2, ginv)):
            coef_out[g, 24 * i : 24 * i + z.shape[0], :K] = z
        shift_out[8 * g : 8 * g + 8, :] = jnp.broadcast_to(theta, (8, 128))
    zeros = jnp.zeros((8, 2 * NY), F32)
    for x in range(0, NX, 2):
        for g in range(2):
            frows = slice(K * g, K * g + K)
            brows = slice(B * g, B * g + B)
            theta = thetas[g]
            made = combination(
                coeffs[g],
                jnp.concatenate(
                    [pair((f0, f1)[g], x), pair(fields, x, frows), pair(f_next, x, frows), zeros],
                    axis=0,
                ),
            )
            b_own = pair(b, x, brows)
            b_one = pair(b1, x, brows)
            q1 = b_one - theta * b_own
            q2 = (pair(b_next, x, brows) - theta * b_one) - theta * q1
            made = made + jnp.concatenate([b_own, q1, q2], axis=0)
            for i in range(2):
                part = made[:, NY * i : NY * i + NY]
                q_out[x + i, 48 * g : 48 * g + 48] = part
                last_out[x + i, brows] = part[2 * B :]


def basis_gram_kernel(q, fields, gram_out):
    for g in range(2):
        qrows = slice(48 * g, 48 * g + 48)
        frows = slice(K * g, K * g + K)
        total = jnp.zeros((48, 128), F32)
        none = jnp.zeros((B, 2 * NY), F32)
        pad = jnp.zeros((40, 2 * NY), F32)
        for x in range(0, NX, 2):
            left = jnp.concatenate([q[x, qrows], q[x + 1, qrows]], axis=1)
            f1 = jnp.concatenate([fields[x, frows], fields[x + 1, frows]], axis=1)
            total = total + row_products(left, jnp.concatenate([left, none, f1, pad], axis=0))
        gram_out[g] = total


def moment_kernel(inside, last, last_across, last_sibling, basis_gram, medium, shift, t_out, gram_out):
    def next_field(x, g):
        theta = shift[8 * g : 8 * g + 1, :]
        brows = slice(B * g, B * g + B)
        out = (medium[x : x + 1, :] - SHIFT - theta) * last[x, brows] - neighbours(
            x, lambda i: last[i, brows], last_across[x, brows] * inside[0], last_sibling[x, brows]
        )
        t_out[x, brows] = out
        return out

    total = jnp.zeros((2 * B, 128), F32)
    pad = jnp.zeros((64, 2 * NY), F32)
    for x in range(0, NX, 2):
        left = []
        right = []
        for g in range(2):
            brows = slice(B * g, B * g + B)
            made = jnp.concatenate([next_field(x, g), next_field(x + 1, g)], axis=1)
            left.append(made)
            right.append(jnp.concatenate([last[x, brows], last[x + 1, brows]], axis=1))
            right.append(made)
        total = total + row_products(
            jnp.concatenate(left, axis=0), jnp.concatenate(right + [pad], axis=0)
        )
    grams = [basis_gram[0], basis_gram[1]]
    ends = [pltpu.roll(total[:B], 80, 1), pltpu.roll(total[B:], 48, 1)]
    lane = iota((B, 128), 1)
    row = iota((B, 128), 0)
    column = lane & 15
    strips = []
    for gram, end in zip(grams, ends):
        middle = jnp.where(lane < 64, pltpu.roll(gram[16:32], 16, 1), pltpu.roll(gram[32:48], 32, 1))
        strips.append(jnp.where(lane < 32, gram[:16], jnp.where(lane < 80, middle, end)))
    packed = jnp.where(row <= column, strips[0], strips[1])
    packed = jnp.where(lane < 112, packed, 0.0)
    on_diagonal = jnp.where((row == column) & (lane < 112), strips[1], 0.0)
    for k in range(7):
        inside = (lane >= 16 * k) & (lane < 16 * k + 16)
        own = jnp.sum(jnp.where(inside, on_diagonal, 0.0), axis=1, keepdims=True)
        packed = jnp.where(lane == 112 + k, own, packed)
    low = jnp.zeros((8, 128), F32)
    lane8 = iota((8, 128), 1)
    for g in range(2):
        for half in range(2):
            at = 24 * (2 * g + half)
            piece = pltpu.roll(grams[g][32 + 8 * half : 40 + 8 * half], (at - 64) % 128, 1)
            low = jnp.where((lane8 >= at) & (lane8 < at + K), piece, low)
    gram_out[:B] = packed
    gram_out[B:] = low


def finish_kernel(
    table,
    index,
    moments,
    coef,
    shift,
    f0,
    f1,
    t,
    u0_far,
    u1_far,
    q_far,
    solution_far,
    residue_far,
    u0,
    u1,
    q,
    solution_out,
    residue_out,
    arrived,
    left,
):
    copies = [
        pltpu.make_async_copy(u0_far, u0, arrived.at[0]),
        pltpu.make_async_copy(u1_far, u1, arrived.at[1]),
        pltpu.make_async_copy(q_far, q, arrived.at[2]),
    ]
    for copy in copies:
        copy.start()
    summed = over_copies(moments)
    packed = summed[:B]
    turned = transposed(packed)
    lane = iota((B, 128), 1)
    row = iota((B, 128), 0)
    column = lane & 15
    flipped = turned[:B]
    for k in range(1, 7):
        flipped = flipped + pltpu.roll(turned[16 * k : 16 * k + 16], 16 * k, 1)
    diagonal = packed
    for k in range(7):
        diagonal = jnp.where(
            (lane >= 16 * k) & (lane < 16 * k + 16), packed[:, 112 + k : 113 + k], diagonal
        )
    strips = [
        jnp.where(row <= column, packed, flipped),
        jnp.where(row == column, diagonal, jnp.where(row > column, packed, flipped)),
    ]
    shifts = []
    thirds = []
    blocks = [[], [], []]
    parts = []
    for g in range(2):
        c = 6.0 + SHIFT + table[index[g]] + shift[8 * g : 8 * g + 1, :]
        shifts.append(c)
        at = 48 * g
        f1q2 = jnp.concatenate(
            [summed[B:, at : at + K], summed[B:, at + K : at + 2 * K]], axis=0
        )
        z3 = small(f1q2, coef[g, 72 : 72 + K, :K])
        thirds.append(z3)
        taken = lax.dot_general(
            z3, f1q2, (((1,), (1,)), ((), ())), precision=HIGH, preferred_element_type=F32
        )
        wide = jnp.concatenate([taken, jnp.zeros((B, 112), F32)], axis=1)
        strip = strips[g] - pltpu.roll(wide, 96, 1)
        once = pltpu.roll(strip, 16, 1)
        twice = pltpu.roll(strip, 32, 1)
        squared = strip + 2.0 * c * once + c * c * twice
        right = strip + c * once
        parts.append(
            [
                jnp.where(
                    lane < 48,
                    pltpu.roll(squared, 128 - 16 * (i + 1), 1),
                    pltpu.roll(right, 48 - 16 * i, 1),
                )
                for i in (1, 2, 3)
            ]
        )
    system = jnp.concatenate(
        [jnp.where(lane < 64, parts[0][i], pltpu.roll(parts[1][i], 64, 1)) for i in range(3)],
        axis=0,
    )
    solved = transposed(eliminate(system, 48))
    coeffs = []
    for g in range(2):
        c = shifts[g][:, :1]
        ys = solved[64 * g + 48 : 64 * g + 64]
        y1, y2, y3 = (ys[:, 16 * i : 16 * i + 16] for i in range(3))
        z0, z1, z2 = (coef[g, 24 * i : 24 * i + B, :K] for i in range(3))
        on_f = small(y3, thirds[g])
        on_u = z0 - small(ys[:, :48], jnp.concatenate([z1, z2, thirds[g]], axis=0))
        none = jnp.zeros((B, K), F32)
        rows = jnp.concatenate(
            [
                jnp.concatenate([on_u, none, y1, y2, y3, jnp.zeros((B, B), F32)], axis=1),
                jnp.concatenate(
                    [none, on_f, -c * y1, -y1 - c * y2, -y2 - c * y3, -y3], axis=1
                ),
            ],
            axis=0,
        )
        coeffs.append(split_coeffs(rows))
    for copy in copies:
        copy.wait()
    leaving = []
    for x in range(0, NX, 2):
        for g in range(2):
            brows = slice(B * g, B * g + B)
            qrows = slice(48 * g, 48 * g + 48)
            made = combination(
                coeffs[g],
                jnp.concatenate(
                    [pair((u0, u1)[g], x, slice(0, K)), pair((f0, f1)[g], x), pair(q, x, qrows), pair(t, x, brows)], axis=0
                ),
            )
            for i in range(2):
                part = made[:, NY * i : NY * i + NY]
                solution_out[brows, x + i, :] = part[:B]
                residue_out[brows, x + i, :] = part[B:] + q[x + i, 48 * g : 48 * g + B]
        if (x + 2) % CHUNK == 0:
            rows = pl.ds(x + 2 - CHUNK, CHUNK)
            for near, far in ((solution_out, solution_far), (residue_out, residue_far)):
                copy = pltpu.make_async_copy(
                    near.at[:, rows, :], far.at[:, rows, :], left.at[len(leaving)]
                )
                copy.start()
                leaving.append(copy)
    for copy in leaving:
        copy.wait()


def here(values):
    return pltpu.with_memory_space_constraint(values, pltpu.VMEM)


def call(kernel, shapes, scalars, *arrays, scratch=(), limit=8):
    count = len(arrays) - scalars
    return pl.pallas_call(
        kernel,
        out_shape=[pltpu.VMEM(s, F32) for s in shapes],
        in_specs=[SMEM] * scalars + [VMEM] * count,
        out_specs=[VMEM] * len(shapes),
        scratch_shapes=[pltpu.VMEM(s, F32) for s in scratch],
        compiler_params=pltpu.CompilerParams(vmem_limit_bytes=limit << 20),
        name=kernel.__name__,
    )(*arrays[:scalars], *(here(a) for a in arrays[scalars:]))


def finish(scalars, near, far, shape):
    copies = 2 * NX // CHUNK
    return pl.pallas_call(
        finish_kernel,
        out_shape=[jax.ShapeDtypeStruct(shape, F32)] * 2,
        in_specs=[SMEM] * len(scalars) + [VMEM] * len(near) + [ANY] * len(far),
        out_specs=[ANY] * 2,
        scratch_shapes=[pltpu.VMEM(a.shape, F32) for a in far]
        + [pltpu.VMEM(shape, F32)] * 2
        + [pltpu.SemaphoreType.DMA((len(far),)), pltpu.SemaphoreType.DMA((copies,))],
        compiler_params=pltpu.CompilerParams(vmem_limit_bytes=14 << 20),
        name="finish_kernel",
    )(*scalars, *(here(a) for a in near), *far)


def add_kernel(one, two, out):
    total = one[...] + two[...]
    for i in range(out.shape[0]):
        out[i] = total


def respread_kernel(parts, out):
    total = over_copies(parts)
    for i in range(out.shape[0]):
        out[i] = total


def everyone(values, beside_it=()):
    far, near = STAGES
    other = lax.ppermute(values, CORES, [(0, 1), (1, 0)])
    other, beside_it = lax.optimization_barrier((other, beside_it))
    (spread,) = call(add_kernel, [(lax.axis_size(far), *values.shape)], 0, values, other)
    parts = lax.all_to_all(spread, far, 0, 0, tiled=True)
    (spread,) = call(respread_kernel, [(lax.axis_size(near), *values.shape)], 0, parts)
    return lax.all_to_all(spread, near, 0, 0, tiled=True), beside_it


def beside(values):
    count = lax.axis_size(GRID)
    edges = [(i, (i + 1) % count) for i in range(1, count, 2)]
    across = lax.ppermute(values, GRID, edges + [(j, i) for i, j in edges])
    sibling = lax.ppermute(values, CORES, [(0, 1), (1, 0)])
    return across, sibling


def on_device(right_sides, recycle, medium, shift_table, shift_index):
    med = medium[0]
    u = recycle.reshape(2, K, NX, NY)
    b = right_sides.reshape(2 * B, NX, NY)
    scalars = (shift_table, shift_index)
    place = lax.axis_index(GRID)
    at_end = (place == 0) | (place == lax.axis_size(GRID) - 1)
    inside = jnp.where(at_end, 0.0, 1.0).astype(F32).reshape(1)
    back = jnp.transpose(jnp.concatenate([u[1], b], axis=0), (1, 0, 2))
    back_sides = beside(back)
    front = jnp.transpose(u[0], (1, 0, 2))
    front_across, front_sibling = beside(front)
    f1, b, b1 = call(
        back_kernel,
        [(NX, K, NY), (NX, 2 * B, NY), (NX, 2 * B, NY)],
        3,
        *scalars,
        inside,
        back,
        *back_sides,
        med,
    )
    f1_sides = beside(f1)
    front_across, f1, f1_sibling = lax.optimization_barrier((front_across, f1, f1_sides[1]))
    f1_sides = (f1_sides[0], f1_sibling)
    (f0,) = call(
        front_kernel, [(NX, K, NY)], 3, *scalars, inside, front, front_across, front_sibling, med
    )
    f0_sides = beside(f0)
    b1_sides = beside(b1)
    (first,) = call(first_gram_kernel, [(K, 128)], 0, f0, f1, b, b1)
    (fields,) = call(
        next_kernel, [(NX, 2 * K, NY)], 1, inside, f0, *f0_sides, f1, *f1_sides, med, first
    )
    field_sides = beside(fields)
    (gram,) = call(second_gram_kernel, [(2 * K, 128)], 0, f0, f1, fields, b1, first)
    grams, b1_sides = everyone(gram, b1_sides)
    q, last, coef, shift = call(
        krylov_kernel,
        [(NX, 96, NY), (NX, 2 * B, NY), (2, 96, 128), (16, 128)],
        1,
        inside,
        grams,
        f0,
        f1,
        b,
        b1,
        *b1_sides,
        fields,
        *field_sides,
        med,
        scratch=[(NX, 2 * K, NY), (NX, 2 * B, NY)],
    )
    last_sides = beside(last)
    (basis_gram,) = call(basis_gram_kernel, [(2, 48, 128)], 0, q, fields)
    t, gram = call(
        moment_kernel,
        [(NX, 2 * B, NY), (K, 128)],
        1,
        inside,
        last,
        *last_sides,
        basis_gram,
        med,
        shift,
    )
    solution, residue = finish(
        scalars, (everyone(gram)[0], coef, shift, f0, f1, t), (front, back, q), (2 * B, NX, NY)
    )
    return solution.reshape(right_sides.shape), residue.reshape(right_sides.shape)


def solution(mesh):
    torus = Mesh(mesh.devices.reshape(4, 4, 8, 2), GRID)
    in_specs = (
        P(None, GRID, None, None),
        P(None, None, GRID, None, None),
        P(GRID, None, None),
        P(),
        P(),
    )
    out_specs = (P(None, GRID, None, None), P(None, GRID, None, None))
    return jax.shard_map(
        on_device, mesh=torus, in_specs=in_specs, out_specs=out_specs, check_vma=False
    )
```
